32 devices in a mesh: rep: 4 (over z), fsdp: 8 (over y, x, core).
Axes of the slice: x: 2, y: 2, z: 4, core: 2. Of those that a mesh axis runs over, the one named last changes fastest.
Arguments:
- tokens: bfloat16 [4096, 2048], P(('rep', 'fsdp')), may hold values from -6 to 6
- cotangent: bfloat16 [4096, 2048], P(('rep', 'fsdp')), may hold values from -6 to 6
- doc_lengths: int32 [4, 8], replicated, may hold values from 1 to 513, as said below
- norm1_gain: bfloat16 [2048], P('fsdp'), may hold values from 0.5 to 1.5
- w_query: bfloat16 [2048, 2048], P('fsdp'), may hold values from -0.125 to 0.125
- w_key: bfloat16 [2048, 256], P('fsdp'), may hold values from -0.125 to 0.125
- w_value: bfloat16 [2048, 256], P('fsdp'), may hold values from -0.125 to 0.125
- w_out: bfloat16 [2048, 2048], P('fsdp'), may hold values from -0.5 to 0.5
- norm2_gain: bfloat16 [2048], P('fsdp'), may hold values from 0.5 to 1.5
- w_gate: bfloat16 [2048, 5632], P('fsdp'), may hold values from -0.125 to 0.125
- w_up: bfloat16 [2048, 5632], P('fsdp'), may hold values from -0.125 to 0.125
- w_down: bfloat16 [5632, 2048], P('fsdp'), may hold values from -0.078125 to 0.078125
Outputs:
- output: bfloat16 [4096, 2048], P(('rep', 'fsdp'))
- grad_input: bfloat16 [4096, 2048], P(('rep', 'fsdp'))
- grad_norm1: float32 [2048], P('fsdp')
- grad_query: float32 [2048, 2048], P('fsdp')
- grad_key: float32 [2048, 256], P('fsdp')
- grad_value: float32 [2048, 256], P('fsdp')
- grad_out_proj: float32 [2048, 2048], P('fsdp')
- grad_norm2: float32 [2048], P('fsdp')
- grad_gate: float32 [2048, 5632], P('fsdp')
- grad_up: float32 [2048, 5632], P('fsdp')
- grad_down: float32 [5632, 2048], P('fsdp')
The draws below stay inside these ranges and needn't reach their ends.
Inputs may be any that keep to these rules, and one draw needn't show every extreme that they name: `doc_lengths`: row s lists in order the lengths of the documents packed into sequence s, and as its last entry the length of the tail padding, at most 128; each row sums to 1024, and in each row exactly one document has 513 tokens.
All inputs are finite; a program needn't handle non-finite values.
Results may differ from the reference program's by a relative error of at most 0.022.
Values may be sent and summed in bfloat16 or wider, within the bound.
No kernel may reach another device: no remote copies, remote signals or barrier semaphores. Data moves between devices by JAX's collectives and lax.ppermute only.
A program may use at most 384 MiB of HBM per device.

```python
import math
import jax
import jax.numpy as jnp
from jax import lax

D = 2048
H = 32
KVH = 4
HD = 64
FF = 5632
DOCS = 8
SEQ = 1024
TOKENS = 4096
NSEQ = 4


def draw_doc_lengths(key, part):
    longest = SEQ // 2 + 1
    row_keys = jax.random.split(jax.random.fold_in(key, 17), NSEQ)

    def one_row(row_key):
        pad_key, weight_key, place_key = jax.random.split(row_key, 3)
        padding = jax.random.randint(pad_key, (), 1, SEQ // 8 + 1, dtype=jnp.int32)
        remaining = SEQ - longest - padding
        extra = remaining - (DOCS - 2)
        weights = jax.random.randint(weight_key, (DOCS - 2,), 1, 64, dtype=jnp.int32)
        weights = weights * weights
        shares = extra * weights // jnp.sum(weights)
        shares = shares.at[0].add(extra - jnp.sum(shares))
        others = 1 + shares
        place = jax.random.randint(place_key, (), 0, DOCS - 1, dtype=jnp.int32)
        slots = jnp.arange(DOCS - 1, dtype=jnp.int32)
        source = jnp.clip(slots - (slots > place).astype(jnp.int32), 0, DOCS - 3)
        documents = jnp.where(slots == place, longest, others[source])
        return jnp.concatenate([documents, padding[None]]).astype(jnp.int32)
    return jax.vmap(one_row)(row_keys)


def steps_of(own_key, dims, cuts, least, top_value):
    factor_of, own = 1.0, jax.random.fold_in(own_key, 6)
    for position, blocks in cuts:
        steps = jnp.exp(jax.random.uniform(jax.random.fold_in(own, position), (blocks,), jnp.float32, least / len(cuts), top_value / len(cuts)))
        factor_of = factor_of * jnp.repeat(steps, dims[position] // blocks).reshape([-1 if axis == position else 1 for axis in range(len(dims))])
    return factor_of


def normal_values(own_key, shape, width, most, shards=(), kind=jnp.bfloat16):
    factor_of = steps_of(own_key, shape, shards, -0.22, 0.18) if shards else 1.0
    drawn = jax.random.normal(own_key, shape, jnp.float32) * width * factor_of
    return jnp.minimum(jnp.maximum(drawn, -most), most).astype(kind)


def setup_inputs(seed: int = 0) -> dict:
    arg_keys = jax.random.split(jax.random.key(seed), 13)
    tokens = normal_values(arg_keys[0], (TOKENS, D), 1.0, 6.0, ((0, 32),))
    cotangent = normal_values(arg_keys[1], (TOKENS, D), 1.0, 6.0, ((0, 32),))
    doc_lengths = draw_doc_lengths(jax.random.fold_in(arg_keys[12], 71), 0)
    norm1_gain = jnp.clip(1.0 + 0.1 * jax.random.normal(arg_keys[3], (D,), jnp.float32), 0.5, 1.5).astype(jnp.bfloat16)
    w_query = normal_values(arg_keys[4], (D, D), D ** -0.5, 0.125, ((0, 8),))
    w_key = normal_values(arg_keys[5], (D, KVH * HD), D ** -0.5, 0.125, ((0, 8),))
    w_value = normal_values(arg_keys[6], (D, KVH * HD), D ** -0.5, 0.125, ((0, 8),))
    w_out = normal_values(arg_keys[7], (D, D), (D // 16) ** -0.5, 0.5, ((0, 8),))
    norm2_gain = jnp.clip(1.0 + 0.1 * jax.random.normal(arg_keys[8], (D,), jnp.float32), 0.5, 1.5).astype(jnp.bfloat16)
    w_gate = normal_values(arg_keys[9], (D, FF), D ** -0.5, 0.125, ((0, 8),))
    w_up = normal_values(arg_keys[10], (D, FF), D ** -0.5, 0.125, ((0, 8),))
    w_down = normal_values(arg_keys[11], (FF, D), FF ** -0.5, 0.078125, ((0, 8),))
    return {"tokens": tokens, "cotangent": cotangent, "doc_lengths": doc_lengths, "norm1_gain": norm1_gain, "w_query": w_query, "w_key": w_key, "w_value": w_value, "w_out": w_out, "norm2_gain": norm2_gain, "w_gate": w_gate, "w_up": w_up, "w_down": w_down}


NORM_EPS = 1e-05
ROPE_BASE = 10000.0
MASK_FILL = -1e+30

@jax.custom_vjp
def low(v):
    return lax.optimization_barrier(v.astype(jnp.bfloat16)).astype(jnp.float32)

@jax.custom_vjp
def low_back(v):
    return v

def low_keep(v):
    return (low(v), None)

def low_pass(kept, grad):
    return (grad,)

def back_keep(v):
    return (v, None)

def back_low(kept, grad):
    return (low(grad),)
low.defvjp(low_keep, low_pass)
low_back.defvjp(back_keep, back_low)

def angle_tables(positions, head_dim):
    fractions = jnp.arange(0, head_dim, 2, dtype=jnp.float32) / head_dim
    inverse = jnp.exp(-math.log(ROPE_BASE) * fractions)
    angles = positions[:, None] * inverse[None, :]
    angles = jnp.concatenate([angles, angles], axis=-1)
    return (jnp.cos(angles)[:, None, :], jnp.sin(angles)[:, None, :])

def rotate(vectors, cos_table, sin_table):
    half_dim = vectors.shape[-1] // 2
    turned = jnp.concatenate([-vectors[..., half_dim:], vectors[..., :half_dim]], axis=-1)
    return vectors * cos_table + turned * sin_table

def masks_for(lengths, offset, tok_count):
    bounds = jnp.cumsum(lengths, dtype=jnp.int32)
    key_pos = jnp.arange(SEQ, dtype=jnp.int32)
    key_seg = lax.optimization_barrier(jnp.sum((bounds[None, :] <= key_pos[:, None]).astype(jnp.int32), axis=1, dtype=jnp.int32))
    key_valid = key_seg < DOCS - 1
    query_pos = offset + jnp.arange(tok_count, dtype=jnp.int32)
    query_seg = lax.dynamic_slice_in_dim(key_seg, offset, tok_count)
    query_valid = lax.dynamic_slice_in_dim(key_valid, offset, tok_count)
    allowed = (key_pos[None, :] <= query_pos[:, None]) & (query_seg[:, None] == key_seg[None, :])
    allowed = allowed & query_valid[:, None] & key_valid[None, :] | (key_pos[None, :] == query_pos[:, None])
    return (allowed, query_valid, query_pos)

def attend_ref(query_grp, key_grp, value_grp, allowed):
    precise = lax.Precision.HIGHEST
    score_scale = 1.0 / math.sqrt(query_grp.shape[-1])
    scores = jnp.einsum('tgd,sd->tgs', query_grp, key_grp, precision=precise) * score_scale
    scores = low_back(scores)
    scores = jnp.where(allowed[:, None, :], scores, MASK_FILL)
    highest = lax.optimization_barrier(jnp.max(scores, axis=-1, keepdims=True))
    weights = jnp.exp(scores - highest)
    totals = lax.optimization_barrier(jnp.sum(weights, axis=-1, keepdims=True))
    prob_low = low(weights / totals)
    return jnp.einsum('tgs,sd->tgd', prob_low, value_grp, precision=precise)

def layer_one(inputs, lengths, gain_one, w_query, w_key, w_value, w_out, gain_two, w_gate, w_up, w_down):
    precise = lax.Precision.HIGHEST

    def product(left_side, right_side):
        return jnp.dot(left_side, right_side, precision=precise)
    heads_per = H // KVH
    scale_one = lax.rsqrt(lax.optimization_barrier(jnp.mean(inputs * inputs, axis=-1, keepdims=True)) + NORM_EPS)
    hidden_one = low(inputs * scale_one * gain_one)
    positions = jnp.arange(SEQ, dtype=jnp.float32)
    cos_table, sin_table = angle_tables(positions, HD)
    queries = low_back(product(hidden_one, w_query)).reshape(SEQ, H, HD)
    key_proj = low_back(product(hidden_one, w_key)).reshape(SEQ, KVH, HD)
    value_proj = low(low_back(product(hidden_one, w_value))).reshape(SEQ, KVH, HD)
    queries = low(rotate(queries, cos_table, sin_table))
    key_proj = low(rotate(key_proj, cos_table, sin_table))
    allowed, query_valid, query_pos = masks_for(lengths, 0, SEQ)
    query_grp = queries.reshape(SEQ, KVH, heads_per, HD).transpose(1, 0, 2, 3)
    key_grp = key_proj.transpose(1, 0, 2)
    value_grp = value_proj.transpose(1, 0, 2)

    def group_attend(packed):
        return attend_ref(packed[0], packed[1], packed[2], allowed)
    mixed = lax.map(jax.checkpoint(group_attend), (query_grp, key_grp, value_grp))
    valid_col = jnp.where(query_valid, 1.0, 0.0).astype(inputs.dtype)[:, None]
    attn_mix = low(low_back(mixed.transpose(1, 0, 2, 3).reshape(SEQ, H * HD) * valid_col))
    resid_one = inputs + low_back(product(attn_mix, w_out))
    scale_two = lax.rsqrt(lax.optimization_barrier(jnp.mean(resid_one * resid_one, axis=-1, keepdims=True)) + NORM_EPS)
    hidden_two = low(resid_one * scale_two * gain_two)
    gate_pre = low_back(product(hidden_two, w_gate))
    up_pre = low_back(product(hidden_two, w_up))
    inner_low = low(jax.nn.silu(gate_pre) * up_pre)
    return resid_one + low_back(product(inner_low, w_down))

def reference(tokens, cotangent, doc_lengths, norm1_gain, w_query, w_key, w_value, w_out, norm2_gain, w_gate, w_up, w_down):
    params = tuple((weight.astype(jnp.float32) for weight in (norm1_gain, w_query, w_key, w_value, w_out, norm2_gain, w_gate, w_up, w_down)))
    seq_inputs = tokens.astype(jnp.float32).reshape(NSEQ, SEQ, D)
    seq_cots = cotangent.astype(jnp.float32).reshape(NSEQ, SEQ, D)

    def one_seq(carried, packed):
        inputs, cots, lengths = packed

        def layer_fn(inputs_in, *weights_in):
            return layer_one(inputs_in, lengths, *weights_in)
        outputs, pull = jax.vjp(layer_fn, inputs, *params)
        gradients = pull(cots)
        updated = tuple((running + gradient for running, gradient in zip(carried, gradients[1:])))
        return (updated, (outputs, gradients[0]))
    zero_sums = tuple((jnp.zeros_like(weight) for weight in params))
    grad_sums, (outputs, grad_inputs) = lax.scan(one_seq, zero_sums, (seq_inputs, seq_cots, doc_lengths))
    return (outputs.reshape(TOKENS, D).astype(jnp.bfloat16), grad_inputs.reshape(TOKENS, D).astype(jnp.bfloat16), grad_sums[0], grad_sums[1], grad_sums[2], grad_sums[3], grad_sums[4], grad_sums[5], grad_sums[6], grad_sums[7], grad_sums[8])
```

```python
import math

import jax
import jax.numpy as jnp
from jax import lax
from jax.experimental import pallas as pl
from jax.experimental.pallas import tpu as pltpu
from jax.sharding import PartitionSpec as P

H = 32
KVH = 4
HD = 64
DOCS = 8

NORM_EPS = 1e-05
ROPE_BASE = 10000.0
MASK_FILL = -1e30
F32 = jnp.float32
BF16 = jnp.bfloat16


def dot(a, b):
    return jnp.dot(a, b, preferred_element_type=F32)


def dot_nt(a, b):
    return lax.dot_general(a, b, (((1,), (1,)), ((), ())), preferred_element_type=F32)


def dot_tn(a, b):
    return lax.dot_general(a, b, (((0,), (0,)), ((), ())), preferred_element_type=F32)


def angle_tables(positions):
    fractions = jnp.arange(0, HD, 2, dtype=F32) / HD
    inverse = jnp.exp(-math.log(ROPE_BASE) * fractions)
    angles = positions[:, None] * inverse[None, :]
    angles = jnp.concatenate([angles, angles], axis=-1)
    return jnp.cos(angles)[:, None, :], jnp.sin(angles)[:, None, :]


def rotate(v, cos_table, sin_table):
    half = HD // 2
    turned = jnp.concatenate([-v[..., half:], v[..., :half]], axis=-1)
    return v * cos_table + turned * sin_table


def rotate_back(v, cos_table, sin_table):
    half = HD // 2
    moved = v * sin_table
    turned = jnp.concatenate([moved[..., half:], -moved[..., :half]], axis=-1)
    return v * cos_table + turned


def norm_parts(v):
    inv = lax.rsqrt(jnp.mean(v * v, axis=-1, keepdims=True) + NORM_EPS)
    return inv, v * inv


def norm_back(grad_hidden, normed, inv, gain):
    e = grad_hidden * gain
    return inv * (e - normed * jnp.mean(e * normed, axis=-1, keepdims=True))


def pick_columns(array, chip, count):
    rows, cols = array.shape
    width = cols // count
    if width % 128:
        split = array.reshape(rows, count, width).transpose(1, 0, 2)
        return jnp.stack(
            [lax.dynamic_index_in_dim(split, chip ^ k, 0, keepdims=False) for k in range(count)]
        )

    def body(c_ref, in_ref, out_ref):
        out_ref[0] = in_ref[...]

    return pl.pallas_call(
        body,
        grid_spec=pltpu.PrefetchScalarGridSpec(
            num_scalar_prefetch=1,
            grid=(count,),
            in_specs=[pl.BlockSpec((rows, width), lambda k, c: (0, c[0] ^ k))],
            out_specs=pl.BlockSpec((1, rows, width), lambda k, c: (k, 0, 0)),
        ),
        out_shape=jax.ShapeDtypeStruct((count, rows, width), array.dtype),
        name="pick_columns",
    )(chip.reshape(1), array)


def place(blocks, order, axis, dtype):
    rows, cols = blocks[0].shape
    count = len(blocks)
    if axis == 1 and cols % 128:
        full = jnp.zeros((count, rows, cols), dtype)
        for k in range(count):
            full = lax.dynamic_update_slice(full, blocks[k].astype(dtype)[None], (order[k], 0, 0))
        return full.transpose(1, 0, 2).reshape(rows, count * cols)

    def body(o_ref, *refs):
        out_ref = refs[-1]
        for k in range(count):

            @pl.when(pl.program_id(0) == k)
            def _():
                out_ref[...] = refs[k][...].astype(dtype)

    if axis == 0:
        shape, spec = (count * rows, cols), pl.BlockSpec((rows, cols), lambda k, o: (o[k], 0))
    else:
        shape, spec = (rows, count * cols), pl.BlockSpec((rows, cols), lambda k, o: (0, o[k]))
    return pl.pallas_call(
        body,
        grid_spec=pltpu.PrefetchScalarGridSpec(
            num_scalar_prefetch=1,
            grid=(count,),
            in_specs=[pl.BlockSpec((rows, cols), lambda k, o: (0, 0))] * count,
            out_specs=spec,
        ),
        out_shape=jax.ShapeDtypeStruct(shape, dtype),
        name="place",
    )(order, *blocks)


def local(
    tokens,
    cotangent,
    doc_lengths,
    norm1_gain,
    w_query,
    w_key,
    w_value,
    w_out,
    norm2_gain,
    w_gate,
    w_up,
    w_down,
):
    rows, model = tokens.shape
    group = lax.axis_size("fsdp")
    reps = lax.axis_size("rep")
    chips = group // 2
    dev = lax.axis_index("fsdp")
    rep = lax.axis_index("rep")
    chip, core = dev // 2, dev % 2
    seq_len = rows * group
    own = rows * chips
    wrows = w_query.shape[0]
    ff = w_gate.shape[1]
    heads = H // chips
    kv_share = chips // KVH
    qw = heads * HD

    def hop(v, k):
        return lax.ppermute(v, "fsdp", [(i, i ^ (2 * k)) for i in range(group)])

    def swap(v):
        return lax.ppermute(v, "fsdp", [(i, i ^ 1) for i in range(group)])

    def by_core(mine, other, axis):
        return jnp.where(
            core == 0,
            jnp.concatenate([mine, other], axis=axis),
            jnp.concatenate([other, mine], axis=axis),
        )

    def gather_chips(v):
        return [v] + [hop(v, k) for k in range(1, chips)]

    def scatter_chips(partial):
        parts = partial.astype(BF16).reshape(chips, rows, model)
        total = parts[0].astype(F32)
        for k in range(1, chips):
            total = total + hop(parts[k], k).astype(F32)
        return total

    half = reps // 2

    def chain(v):
        acc = v
        for s in range(half - 1):
            got = lax.ppermute(acc, "rep", [(s, s + 1), (reps - 1 - s, reps - 2 - s)])
            acc = acc + got
        got = lax.ppermute(acc, "rep", [(half - 1, half), (half, half - 1)])
        tot = lax.optimization_barrier(acc + got)
        for s in reversed(range(half - 1)):
            got = lax.ppermute(tot, "rep", [(s + 1, s), (reps - 2 - s, reps - 1 - s)])
            tot = jnp.where((rep == s) | (rep == reps - 1 - s), got, tot)
        return tot

    chip_order = jnp.stack([chip ^ k for k in range(chips)]).astype(jnp.int32)

    gains = jnp.stack([norm1_gain, norm2_gain])
    gain_blocks = gather_chips(gains)
    gain_blocks = [(g, swap(g)) for g in gain_blocks]
    gain_full = jnp.zeros((group, 2, wrows), BF16)
    for k in range(chips):
        mine, other = gain_blocks[k]
        gain_full = lax.dynamic_update_slice(gain_full, mine[None], ((chip ^ k) * 2 + core, 0, 0))
        gain_full = lax.dynamic_update_slice(
            gain_full, other[None], ((chip ^ k) * 2 + 1 - core, 0, 0)
        )
    gain_full = gain_full.astype(F32).transpose(1, 0, 2).reshape(2, model)
    gain_one, gain_two = gain_full[0], gain_full[1]

    row_order = jnp.concatenate([chip_order * 2 + core, chip_order * 2 + 1 - core])

    def columns_of_chip(blocks):
        got = [blocks[0]] + [hop(blocks[k], k) for k in range(1, chips)]
        return place(got + [swap(b) for b in got], row_order, 0, BF16)

    x_blocks = gather_chips(tokens)
    q_blocks = pick_columns(w_query, chip, chips)
    kv_cols = jnp.stack([w_key.reshape(wrows, KVH, HD), w_value.reshape(wrows, KVH, HD)], axis=2)
    kv_cols = kv_cols.transpose(1, 0, 2, 3).reshape(KVH, wrows, 2 * HD)
    qkv_blocks = [
        jnp.concatenate(
            [
                q_blocks[k],
                lax.dynamic_index_in_dim(kv_cols, (chip ^ k) // kv_share, 0, keepdims=False),
            ],
            axis=1,
        )
        for k in range(chips)
    ]
    w_qkv = columns_of_chip(qkv_blocks)
    w_out_c = by_core(w_out, swap(w_out), 0)
    w_gate_c = columns_of_chip(pick_columns(w_gate, chip, chips))
    w_up_c = columns_of_chip(pick_columns(w_up, chip, chips))
    w_down_c = by_core(w_down, swap(w_down), 0)
    cot_rows = jnp.concatenate(gather_chips(cotangent), axis=0)

    lengths = lax.dynamic_index_in_dim(doc_lengths, rep, 0, keepdims=False)
    bounds = jnp.cumsum(lengths, dtype=jnp.int32)
    starts = chip_order * (2 * rows)
    within = jnp.arange(rows, dtype=jnp.int32)
    own_pos = (starts[:, None] + core * rows + within[None, :]).reshape(own)
    other_pos = (starts[:, None] + (1 - core) * rows + within[None, :]).reshape(own)
    key_pos = jnp.concatenate([own_pos, other_pos])

    def segment(pos):
        return jnp.sum((bounds[None, :] <= pos[:, None]).astype(jnp.int32), axis=1)

    q_seg, k_seg = segment(own_pos), segment(key_pos)
    q_valid, k_valid = q_seg < DOCS - 1, k_seg < DOCS - 1
    allowed = (key_pos[None, :] <= own_pos[:, None]) & (q_seg[:, None] == k_seg[None, :])
    allowed = allowed & q_valid[:, None] & k_valid[None, :] | (key_pos[None, :] == own_pos[:, None])
    valid_col = q_valid.astype(F32)[:, None]
    cos_table, sin_table = angle_tables(own_pos.astype(F32))

    x_rows = jnp.concatenate(x_blocks, axis=0).astype(F32)
    _, normed_rows = norm_parts(x_rows)
    hidden_one = (normed_rows * gain_one).astype(BF16)
    qkv = dot(hidden_one, w_qkv)
    scale = 1.0 / math.sqrt(HD)
    q_low = rotate(qkv[:, :qw].reshape(own, heads, HD), cos_table, sin_table).astype(BF16)
    k_low = rotate(qkv[:, qw : qw + HD].reshape(own, 1, HD), cos_table, sin_table)
    kv_low = jnp.concatenate([k_low.astype(BF16)[:, 0], qkv[:, qw + HD :].astype(BF16)], axis=1)
    kv_all = jnp.concatenate([kv_low, swap(kv_low)], axis=0)
    k_all, v_all = kv_all[:, :HD], kv_all[:, HD:]
    q_heads = q_low.transpose(1, 0, 2)

    def scores():
        s = jnp.einsum("htd,sd->hts", q_heads, k_all, preferred_element_type=F32) * scale
        return jnp.where(allowed[None], s, MASK_FILL)

    s = scores()
    highest = jnp.max(s, axis=-1, keepdims=True)
    weights = jnp.exp(s - highest)
    totals = jnp.sum(weights, axis=-1, keepdims=True)
    prob = (weights / totals).astype(BF16)
    logsum = highest + jnp.log(totals)
    mixed = jnp.einsum("hts,sd->htd", prob, v_all, preferred_element_type=F32)
    attn = (mixed.transpose(1, 0, 2).reshape(own, qw) * valid_col).astype(BF16)
    inputs = tokens.astype(F32)
    resid = inputs + scatter_chips(dot(attn, w_out_c))

    inv_two, normed_two = norm_parts(resid)
    hidden_two = jnp.concatenate(
        gather_chips((normed_two * gain_two).astype(BF16)), axis=0
    )
    gate = dot(hidden_two, w_gate_c)
    up = dot(hidden_two, w_up_c)
    sig = jax.nn.sigmoid(gate)
    silu = gate * sig
    inner = (silu * up).astype(BF16)
    result = (resid + scatter_chips(dot(inner, w_down_c))).astype(BF16)
    grad_inner = dot_nt(cot_rows, w_down_c)
    grad_gate = (grad_inner * up * sig * (1.0 + gate * (1.0 - sig))).astype(BF16)
    grad_up = (grad_inner * silu).astype(BF16)

    def pair_sum(partial, size):
        p = partial.astype(BF16)
        mine = lax.dynamic_index_in_dim(p, core, 0, keepdims=False)
        other = lax.dynamic_index_in_dim(p, 1 - core, 0, keepdims=False)
        return (mine.astype(F32) + swap(other).astype(F32)).astype(BF16)

    def rows_to_owner(partial):
        width = partial.shape[1]
        p = partial.astype(BF16).reshape(chips, 2, wrows, width).transpose(1, 0, 2, 3)
        p = pair_sum(p, width)
        sent = [lax.dynamic_index_in_dim(p, chip ^ k, 0, keepdims=False) for k in range(chips)]
        return [sent[0]] + [hop(sent[k], k) for k in range(1, chips)]

    down_rows = w_down.shape[0]
    down_part = pair_sum(
        dot_tn(inner, cot_rows).reshape(2, down_rows, model), down_rows
    )
    cuts = 4
    grad_down = jnp.concatenate(
        [chain(v) for v in jnp.split(down_part, cuts, axis=0)], axis=0
    ).astype(F32)

    gate_blocks = rows_to_owner(dot_tn(hidden_two, grad_gate))
    up_blocks = rows_to_owner(dot_tn(hidden_two, grad_up))
    grad_gate_out = place([chain(b) for b in gate_blocks], chip_order, 1, F32)
    grad_up_out = place([chain(b) for b in up_blocks], chip_order, 1, F32)

    grad_hidden_two = scatter_chips(dot_nt(grad_gate, w_gate_c) + dot_nt(grad_up, w_up_c))
    gain_two_local = jnp.sum(grad_hidden_two * normed_two, axis=0)
    grad_resid = cotangent.astype(F32) + norm_back(grad_hidden_two, normed_two, inv_two, gain_two)

    da = jnp.concatenate(gather_chips(grad_resid.astype(BF16)), axis=0)
    dob = dot_nt(da, w_out_c).astype(BF16) * q_valid.astype(BF16)[:, None]
    out_part = pair_sum(dot_tn(attn, da).reshape(2, wrows, model), wrows)
    grad_out = chain(out_part).astype(F32)
    dob_heads = dob.reshape(own, heads, HD).transpose(1, 0, 2)
    probs = jnp.exp(scores() - logsum)
    dp = jnp.einsum("htd,sd->hts", dob_heads, v_all, preferred_element_type=F32)
    inner_sum = jnp.sum(probs * dp, axis=-1, keepdims=True)
    ds = (probs * (dp - inner_sum)).astype(BF16)
    dq = jnp.einsum("hts,sd->htd", ds, k_all, preferred_element_type=F32) * scale
    dk = jnp.einsum("hts,htd->sd", ds, q_heads, preferred_element_type=F32) * scale
    dv = jnp.einsum("hts,htd->sd", probs.astype(BF16), dob_heads, preferred_element_type=F32)
    dkv = jnp.concatenate([dk, dv], axis=1)
    dkv = dkv[:own] + swap(dkv[own:].astype(BF16)).astype(F32)
    dq = rotate_back(dq.transpose(1, 0, 2), cos_table, sin_table).reshape(own, qw)
    dk = rotate_back(dkv[:, None, :HD], cos_table, sin_table)[:, 0]
    dqkv = jnp.concatenate([dq, dk, dkv[:, HD:]], axis=1).astype(BF16)
    grad_hidden_one = scatter_chips(dot_nt(dqkv, w_qkv))
    inv_one, normed_one = norm_parts(inputs)
    gain_one_local = jnp.sum(grad_hidden_one * normed_one, axis=0)
    grad_inputs = (
        grad_resid + norm_back(grad_hidden_one, normed_one, inv_one, gain_one)
    ).astype(BF16)
    qkv_blocks = [chain(b) for b in rows_to_owner(dot_tn(hidden_one, dqkv))]
    grad_query = place([b[:, :qw] for b in qkv_blocks], chip_order, 1, F32)
    kv_blocks = jnp.stack([b[:, qw:].astype(F32) for b in qkv_blocks])
    kv_abs = jnp.concatenate(
        [
            lax.dynamic_index_in_dim(kv_blocks, chip ^ a, 0, keepdims=True)
            for a in range(chips)
        ],
        axis=0,
    )
    kv_abs = kv_abs.reshape(KVH, kv_share, wrows, 2, HD).sum(axis=1)
    grad_key = kv_abs[:, :, 0].transpose(1, 0, 2).reshape(wrows, KVH * HD)
    grad_value = kv_abs[:, :, 1].transpose(1, 0, 2).reshape(wrows, KVH * HD)

    norms = jnp.stack([gain_one_local, gain_two_local])
    norms = norms.reshape(2, chips, 2, wrows).transpose(2, 1, 0, 3)
    mine = lax.dynamic_index_in_dim(norms, core, 0, keepdims=False)
    other = lax.dynamic_index_in_dim(norms, 1 - core, 0, keepdims=False)
    mine = mine + swap(other)
    total = lax.dynamic_index_in_dim(mine, chip, 0, keepdims=False)
    for k in range(1, chips):
        total = total + hop(lax.dynamic_index_in_dim(mine, chip ^ k, 0, keepdims=False), k)
    total = chain(total)
    return (
        result,
        grad_inputs,
        total[0],
        grad_query,
        grad_key,
        grad_value,
        grad_out,
        total[1],
        grad_gate_out,
        grad_up_out,
        grad_down,
    )


def solution(mesh):
    placed = (
        P(("rep", "fsdp"), None),
        P(("rep", "fsdp"), None),
        P(),
        P("fsdp"),
        P("fsdp", None),
        P("fsdp", None),
        P("fsdp", None),
        P("fsdp", None),
        P("fsdp"),
        P("fsdp", None),
        P("fsdp", None),
        P("fsdp", None),
    )
    return jax.shard_map(
        local,
        mesh=mesh,
        in_specs=placed,
        out_specs=(
            P(("rep", "fsdp"), None),
            P(("rep", "fsdp"), None),
            P("fsdp"),
            P("fsdp", None),
            P("fsdp", None),
            P("fsdp", None),
            P("fsdp", None),
            P("fsdp"),
            P("fsdp", None),
            P("fsdp", None),
            P("fsdp", None),
        ),
        check_vma=False,
    )
```

```python
import math

import jax
import jax.numpy as jnp
from jax import lax
from jax.experimental import pallas as pl
from jax.experimental.pallas import tpu as pltpu
from jax.sharding import PartitionSpec as P

H = 32
KVH = 4
HD = 64
DOCS = 8

NORM_EPS = 1e-05
ROPE_BASE = 10000.0
MASK_FILL = -1e30
F32 = jnp.float32
BF16 = jnp.bfloat16


def dot(a, b):
    return jnp.dot(a, b, preferred_element_type=F32)


def dot_nt(a, b):
    return lax.dot_general(a, b, (((1,), (1,)), ((), ())), preferred_element_type=F32)


def dot_tn(a, b):
    return lax.dot_general(a, b, (((0,), (0,)), ((), ())), preferred_element_type=F32)


def tiny():
    return pl.CostEstimate(flops=1024, bytes_accessed=1024, transcendentals=0)


def whole():
    return pl.BlockSpec(memory_space=pltpu.VMEM)


def turned(v):
    low = lax.broadcasted_iota(jnp.int32, v.shape, 1) % HD < HD // 2
    return jnp.where(low, pltpu.roll(v, 128 - HD // 2, 1), pltpu.roll(v, HD // 2, 1))


def scalars():
    return pl.BlockSpec(memory_space=pltpu.SMEM)


def pick_qkv(w_query, w_key, w_value, gain, chips):
    rows, cols = w_query.shape
    qw, share = cols // chips, chips // KVH

    def body(g_ref, q_ref, k_ref, v_ref, out_ref):
        gain = g_ref[...]
        out_ref[0, :, :qw] = (q_ref[...].astype(F32) * gain).astype(BF16)
        for n in range(KVH):

            @pl.when(pl.program_id(0) // share == n)
            def _():
                at = slice(n * HD, (n + 1) * HD)
                kv = jnp.concatenate([k_ref[:, at], v_ref[:, at]], axis=1)
                out_ref[0, :, qw:] = (kv.astype(F32) * gain).astype(BF16)

    small = pl.BlockSpec((rows, KVH * HD), lambda k: (0, 0))
    return pl.pallas_call(
        body,
        grid=(chips,),
        in_specs=[
            pl.BlockSpec((rows, 1), lambda k: (0, 0)),
            pl.BlockSpec((rows, qw), lambda k: (0, k)),
            small,
            small,
        ],
        out_specs=pl.BlockSpec((1, rows, qw + 2 * HD), lambda k: (k, 0, 0)),
        out_shape=jax.ShapeDtypeStruct((chips, rows, qw + 2 * HD), BF16),
        cost_estimate=tiny(),
        name="pick_qkv",
    )(gain, w_query, w_key, w_value)


def pick_half(w_gate, w_up, gain, ids, count):
    rows, cols = w_gate.shape
    width, part = cols // count, rows // 2
    if width % 128:
        out = []
        for w in (w_gate, w_up):
            v = lax.dynamic_slice_in_dim((w.astype(F32) * gain).astype(BF16), ids[2] * part, part)
            out.append(v.reshape(part, count, width).transpose(1, 0, 2))
        return out

    def body(s_ref, n_ref, a_ref, b_ref, c_ref, d_ref):
        c_ref[0] = (a_ref[...].astype(F32) * n_ref[...]).astype(BF16)
        d_ref[0] = (b_ref[...].astype(F32) * n_ref[...]).astype(BF16)

    return pl.pallas_call(
        body,
        grid_spec=pltpu.PrefetchScalarGridSpec(
            num_scalar_prefetch=1,
            grid=(count,),
            in_specs=[pl.BlockSpec((part, 1), lambda k, s: (s[2], 0))]
            + [pl.BlockSpec((part, width), lambda k, s: (s[2], k))] * 2,
            out_specs=[pl.BlockSpec((1, part, width), lambda k, s: (k, 0, 0))] * 2,
        ),
        out_shape=[jax.ShapeDtypeStruct((count, part, width), BF16)] * 2,
        cost_estimate=tiny(),
        name="pick_half",
    )(ids, gain, w_gate, w_up)


def join_cores(ids, near, far):
    rows, cols = near.shape

    def body(s_ref, a_ref, b_ref, out_ref):
        @pl.when(pl.program_id(0) == 0)
        def _():
            out_ref[...] = a_ref[...]

        @pl.when(pl.program_id(0) == 1)
        def _():
            out_ref[...] = b_ref[...]

    return pl.pallas_call(
        body,
        grid_spec=pltpu.PrefetchScalarGridSpec(
            num_scalar_prefetch=1,
            grid=(2,),
            in_specs=[pl.BlockSpec((rows, cols), lambda f, s: (0, 0))] * 2,
            out_specs=pl.BlockSpec((rows, cols), lambda f, s: (s[1] ^ f, 0)),
        ),
        out_shape=jax.ShapeDtypeStruct((2 * rows, cols), near.dtype),
        cost_estimate=tiny(),
        name="join_cores",
    )(ids, near, far)


def qkv_kernel(ids, x_blocks, near, far, cos_table, sin_table):
    rows, model = x_blocks[0].shape
    chips = len(x_blocks)
    own = rows * chips
    wrows, width = near.shape[1:]
    qw = width - 2 * HD

    def body(c_ref, cos_ref, sin_ref, n_ref, f_ref, *refs):
        x_refs, (z_ref, q_ref, kv_ref, w_ref) = refs[:chips], refs[chips:]
        chip, core = c_ref[0], c_ref[1]
        for k in range(chips):
            at = pl.multiple_of((2 * k + core) * wrows, wrows)
            w_ref[pl.ds(at, wrows), :] = n_ref[k]
            at = pl.multiple_of((2 * k + 1 - core) * wrows, wrows)
            w_ref[pl.ds(at, wrows), :] = f_ref[k]
            x = x_refs[k][...].astype(F32)
            inv = lax.rsqrt(jnp.mean(x * x, axis=-1, keepdims=True) + NORM_EPS)
            at = pl.multiple_of((chip ^ k) * rows, rows)
            z_ref[pl.ds(at, rows), :] = (x * inv).astype(BF16)
        total = dot(z_ref[...], w_ref[...])
        cos, sin = cos_ref[...], sin_ref[...]
        for j in range(qw // 128):
            v = total[:, j * 128 : (j + 1) * 128]
            q_ref[:, j * 128 : (j + 1) * 128] = (v * cos + turned(v) * sin).astype(BF16)
        v = total[:, qw:]
        key = lax.broadcasted_iota(jnp.int32, v.shape, 1) < HD
        kv_ref[...] = jnp.where(key, v * cos + turned(v) * sin, v).astype(BF16)

    return pl.pallas_call(
        body,
        in_specs=[scalars()] + [whole()] * (4 + chips),
        out_specs=[whole()] * 4,
        out_shape=[
            jax.ShapeDtypeStruct((own, model), BF16),
            jax.ShapeDtypeStruct((own, qw), BF16),
            jax.ShapeDtypeStruct((own, 2 * HD), BF16),
            jax.ShapeDtypeStruct((2 * chips * wrows, width), BF16),
        ],
        cost_estimate=tiny(),
        name="qkv_forward",
    )(ids, cos_table, sin_table, near, far, *x_blocks)


def attention_mask(s_ref, l_ref, rows, own):
    core, rep, block = s_ref[1], s_ref[4], pl.program_id(0)

    def coded(pos):
        bound, code = 0, jnp.zeros(pos.shape, jnp.int32)
        for n in range(DOCS):
            bound = bound + l_ref[rep, n]
            code = code + jnp.where(pos >= bound, 1, 0)
        return jnp.where(code < DOCS - 1, code, 1000 + pos)

    q_pos = (2 * block + core) * rows + lax.broadcasted_iota(jnp.int32, (rows, 1), 0)
    index = lax.broadcasted_iota(jnp.int32, (1, 2 * own), 1)
    side = jnp.where(index < own, core, 1 - core)
    index = jnp.where(index < own, index, index - own)
    k_pos = (2 * (index // rows) + side) * rows + index % rows
    q_code = coded(q_pos)
    allowed = (coded(k_pos) == q_code) & (k_pos <= q_pos)
    return jnp.where(allowed, 0.0, MASK_FILL), jnp.where(q_code < DOCS, 1.0, 0.0)


def attention_forward(ids, lengths, q, kv_own, kv_other, rows):
    own, qw = q.shape
    heads = qw // HD
    scale = 1.0 / math.sqrt(HD)

    def body(s_ref, d_ref, q_ref, a_ref, b_ref, o_ref, l_ref):
        bias, valid = attention_mask(s_ref, d_ref, rows, own)
        lane = lax.broadcasted_iota(jnp.int32, (rows, 128), 1)
        k_a, v_a = a_ref[:, :HD], a_ref[:, HD:]
        k_b, v_b = b_ref[:, :HD], b_ref[:, HD:]
        sums = jnp.zeros((rows, 128), F32)
        pair = []
        for h in range(heads):
            qh = q_ref[:, h * HD : (h + 1) * HD] * jnp.asarray(scale, BF16)
            s = jnp.concatenate([dot_nt(qh, k_a), dot_nt(qh, k_b)], axis=1) + bias
            top = jnp.max(s, axis=-1, keepdims=True)
            p = jnp.exp(s - top)
            tot = jnp.sum(p, axis=-1, keepdims=True)
            p = (p * (1.0 / tot)).astype(BF16)
            mixed = dot(p[:, :own], v_a) + dot(p[:, own:], v_b)
            pair.append((mixed * valid).astype(BF16))
            sums = jnp.where(lane == h, top + jnp.log(tot), sums)
            if h % 2:
                o_ref[:, (h - 1) * HD : (h + 1) * HD] = jnp.concatenate(pair, axis=1)
                pair = []
        l_ref[...] = sums

    return pl.pallas_call(
        body,
        grid=(own // rows,),
        in_specs=[
            scalars(),
            scalars(),
            pl.BlockSpec((rows, qw), lambda i: (i, 0)),
            pl.BlockSpec((own, 2 * HD), lambda i: (0, 0)),
            pl.BlockSpec((own, 2 * HD), lambda i: (0, 0)),
        ],
        out_specs=[
            pl.BlockSpec((rows, qw), lambda i: (i, 0)),
            pl.BlockSpec((rows, 128), lambda i: (i, 0)),
        ],
        out_shape=[
            jax.ShapeDtypeStruct((own, qw), BF16),
            jax.ShapeDtypeStruct((own, 128), F32),
        ],
        cost_estimate=tiny(),
        name="attention_forward",
    )(ids, lengths, q, kv_own, kv_other)


def attention_backward(
    ids, lengths, q, kv_own, kv_other, sums, d_out, cos_table, sin_table, rows
):
    own, qw = q.shape
    heads = qw // HD
    scale = 1.0 / math.sqrt(HD)
    seq_len = 2 * own

    def body(
        s_ref, n_ref, q_ref, a_ref, b_ref, l_ref, d_ref, cos_ref, sin_ref, dq_ref, dkv_ref,
    ):
        @pl.when(pl.program_id(0) == 0)
        def _():
            dkv_ref[...] = jnp.zeros_like(dkv_ref)

        bias, valid = attention_mask(s_ref, n_ref, rows, own)
        valid = valid.astype(BF16)
        k_a, v_a = a_ref[:, :HD], a_ref[:, HD:]
        k_b, v_b = b_ref[:, :HD], b_ref[:, HD:]
        cos, sin = cos_ref[...], sin_ref[...]
        pair = []
        dk = jnp.zeros((seq_len, HD), F32)
        dv = jnp.zeros((seq_len, HD), F32)
        for h in range(heads):
            qh = q_ref[:, h * HD : (h + 1) * HD] * jnp.asarray(scale, BF16)
            dh = d_ref[:, h * HD : (h + 1) * HD] * valid
            s = jnp.concatenate([dot_nt(qh, k_a), dot_nt(qh, k_b)], axis=1) + bias
            p = jnp.exp(s - l_ref[:, h : h + 1])
            dp = jnp.concatenate([dot_nt(dh, v_a), dot_nt(dh, v_b)], axis=1)
            inner = jnp.sum(p * dp, axis=-1, keepdims=True)
            ds = (p * (dp - inner)).astype(BF16)
            dq = (dot(ds[:, :own], k_a) + dot(ds[:, own:], k_b)) * scale
            dk = dk + dot_tn(ds, qh)
            dv = dv + dot_tn(p.astype(BF16), dh)
            pair.append(dq)
            if h % 2:
                v = jnp.concatenate(pair, axis=1)
                dq_ref[:, (h - 1) * HD : (h + 1) * HD] = (v * cos - turned(v) * sin).astype(BF16)
                pair = []
        dkv_ref[...] += jnp.concatenate([dk, dv], axis=1)

    return pl.pallas_call(
        body,
        grid=(own // rows,),
        in_specs=[
            scalars(),
            scalars(),
            pl.BlockSpec((rows, qw), lambda i: (i, 0)),
            pl.BlockSpec((own, 2 * HD), lambda i: (0, 0)),
            pl.BlockSpec((own, 2 * HD), lambda i: (0, 0)),
            pl.BlockSpec((rows, 128), lambda i: (i, 0)),
            pl.BlockSpec((rows, qw), lambda i: (i, 0)),
            pl.BlockSpec((rows, 128), lambda i: (i, 0)),
            pl.BlockSpec((rows, 128), lambda i: (i, 0)),
        ],
        out_specs=[
            pl.BlockSpec((rows, qw), lambda i: (i, 0)),
            pl.BlockSpec((seq_len, 2 * HD), lambda i: (0, 0)),
        ],
        out_shape=[
            jax.ShapeDtypeStruct((own, qw), BF16),
            jax.ShapeDtypeStruct((seq_len, 2 * HD), F32),
        ],
        cost_estimate=tiny(),
        name="attention_backward",
    )(ids, lengths, q, kv_own, kv_other, sums, d_out, cos_table, sin_table)


def out_proj(ids, attn, near, far, chips):
    own, depth = attn.shape
    wrows, model = near.shape
    rows = own // chips

    def body(c_ref, a_ref, n_ref, f_ref, *outs):
        chip, core, w_ref = c_ref[0], c_ref[1], outs[-1]
        w_ref[pl.ds(pl.multiple_of(core * wrows, wrows), wrows), :] = n_ref[...]
        w_ref[pl.ds(pl.multiple_of((1 - core) * wrows, wrows), wrows), :] = f_ref[...]
        for k in range(chips):
            at = pl.multiple_of((chip ^ k) * rows, rows)
            outs[k][...] = dot(a_ref[pl.ds(at, rows), :], w_ref[...]).astype(BF16)

    return pl.pallas_call(
        body,
        in_specs=[scalars()] + [whole()] * 3,
        out_specs=[whole()] * (chips + 1),
        out_shape=[jax.ShapeDtypeStruct((rows, model), BF16)] * chips
        + [jax.ShapeDtypeStruct((depth, model), BF16)],
        cost_estimate=tiny(),
        name="out_proj",
    )(ids, attn, near, far)


def residual_norm(tokens, parts):
    rows, model = tokens.shape

    def body(x_ref, *refs):
        y_ref, z_ref = refs[-2:]
        y = x_ref[...].astype(F32)
        for p in refs[:-2]:
            y = y + p[...].astype(F32)
        y_ref[...] = y
        inv = lax.rsqrt(jnp.mean(y * y, axis=-1, keepdims=True) + NORM_EPS)
        z_ref[...] = (y * inv).astype(BF16)

    return pl.pallas_call(
        body,
        in_specs=[whole()] * (1 + len(parts)),
        out_specs=[whole()] * 2,
        out_shape=[
            jax.ShapeDtypeStruct((rows, model), F32),
            jax.ShapeDtypeStruct((rows, model), BF16),
        ],
        cost_estimate=tiny(),
        name="residual_norm",
    )(tokens, *parts)


def residual_norm_back(base, parts, y, copies):
    rows, model = y.shape
    count = parts.shape[0] // rows

    def body(b_ref, y_ref, p_ref, f_ref, l_ref, n_ref):
        e = p_ref[:rows, :].astype(F32)
        for i in range(1, count):
            e = e + p_ref[i * rows : (i + 1) * rows, :].astype(F32)
        v = y_ref[...].astype(F32)
        inv = lax.rsqrt(jnp.mean(v * v, axis=-1, keepdims=True) + NORM_EPS)
        z = v * inv
        ez = e * z
        n_ref[...] = jnp.sum(ez, axis=0, keepdims=True)
        out = b_ref[...].astype(F32) + inv * (e - z * jnp.mean(ez, axis=-1, keepdims=True))
        f_ref[...] = out
        for i in range(copies):
            l_ref[i * rows : (i + 1) * rows, :] = out.astype(BF16)

    return pl.pallas_call(
        body,
        in_specs=[whole()] * 3,
        out_specs=[whole()] * 3,
        out_shape=[
            jax.ShapeDtypeStruct((rows, model), F32),
            jax.ShapeDtypeStruct((copies * rows, model), BF16),
            jax.ShapeDtypeStruct((1, model), F32),
        ],
        cost_estimate=tiny(),
        name="residual_norm_back",
    )(base, y, parts)


def feed_forward(ids, z_blocks, cot, weights, w_down):
    rows, model = z_blocks[0].shape
    chips = len(z_blocks)
    part, width = weights[0][0].shape[1:]
    own, tile = rows * chips, 256

    def body(s_ref, *refs):
        z_refs, c_ref, w_refs = refs[:chips], refs[chips], refs[chips + 1 : chips + 9]
        d_ref, m_ref, dg_ref, du_ref, z_ref, g_ref, u_ref = refs[chips + 9 :]
        chip, core, half = s_ref[0], s_ref[1], s_ref[2]

        @pl.when(pl.program_id(0) == 0)
        def _():
            for k in range(chips):
                at = pl.multiple_of((chip ^ k) * rows, rows)
                z_ref[pl.ds(at, rows), :] = z_refs[k][...]

        for w, out in ((w_refs[:4], g_ref), (w_refs[4:], u_ref)):
            for i in range(4):
                side = core if i < 2 else 1 - core
                piece = half if i % 2 == 0 else 1 - half
                for j in range(chips):
                    at = pl.multiple_of((2 * (2 * j + side) + piece) * part, part)
                    out[pl.ds(at, part), :] = w[i][j]
        gate = dot(z_ref[...], g_ref[...])
        up = dot(z_ref[...], u_ref[...])
        sig = 1.0 / (1.0 + jnp.exp(-gate))
        silu = gate * sig
        m_ref[...] = (silu * up).astype(BF16)
        dm = dot_nt(c_ref[...], d_ref[...])
        dg_ref[...] = (dm * up * sig * (1.0 + gate * (1.0 - sig))).astype(BF16)
        du_ref[...] = (dm * silu).astype(BF16)

    joined = pl.BlockSpec((own, model), lambda n, s: (0, 0))
    out_tile = pl.BlockSpec((own, tile), lambda n, s: (0, n))
    return pl.pallas_call(
        body,
        grid_spec=pltpu.PrefetchScalarGridSpec(
            num_scalar_prefetch=1,
            grid=(pl.cdiv(width, tile),),
            in_specs=[pl.BlockSpec((rows, model), lambda n, s: (0, 0))] * chips
            + [joined]
            + [pl.BlockSpec((chips, part, tile), lambda n, s: (0, 0, n))] * 8
            + [pl.BlockSpec((tile, model), lambda n, s: (n, 0))],
            out_specs=[out_tile] * 3
            + [joined]
            + [pl.BlockSpec((model, tile), lambda n, s: (0, n))] * 2,
        ),
        out_shape=[jax.ShapeDtypeStruct((own, width), BF16)] * 3
        + [jax.ShapeDtypeStruct((own, model), BF16)]
        + [jax.ShapeDtypeStruct((model, width), BF16)] * 2,
        cost_estimate=tiny(),
        name="feed_forward",
    )(ids, *z_blocks, cot, *weights[0], *weights[1], w_down)


def strips(value, ref, lead=()):
    rows, width = value.shape
    for t in range(pl.cdiv(width, 128)):
        v = value[:, t * 128 : (t + 1) * 128]
        if v.shape[1] < 128:
            v = jnp.concatenate([v, jnp.zeros((rows, 128 - v.shape[1]), v.dtype)], axis=1)
        ref[(*lead, slice(t * rows, (t + 1) * rows), slice(None))] = v


def weight_grad(ids, left, right, chips):
    own, model = left.shape
    width = right.shape[1]
    rows = model // (2 * chips)
    long = pl.cdiv(width, 128) * rows
    group = min(4, chips)
    turns = chips // group

    def body(c_ref, l_ref, r_ref, near_ref, far_ref):
        step = pl.program_id(0)
        near = step >= turns
        side = jnp.where(near, c_ref[1], 1 - c_ref[1])
        first = jnp.where(near, step - turns, step) * group
        blocks = []
        for j in range(group):
            at = pl.multiple_of((2 * (first + j) + side) * rows, rows)
            blocks.append(l_ref[:, pl.ds(at, rows)])
        out = dot_tn(jnp.concatenate(blocks, axis=1), r_ref[...]).astype(BF16)

        @pl.when(near)
        def _():
            for j in range(group):
                strips(out[j * rows : (j + 1) * rows], near_ref, (j,))

        @pl.when(step < turns)
        def _():
            for j in range(group):
                strips(out[j * rows : (j + 1) * rows], far_ref, (j,))

    return pl.pallas_call(
        body,
        grid_spec=pltpu.PrefetchScalarGridSpec(
            num_scalar_prefetch=1,
            grid=(2 * turns,),
            in_specs=[
                pl.BlockSpec((own, model), lambda t, c: (0, 0)),
                pl.BlockSpec((own, width), lambda t, c: (0, 0)),
            ],
            out_specs=[
                pl.BlockSpec((group, long, 128), lambda t, c: (jnp.maximum(t - turns, 0), 0, 0)),
                pl.BlockSpec((group, long, 128), lambda t, c: (jnp.minimum(t, turns - 1), 0, 0)),
            ],
        ),
        out_shape=[jax.ShapeDtypeStruct((chips, long, 128), BF16)] * 2,
        cost_estimate=tiny(),
        name="weight_grad",
    )(ids, left, right)


def row_grad(ids, left, right, cuts):
    own, depth = left.shape
    model = right.shape[1]
    rows, width = depth // 2, model // cuts
    long = width // 128 * rows

    def body(c_ref, l_ref, r_ref, near_ref, far_ref, full_ref):
        core = c_ref[1]
        full_ref[...] = dot_tn(l_ref[...], r_ref[...])
        near = full_ref[pl.ds(pl.multiple_of(core * rows, 8), rows), :]
        far = full_ref[pl.ds(pl.multiple_of((1 - core) * rows, 8), rows), :]
        strips(near.astype(BF16), near_ref, (0,))
        strips(far.astype(BF16), far_ref, (0,))

    out = pl.BlockSpec((1, long, 128), lambda n, c: (n, 0, 0))
    return pl.pallas_call(
        body,
        grid_spec=pltpu.PrefetchScalarGridSpec(
            num_scalar_prefetch=1,
            grid=(cuts,),
            in_specs=[
                pl.BlockSpec((own, depth), lambda n, c: (0, 0)),
                pl.BlockSpec((own, width), lambda n, c: (0, n)),
            ],
            out_specs=[out] * 2,
            scratch_shapes=[pltpu.VMEM((depth, width), F32)],
        ),
        out_shape=[jax.ShapeDtypeStruct((cuts, long, 128), BF16)] * 2,
        cost_estimate=tiny(),
        name="row_grad",
    )(ids, left, right)


def beside(blocks, rows, width, scale=None):
    count = len(blocks)
    tiles = pl.cdiv(width, 128)
    if scale is None:
        scale = jnp.ones((rows, 1), F32)
    if width % 128:
        full = [b.reshape(tiles, rows, 128).transpose(1, 0, 2).reshape(rows, -1) for b in blocks]
        return jnp.concatenate([f[:, :width] for f in full], axis=1).astype(F32) * scale

    def body(s_ref, *refs):
        scale, out_ref = s_ref[...], refs[-1]
        for k in range(count):

            @pl.when(pl.program_id(0) == k)
            def _():
                for t in range(tiles):
                    v = refs[k][t * rows : (t + 1) * rows, :].astype(F32)
                    out_ref[:, t * 128 : (t + 1) * 128] = v * scale

    return pl.pallas_call(
        body,
        grid=(count,),
        in_specs=[pl.BlockSpec((rows, 1), lambda k: (0, 0))]
        + [pl.BlockSpec((tiles * rows, 128), lambda k: (0, 0))] * count,
        out_specs=pl.BlockSpec((rows, width), lambda k: (0, k)),
        out_shape=jax.ShapeDtypeStruct((rows, count * width), F32),
        cost_estimate=tiny(),
        name="beside",
    )(scale, *blocks)


def chain_step(ids, own, outer, sent, inner, total, coming):
    def size(v):
        return 0 if v is None else v.shape[0]

    ins = [own, outer, sent, inner, total, coming]
    have = [v is not None for v in ins]
    sizes = [size(own), size(sent), max(size(sent), size(coming)), size(total)]
    wanted = [have[0], have[2], have[2] and have[5], have[4]]

    def body(s_ref, *refs):
        refs = list(refs)
        o_ref, x_ref, i_ref, y_ref, t_ref, c_ref = [refs.pop(0) if h else None for h in have]
        s_out, t_out, a_out, f_out = [refs.pop(0) if w else None for w in wanted]
        ends = s_ref[3] == 1
        if s_out is not None:
            s_out[...] = (o_ref[...].astype(F32) + x_ref[: size(own)].astype(F32)).astype(BF16)
        if t_out is not None:
            t_out[...] = (i_ref[...].astype(F32) + y_ref[...].astype(F32)).astype(BF16)
        if f_out is not None:
            f_out[...] = jnp.where(ends, x_ref[: size(total)], t_ref[...])
        if a_out is not None:

            @pl.when(ends)
            def _():
                a_out[: size(coming)] = c_ref[...]

            @pl.when(jnp.logical_not(ends))
            def _():
                a_out[: size(sent)] = t_out[...]

    outs = pl.pallas_call(
        body,
        in_specs=[scalars()] + [whole()] * sum(have),
        out_specs=[whole()] * sum(wanted),
        out_shape=[jax.ShapeDtypeStruct((n, 128), BF16) for n, w in zip(sizes, wanted) if w],
        cost_estimate=tiny(),
        name="chain_step",
    )(ids, *[v for v in ins if v is not None])
    outs = list(outs)
    return [outs.pop(0) if w else None for w in wanted]


def local(
    tokens,
    cotangent,
    doc_lengths,
    norm1_gain,
    w_query,
    w_key,
    w_value,
    w_out,
    norm2_gain,
    w_gate,
    w_up,
    w_down,
):
    rows, model = tokens.shape
    group = lax.axis_size("fsdp")
    reps = lax.axis_size("rep")
    chips = group // 2
    dev = lax.axis_index("fsdp").astype(jnp.int32)
    rep = lax.axis_index("rep").astype(jnp.int32)
    chip, core, half = dev >> 1, dev & 1, rep & 1
    ends = jnp.where((rep == 0) | (rep == reps - 1), 1, 0).astype(jnp.int32)
    ids = jnp.stack([chip, core, half, ends, rep])
    seq_len = rows * group
    own = rows * chips
    wrows = w_query.shape[0]
    width = w_gate.shape[1] // chips
    kv_share = chips // KVH
    qw = H // chips * HD
    tie = lax.optimization_barrier
    sides = [[2 * k + c for k in range(chips)] for c in range(2)]

    def exchange(v):
        return lax.all_to_all(v, "fsdp", 0, 0, axis_index_groups=sides, tiled=True)

    def hop(v, k):
        return lax.ppermute(v, "fsdp", [(i, i ^ (2 * k)) for i in range(group)])

    def hops(blocks):
        return [blocks[0]] + [hop(blocks[k], k) for k in range(1, chips)]

    def swap(v):
        return lax.ppermute(v, "fsdp", [(i, i ^ 1) for i in range(group)])

    def trade(v):
        return lax.ppermute(v, "rep", [(i, i ^ 1) for i in range(reps)])

    def copies(v):
        return jnp.broadcast_to(v[None], (chips,) + v.shape).reshape(chips * v.shape[0], -1)

    sums_of = {}
    outer_pairs = [(0, 1), (1, 0), (2, 3), (3, 2)]

    class Line:
        def __init__(self):
            self.own = self.sent = self.total = self.outer = self.inner = None

        def busy(self):
            return any(v is not None for v in (self.own, self.sent, self.total))

    lines = [Line(), Line()]
    turn = [0]

    def visit(*carry, new=None):
        if reps != 4:
            if new is not None:
                sums_of[new[0]] = lax.psum(new[1], "rep")
            return carry if len(carry) != 1 else carry[0]
        line = lines[turn[0] % 2]
        turn[0] += 1
        extra = [line.outer, line.inner, None if new is None else new[1]]
        tied = tie(tuple(carry) + tuple(v for v in extra if v is not None))
        carry, tied = tied[: len(carry)], list(tied[len(carry) :])
        outer, inner, coming = [None if v is None else tied.pop(0) for v in extra]
        value = lambda pair: None if pair is None else pair[1]
        if outer is None:
            ahead = coming
        else:
            own_sum, middle, ahead, final = chain_step(
                ids, value(line.own), outer, value(line.sent), inner, value(line.total), coming
            )
            if final is not None:
                sums_of[line.total[0]] = final
            line.total = None if middle is None else (line.sent[0], middle)
            line.sent = None if own_sum is None else (line.own[0], own_sum)
            if ahead is None:
                ahead = coming if coming is not None else middle
        line.own = None if coming is None else (new[0], coming)
        line.outer = None if ahead is None else lax.ppermute(ahead, "rep", outer_pairs)
        line.inner = (
            None if line.sent is None else lax.ppermute(line.sent[1], "rep", [(1, 2), (2, 1)])
        )
        return carry if len(carry) != 1 else carry[0]

    starts = 2 * rows * jnp.arange(chips, dtype=jnp.int32) + core * rows
    own_pos = (starts[:, None] + jnp.arange(rows, dtype=jnp.int32)[None, :]).reshape(own)
    lane = jnp.arange(128)
    inverse = jnp.exp(-math.log(ROPE_BASE) / (HD // 2) * (lane % (HD // 2)).astype(F32))
    angles = own_pos.astype(F32)[:, None] * inverse[None, :]
    cos_table = jnp.cos(angles)
    sin_table = jnp.sin(angles) * jnp.where(lane % HD < HD // 2, -1.0, 1.0)[None, :]

    gain_one = norm1_gain.astype(F32)[:, None]
    gain_two = norm2_gain.astype(F32)[:, None]
    x_blocks = hops([tokens] * chips)
    qkv_near = exchange(pick_qkv(w_query, w_key, w_value, gain_one, chips))
    gate_part, up_part = pick_half(w_gate, w_up, gain_two, ids, chips)
    w_out_far = swap(w_out)
    w_down_c = join_cores(ids, w_down, swap(w_down))
    *x_blocks, qkv_near, cos_table, sin_table, gate_part, up_part, w_out_far, w_down_c = tie(
        (*x_blocks, qkv_near, cos_table, sin_table, gate_part, up_part, w_out_far, w_down_c)
    )
    gate_near = exchange(gate_part)
    normed_one, queries, kv_near, w_qkv = qkv_kernel(
        ids, x_blocks, qkv_near, swap(qkv_near), cos_table, sin_table
    )
    queries, gate_near, up_part, cot = tie((queries, gate_near, up_part, cotangent))
    up_near = exchange(up_part)
    gate_traded = trade(gate_near)
    kv_far = swap(kv_near)
    attn, sums = attention_forward(ids, doc_lengths, queries, kv_near, kv_far, rows)
    attn, up_near = tie((attn, up_near))
    up_traded = trade(up_near)
    *mixed, w_out_c = out_proj(ids, attn, w_out, w_out_far, chips)
    *mixed, cot = tie((*mixed, cot))
    parts = hops(mixed)
    cot_rows = exchange(copies(cot))
    *parts, gate_traded = tie((*parts, gate_traded))
    resid, normed = residual_norm(tokens, parts)
    z_blocks = hops([normed] * chips)
    weights = [
        [near, far, swap(near), swap(far)]
        for near, far in ((gate_near, gate_traded), (up_near, up_traded))
    ]
    inner, grad_gate, grad_up, normed_two, w_gate_c, w_up_c = feed_forward(
        ids, z_blocks, cot_rows, weights, w_down_c
    )

    down_near, down_far = row_grad(ids, inner, cot_rows, 4)
    down_far = swap(down_far)
    grad_gate, grad_up, down_near = tie((grad_gate, grad_up, down_near))
    back = (dot_nt(grad_gate, w_gate_c) + dot_nt(grad_up, w_up_c)).astype(BF16)
    back, down_near, down_far, grad_gate = tie((back, down_near, down_far, grad_gate))
    parts = exchange(back)
    down = [down_near[k] + down_far[k] for k in range(4)]
    grad_gate = visit(grad_gate, new=("down0", down[0]))
    gate_near, gate_far = weight_grad(ids, normed_two, grad_gate, chips)
    gate_near, gate_far, grad_up = visit(gate_near, gate_far, grad_up, new=("down1", down[1]))
    gate_far = swap(gate_far)
    up_near, up_far = weight_grad(ids, normed_two, grad_up, chips)
    up_near, up_far, parts = visit(up_near, up_far, parts, new=("down2", down[2]))
    gate_part = exchange(gate_near + gate_far)
    up_far = swap(up_far)
    grad_resid, da, gain_two_local = residual_norm_back(cotangent, parts, resid, chips)
    da, inner = visit(da, inner, new=("down3", down[3]))
    out = dot(inner, w_down_c).astype(BF16)
    up_part = up_near + up_far
    out, up_part, gate_part = visit(out, up_part, gate_part, new=None)
    da = exchange(da)
    da, up_part = visit(da, up_part, new=("gate0", gate_part[0]))
    up_part = exchange(up_part)
    dob = dot_nt(da, w_out_c).astype(BF16)
    out_near, out_far = row_grad(ids, attn, da, 2)
    dob, out_near, out_far = visit(dob, out_near, out_far, new=("gate1", gate_part[1]))
    out_far = swap(out_far)
    dq, dkv = attention_backward(
        ids, doc_lengths, queries, kv_near, kv_far, sums, dob, cos_table, sin_table, rows
    )
    dq, dkv = visit(dq, dkv, new=("gate2", gate_part[2]))
    dkv = dkv[:own] + swap(dkv[own:].astype(BF16)).astype(F32)
    half_turn = jnp.concatenate([dkv[:, HD // 2 : HD], dkv[:, : HD // 2]], axis=1)
    dk = dkv[:, :HD] * cos_table[:, :HD] - half_turn * sin_table[:, :HD]
    dqkv = jnp.concatenate([dq, dk.astype(BF16), dkv[:, HD:].astype(BF16)], axis=1)
    back = dot_nt(dqkv, w_qkv).astype(BF16)
    dqkv, back, up_part = visit(dqkv, back, up_part, new=("gate3", gate_part[3]))
    parts = exchange(back)
    qkv_near, qkv_far = weight_grad(ids, normed_one, dqkv, chips)
    qkv_near, qkv_far = visit(qkv_near, qkv_far, new=("up0", up_part[0]))
    qkv_part = qkv_near + swap(qkv_far)
    qkv_part, parts = visit(qkv_part, parts, new=("up1", up_part[1]))
    qkv_part = exchange(qkv_part)
    _, grad_inputs, gain_one_local = residual_norm_back(grad_resid, parts, tokens, 1)
    gain_one_local = visit(gain_one_local, new=("up2", up_part[2]))
    norms = jnp.concatenate([gain_one_local, gain_two_local], axis=0)
    norms = norms.reshape(2, chips, 2, wrows).transpose(2, 1, 0, 3)
    mine = lax.dynamic_index_in_dim(norms, core, 0, keepdims=False)
    other = lax.dynamic_index_in_dim(norms, 1 - core, 0, keepdims=False)
    norms = mine + swap(other)
    out_part = out_near + out_far
    norms, qkv_part, out_part = visit(norms, qkv_part, out_part, new=("up3", up_part[3]))
    parts = exchange(out).reshape(chips, rows, model)
    visit(new=("out0", out_part[0]))
    parts = visit(parts, new=("out1", out_part[1]))
    norms = jnp.sum(exchange(norms), axis=0)
    result = (resid + jnp.sum(parts.astype(F32), axis=0)).astype(BF16)
    qkv_part = qkv_part.reshape(2, chips // 2 * qkv_part.shape[1], 128)
    visit(new=("qkv0", qkv_part[0]))
    norms = visit(norms, new=("qkv1", qkv_part[1]))
    if reps == 4:
        norms = norms + lax.ppermute(norms, "rep", [(0, 1), (3, 2)])
        norms = norms + lax.ppermute(norms, "rep", [(1, 2), (2, 1)])
        norms = jnp.where(ends == 1, lax.ppermute(norms, "rep", [(1, 0), (2, 3)]), norms)
    else:
        norms = lax.psum(norms, "rep")
        for k in range(4, chips):
            visit(new=(f"gate{k}", gate_part[k]))
            visit(new=(f"up{k}", up_part[k]))
    while any(line.busy() for line in lines):
        visit()

    def summed(name, count):
        return [sums_of[f"{name}{k}"] for k in range(count)]

    qkv = jnp.concatenate(summed("qkv", 2)).reshape(chips, -1, 128)
    grad_query = beside([b[: qw // 128 * wrows] for b in qkv], wrows, qw, gain_one)
    kv = qkv[:, qw // 128 * wrows :].astype(F32).reshape(KVH, kv_share, wrows, 2, HD).sum(axis=1)
    kv = kv * gain_one[None, :, :, None]
    grad_key = kv[:, :, 0].transpose(1, 0, 2).reshape(wrows, KVH * HD)
    grad_value = kv[:, :, 1].transpose(1, 0, 2).reshape(wrows, KVH * HD)
    return (
        result,
        grad_inputs,
        norms[0] / gain_one[:, 0],
        grad_query,
        grad_key,
        grad_value,
        beside(summed("out", 2), wrows, model // 2),
        norms[1] / gain_two[:, 0],
        beside(summed("gate", chips), wrows, width, gain_two),
        beside(summed("up", chips), wrows, width, gain_two),
        beside(summed("down", 4), w_down.shape[0], model // 4),
    )


def solution(mesh):
    placed = (
        P(("rep", "fsdp"), None),
        P(("rep", "fsdp"), None),
        P(),
        P("fsdp"),
        P("fsdp", None),
        P("fsdp", None),
        P("fsdp", None),
        P("fsdp", None),
        P("fsdp"),
        P("fsdp", None),
        P("fsdp", None),
        P("fsdp", None),
    )
    return jax.shard_map(
        local,
        mesh=mesh,
        in_specs=placed,
        out_specs=(
            P(("rep", "fsdp"), None),
            P(("rep", "fsdp"), None),
            P("fsdp"),
            P("fsdp", None),
            P("fsdp", None),
            P("fsdp", None),
            P("fsdp", None),
            P("fsdp"),
            P("fsdp", None),
            P("fsdp", None),
            P("fsdp", None),
        ),
        check_vma=False,
    )
```

```python
import math

import jax
import jax.numpy as jnp
from jax import lax
from jax.experimental import pallas as pl
from jax.experimental.pallas import tpu as pltpu
from jax.sharding import PartitionSpec as P

H = 32
KVH = 4
HD = 64
DOCS = 8

NORM_EPS = 1e-05
ROPE_BASE = 10000.0
MASK_FILL = -1e30
TILE = 512
F32 = jnp.float32
BF16 = jnp.bfloat16


def dot(a, b):
    return jnp.dot(a, b, preferred_element_type=F32)


def dot_nt(a, b):
    return lax.dot_general(a, b, (((1,), (1,)), ((), ())), preferred_element_type=F32)


def dot_tn(a, b):
    return lax.dot_general(a, b, (((0,), (0,)), ((), ())), preferred_element_type=F32)


def tiny():
    return pl.CostEstimate(flops=1024, bytes_accessed=1024, transcendentals=0)


def whole():
    return pl.BlockSpec(memory_space=pltpu.VMEM)


def turned(v):
    low = lax.broadcasted_iota(jnp.int32, v.shape, 1) % HD < HD // 2
    return jnp.where(low, pltpu.roll(v, 128 - HD // 2, 1), pltpu.roll(v, HD // 2, 1))


def scalars():
    return pl.BlockSpec(memory_space=pltpu.SMEM)


def pick_qkv(w_query, w_key, w_value, gain, chips):
    rows, cols = w_query.shape
    qw, share = cols // chips, chips // KVH

    def body(g_ref, q_ref, k_ref, v_ref, out_ref):
        gain = g_ref[...]
        out_ref[0, :, :qw] = (q_ref[...].astype(F32) * gain).astype(BF16)
        for n in range(KVH):

            @pl.when(pl.program_id(0) // share == n)
            def _():
                at = slice(n * HD, (n + 1) * HD)
                kv = jnp.concatenate([k_ref[:, at], v_ref[:, at]], axis=1)
                out_ref[0, :, qw:] = (kv.astype(F32) * gain).astype(BF16)

    small = pl.BlockSpec((rows, KVH * HD), lambda k: (0, 0))
    return pl.pallas_call(
        body,
        grid=(chips,),
        in_specs=[
            pl.BlockSpec((rows, 1), lambda k: (0, 0)),
            pl.BlockSpec((rows, qw), lambda k: (0, k)),
            small,
            small,
        ],
        out_specs=pl.BlockSpec((1, rows, qw + 2 * HD), lambda k: (k, 0, 0)),
        out_shape=jax.ShapeDtypeStruct((chips, rows, qw + 2 * HD), BF16),
        cost_estimate=tiny(),
        name="pick_qkv",
    )(gain, w_query, w_key, w_value)


def pick_half(w_gate, w_up, gain, ids, count):
    rows, cols = w_gate.shape
    width, part = cols // count, rows // 2
    if width % 128:
        out = []
        for w in (w_gate, w_up):
            v = lax.dynamic_slice_in_dim((w.astype(F32) * gain).astype(BF16), ids[2] * part, part)
            out.append(v.reshape(part, count, width).transpose(1, 0, 2))
        return out

    def body(s_ref, n_ref, a_ref, b_ref, c_ref, d_ref):
        c_ref[0] = (a_ref[...].astype(F32) * n_ref[...]).astype(BF16)
        d_ref[0] = (b_ref[...].astype(F32) * n_ref[...]).astype(BF16)

    return pl.pallas_call(
        body,
        grid_spec=pltpu.PrefetchScalarGridSpec(
            num_scalar_prefetch=1,
            grid=(count,),
            in_specs=[pl.BlockSpec((part, 1), lambda k, s: (s[2], 0))]
            + [pl.BlockSpec((part, width), lambda k, s: (s[2], k))] * 2,
            out_specs=[pl.BlockSpec((1, part, width), lambda k, s: (k, 0, 0))] * 2,
        ),
        out_shape=[jax.ShapeDtypeStruct((count, part, width), BF16)] * 2,
        cost_estimate=tiny(),
        name="pick_half",
    )(ids, gain, w_gate, w_up)


def join_cores(ids, near, far):
    rows, cols = near.shape

    def body(s_ref, a_ref, b_ref, out_ref):
        @pl.when(pl.program_id(0) == 0)
        def _():
            out_ref[...] = a_ref[...]

        @pl.when(pl.program_id(0) == 1)
        def _():
            out_ref[...] = b_ref[...]

    return pl.pallas_call(
        body,
        grid_spec=pltpu.PrefetchScalarGridSpec(
            num_scalar_prefetch=1,
            grid=(2,),
            in_specs=[pl.BlockSpec((rows, cols), lambda f, s: (0, 0))] * 2,
            out_specs=pl.BlockSpec((rows, cols), lambda f, s: (s[1] ^ f, 0)),
        ),
        out_shape=jax.ShapeDtypeStruct((2 * rows, cols), near.dtype),
        cost_estimate=tiny(),
        name="join_cores",
    )(ids, near, far)


def qkv_kernel(ids, x_blocks, near, far, cos_table, sin_table):
    rows, model = x_blocks[0].shape
    chips = len(x_blocks)
    own = rows * chips
    wrows, width = near.shape[1:]
    qw = width - 2 * HD

    def body(c_ref, cos_ref, sin_ref, n_ref, f_ref, *refs):
        x_refs, (z_ref, q_ref, kv_ref, w_ref) = refs[:chips], refs[chips:]
        chip, core = c_ref[0], c_ref[1]
        for k in range(chips):
            at = pl.multiple_of((2 * k + core) * wrows, wrows)
            w_ref[pl.ds(at, wrows), :] = n_ref[k]
            at = pl.multiple_of((2 * k + 1 - core) * wrows, wrows)
            w_ref[pl.ds(at, wrows), :] = f_ref[k]
            x = x_refs[k][...].astype(F32)
            inv = lax.rsqrt(jnp.mean(x * x, axis=-1, keepdims=True) + NORM_EPS)
            at = pl.multiple_of((chip ^ k) * rows, rows)
            z_ref[pl.ds(at, rows), :] = (x * inv).astype(BF16)
        total = dot(z_ref[...], w_ref[...])
        cos, sin = cos_ref[...], sin_ref[...]
        for j in range(qw // 128):
            v = total[:, j * 128 : (j + 1) * 128]
            q_ref[:, j * 128 : (j + 1) * 128] = (v * cos + turned(v) * sin).astype(BF16)
        v = total[:, qw:]
        key = lax.broadcasted_iota(jnp.int32, v.shape, 1) < HD
        kv_ref[...] = jnp.where(key, v * cos + turned(v) * sin, v).astype(BF16)

    return pl.pallas_call(
        body,
        in_specs=[scalars()] + [whole()] * (4 + chips),
        out_specs=[whole()] * 4,
        out_shape=[
            jax.ShapeDtypeStruct((own, model), BF16),
            jax.ShapeDtypeStruct((own, qw), BF16),
            jax.ShapeDtypeStruct((own, 2 * HD), BF16),
            jax.ShapeDtypeStruct((2 * chips * wrows, width), BF16),
        ],
        cost_estimate=tiny(),
        name="qkv_forward",
    )(ids, cos_table, sin_table, near, far, *x_blocks)


def attention_mask(s_ref, l_ref, rows, block):
    core, rep, span = s_ref[1], s_ref[4], (block + 1) * rows

    def coded(pos):
        bound, code = 0, jnp.zeros(pos.shape, jnp.int32)
        for n in range(DOCS):
            bound = bound + l_ref[rep, n]
            code = code + jnp.where(pos >= bound, 1, 0)
        return jnp.where(code < DOCS - 1, code, 1000 + pos)

    q_pos = (2 * block + core) * rows + lax.broadcasted_iota(jnp.int32, (rows, 1), 0)
    index = lax.broadcasted_iota(jnp.int32, (1, 2 * span), 1)
    side = jnp.where(index < span, core, 1 - core)
    index = jnp.where(index < span, index, index - span)
    k_pos = (2 * (index // rows) + side) * rows + index % rows
    q_code = coded(q_pos)
    allowed = (coded(k_pos) == q_code) & (k_pos <= q_pos)
    return jnp.where(allowed, 0.0, MASK_FILL), jnp.where(q_code < DOCS, 1.0, 0.0)


def attention_forward(ids, lengths, q, kv_own, kv_other, rows, stack=4):
    own, qw = q.shape
    scale = 1.0 / math.sqrt(HD)
    heads = qw // HD
    stack = min(stack, heads)

    def body(s_ref, d_ref, q_ref, a_ref, b_ref, o_ref, l_ref):
        for block in range(own // rows):

            @pl.when(pl.program_id(0) == block)
            def _(block=block):
                span = (block + 1) * rows
                bias, valid = attention_mask(s_ref, d_ref, rows, block)
                lane = lax.broadcasted_iota(jnp.int32, (rows, 128), 1)
                sums = jnp.zeros((rows, 128), F32)
                keys = jnp.concatenate([a_ref[:span, :], b_ref[:span, :]], axis=0)
                k, v = keys[:, :HD], keys[:, HD:]
                for g in range(heads // stack):
                    qs = [q_ref[:, h * HD : (h + 1) * HD] for h in range(g * stack, (g + 1) * stack)]
                    qs = jnp.concatenate(qs, axis=0) * jnp.asarray(scale, BF16)
                    s = dot_nt(qs, k).reshape(stack, rows, 2 * span) + bias[None]
                    top = jnp.max(s, axis=-1, keepdims=True)
                    p = jnp.exp(s - top)
                    tot = jnp.sum(p, axis=-1, keepdims=True)
                    p = (p * (1.0 / tot)).astype(BF16).reshape(stack * rows, 2 * span)
                    o = dot(p, v).reshape(stack, rows, HD) * valid[None]
                    o = o.astype(BF16)
                    lse = top + jnp.log(tot)
                    for t in range(stack):
                        h = g * stack + t
                        sums = jnp.where(lane == h, lse[t], sums)
                        if t % 2:
                            pair = jnp.concatenate([o[t - 1], o[t]], axis=1)
                            o_ref[:, (h - 1) * HD : (h + 1) * HD] = pair
                l_ref[...] = sums

    blocked = lambda i: (i, 0)
    fixed = pl.BlockSpec((own, 2 * HD), lambda i: (0, 0))
    return pl.pallas_call(
        body,
        grid=(own // rows,),
        in_specs=[scalars(), scalars(), pl.BlockSpec((rows, qw), blocked), fixed, fixed],
        out_specs=[pl.BlockSpec((rows, qw), blocked), pl.BlockSpec((rows, 128), blocked)],
        out_shape=[
            jax.ShapeDtypeStruct((own, qw), BF16),
            jax.ShapeDtypeStruct((own, 128), F32),
        ],
        cost_estimate=tiny(),
        name="attention_forward",
    )(ids, lengths, q, kv_own, kv_other)


def attention_backward(
    ids, lengths, q, kv_own, kv_other, sums, d_out, cos_table, sin_table, rows, stack=2
):
    own, qw = q.shape
    scale = 1.0 / math.sqrt(HD)
    heads = qw // HD
    stack = min(stack, heads)
    blocks = own // rows

    def body(
        s_ref, n_ref, q_ref, a_ref, b_ref, l_ref, d_ref, cos_ref, sin_ref, dq_ref, dkv_ref,
    ):
        @pl.when(pl.program_id(0) == 0)
        def _():
            dkv_ref[...] = jnp.zeros_like(dkv_ref)

        for block in range(blocks):

            @pl.when(pl.program_id(0) == block)
            def _(block=block):
                span = (block + 1) * rows
                bias, valid = attention_mask(s_ref, n_ref, rows, block)
                valid = valid.astype(BF16)
                cos, sin = cos_ref[...], sin_ref[...]
                keys = jnp.concatenate([a_ref[:span, :], b_ref[:span, :]], axis=0)
                k, v = keys[:, :HD], keys[:, HD:]
                dk, dv = 0.0, 0.0
                for g in range(heads // stack):
                    part = range(g * stack, (g + 1) * stack)
                    qs = [q_ref[:, h * HD : (h + 1) * HD] for h in part]
                    qs = jnp.concatenate(qs, axis=0) * jnp.asarray(scale, BF16)
                    ds = [d_ref[:, h * HD : (h + 1) * HD] * valid for h in part]
                    ds = jnp.concatenate(ds, axis=0)
                    lse = jnp.stack([l_ref[:, h : h + 1] for h in part])
                    s = dot_nt(qs, k).reshape(stack, rows, 2 * span) + bias[None]
                    p = jnp.exp(s - lse)
                    dp = dot_nt(ds, v).reshape(stack, rows, 2 * span)
                    inner = jnp.sum(p * dp, axis=-1, keepdims=True)
                    grad = (p * (dp - inner)).astype(BF16).reshape(stack * rows, 2 * span)
                    p = p.astype(BF16).reshape(stack * rows, 2 * span)
                    dq = (dot(grad, k) * scale).reshape(stack, rows, HD)
                    dk = dk + dot_tn(grad, qs)
                    dv = dv + dot_tn(p, ds)
                    for t in range(1, stack, 2):
                        h = g * stack + t
                        w = jnp.concatenate([dq[t - 1], dq[t]], axis=1)
                        w = w * cos - turned(w) * sin
                        dq_ref[:, (h - 1) * HD : (h + 1) * HD] = w.astype(BF16)
                both = jnp.concatenate([dk, dv], axis=1)
                dkv_ref[:span, :] += both[:span]
                dkv_ref[own : own + span, :] += both[span:]

    blocked = lambda i: (i, 0)
    fixed = pl.BlockSpec((own, 2 * HD), lambda i: (0, 0))
    table = pl.BlockSpec((rows, 128), blocked)
    wide = pl.BlockSpec((rows, qw), blocked)
    return pl.pallas_call(
        body,
        grid=(blocks,),
        in_specs=[scalars(), scalars(), wide, fixed, fixed, table, wide, table, table],
        out_specs=[wide, pl.BlockSpec((2 * own, 2 * HD), lambda i: (0, 0))],
        out_shape=[
            jax.ShapeDtypeStruct((own, qw), BF16),
            jax.ShapeDtypeStruct((2 * own, 2 * HD), F32),
        ],
        cost_estimate=tiny(),
        name="attention_backward",
    )(ids, lengths, q, kv_own, kv_other, sums, d_out, cos_table, sin_table)


def feed_forward(ids, z_blocks, cot, weights, w_down):
    rows, model = z_blocks[0].shape
    chips = len(z_blocks)
    part, width = weights[0][0].shape[1:]
    own, tile = rows * chips, min(TILE, width)
    turns = pl.cdiv(width, tile)

    def body(s_ref, *refs):
        z_refs, c_ref, w_refs = refs[:chips], refs[chips], refs[chips + 1 : chips + 9]
        d_ref, m_ref, dg_ref, du_ref, z_ref, b_ref, w_ref, acc_ref = refs[chips + 9 :]
        chip, core, half = s_ref[0], s_ref[1], s_ref[2]
        turn = pl.program_id(0)

        @pl.when(turn == 0)
        def _():
            for k in range(chips):
                at = pl.multiple_of((chip ^ k) * rows, rows)
                z_ref[pl.ds(at, rows), :] = z_refs[k][...]

        def work(cols, first, last):
            for m in range(2):
                for i in range(4):
                    side = core if i < 2 else 1 - core
                    piece = half if i % 2 == 0 else 1 - half
                    for j in range(chips):
                        at = pl.multiple_of((2 * (2 * j + side) + piece) * part, part)
                        w_ref[m, pl.ds(at, part), :cols] = w_refs[4 * m + i][j, :, :cols]
            gate = dot(z_ref[...], w_ref[0, :, :cols])
            up = dot(z_ref[...], w_ref[1, :, :cols])
            dm = dot_nt(c_ref[...], d_ref[:cols, :])
            sig = 1.0 / (1.0 + jnp.exp(-gate))
            silu = gate * sig
            m_ref[:, :cols] = (silu * up).astype(BF16)
            dg = (dm * up * sig * (1.0 + gate * (1.0 - sig))).astype(BF16)
            du = (dm * silu).astype(BF16)
            dg_ref[:, :cols] = dg
            du_ref[:, :cols] = du
            back = dot_nt(dg, w_ref[0, :, :cols]) + dot_nt(du, w_ref[1, :, :cols])
            if not first:
                back = back + acc_ref[...]
            if last:
                b_ref[...] = back.astype(BF16)
            else:
                acc_ref[...] = back

        for n in range(turns):

            @pl.when(turn == n)
            def _(n=n):
                work(min(tile, width - n * tile), n == 0, n == turns - 1)

    joined = pl.BlockSpec((own, model), lambda n, s: (0, 0))
    out_tile = pl.BlockSpec((own, tile), lambda n, s: (0, n))
    return pl.pallas_call(
        body,
        grid_spec=pltpu.PrefetchScalarGridSpec(
            num_scalar_prefetch=1,
            grid=(turns,),
            in_specs=[pl.BlockSpec((rows, model), lambda n, s: (0, 0))] * chips
            + [joined]
            + [pl.BlockSpec((chips, part, tile), lambda n, s: (0, 0, n))] * 8
            + [pl.BlockSpec((tile, model), lambda n, s: (n, 0))],
            out_specs=[out_tile] * 3 + [joined] * 2,
            scratch_shapes=[
                pltpu.VMEM((2, model, tile), BF16),
                pltpu.VMEM((own, model), F32),
            ],
        ),
        out_shape=[jax.ShapeDtypeStruct((own, width), BF16)] * 3
        + [jax.ShapeDtypeStruct((own, model), BF16)] * 2,
        cost_estimate=tiny(),
        name="feed_forward",
    )(ids, *z_blocks, cot, *weights[0], *weights[1], w_down)


def out_proj(ids, attn, near, far, chips):
    own, depth = attn.shape
    wrows, model = near.shape
    rows = own // chips

    def body(c_ref, a_ref, n_ref, f_ref, *outs):
        chip, core, w_ref = c_ref[0], c_ref[1], outs[-1]
        w_ref[pl.ds(pl.multiple_of(core * wrows, wrows), wrows), :] = n_ref[...]
        w_ref[pl.ds(pl.multiple_of((1 - core) * wrows, wrows), wrows), :] = f_ref[...]
        for k in range(chips):
            at = pl.multiple_of((chip ^ k) * rows, rows)
            outs[k][...] = dot(a_ref[pl.ds(at, rows), :], w_ref[...]).astype(BF16)

    return pl.pallas_call(
        body,
        in_specs=[scalars()] + [whole()] * 3,
        out_specs=[whole()] * (chips + 1),
        out_shape=[jax.ShapeDtypeStruct((rows, model), BF16)] * chips
        + [jax.ShapeDtypeStruct((depth, model), BF16)],
        cost_estimate=tiny(),
        name="out_proj",
    )(ids, attn, near, far)


def residual_norm(tokens, parts):
    rows, model = tokens.shape

    def body(x_ref, *refs):
        y_ref, z_ref = refs[-2:]
        y = x_ref[...].astype(F32)
        for p in refs[:-2]:
            y = y + p[...].astype(F32)
        y_ref[...] = y
        inv = lax.rsqrt(jnp.mean(y * y, axis=-1, keepdims=True) + NORM_EPS)
        z_ref[...] = (y * inv).astype(BF16)

    return pl.pallas_call(
        body,
        in_specs=[whole()] * (1 + len(parts)),
        out_specs=[whole()] * 2,
        out_shape=[
            jax.ShapeDtypeStruct((rows, model), F32),
            jax.ShapeDtypeStruct((rows, model), BF16),
        ],
        cost_estimate=tiny(),
        name="residual_norm",
    )(tokens, *parts)


def residual_norm_back(base, parts, y, copies):
    rows, model = y.shape
    count = parts.shape[0] // rows

    def body(b_ref, y_ref, p_ref, f_ref, l_ref, n_ref):
        e = p_ref[:rows, :].astype(F32)
        for i in range(1, count):
            e = e + p_ref[i * rows : (i + 1) * rows, :].astype(F32)
        v = y_ref[...].astype(F32)
        inv = lax.rsqrt(jnp.mean(v * v, axis=-1, keepdims=True) + NORM_EPS)
        z = v * inv
        ez = e * z
        n_ref[...] = jnp.sum(ez, axis=0, keepdims=True)
        out = b_ref[...].astype(F32) + inv * (e - z * jnp.mean(ez, axis=-1, keepdims=True))
        f_ref[...] = out
        for i in range(copies):
            l_ref[i * rows : (i + 1) * rows, :] = out.astype(BF16)

    return pl.pallas_call(
        body,
        in_specs=[whole()] * 3,
        out_specs=[whole()] * 3,
        out_shape=[
            jax.ShapeDtypeStruct((rows, model), F32),
            jax.ShapeDtypeStruct((copies * rows, model), BF16),
            jax.ShapeDtypeStruct((1, model), F32),
        ],
        cost_estimate=tiny(),
        name="residual_norm_back",
    )(base, y, parts)


def strips(value, ref, lead=()):
    rows, width = value.shape
    for t in range(pl.cdiv(width, 128)):
        v = value[:, t * 128 : (t + 1) * 128]
        if v.shape[1] < 128:
            v = jnp.concatenate([v, jnp.zeros((rows, 128 - v.shape[1]), v.dtype)], axis=1)
        ref[(*lead, slice(t * rows, (t + 1) * rows), slice(None))] = v


def weight_grad(ids, left, right, chips):
    own, model = left.shape
    width = right.shape[1]
    rows = model // (2 * chips)
    long = pl.cdiv(width, 128) * rows
    group = min(4, chips)
    turns = chips // group

    def body(c_ref, l_ref, r_ref, near_ref, far_ref):
        step = pl.program_id(0)
        near = step >= turns
        side = jnp.where(near, c_ref[1], 1 - c_ref[1])
        first = jnp.where(near, step - turns, step) * group
        blocks = []
        for j in range(group):
            at = pl.multiple_of((2 * (first + j) + side) * rows, rows)
            blocks.append(l_ref[:, pl.ds(at, rows)])
        out = dot_tn(jnp.concatenate(blocks, axis=1), r_ref[...]).astype(BF16)

        @pl.when(near)
        def _():
            for j in range(group):
                strips(out[j * rows : (j + 1) * rows], near_ref, (j,))

        @pl.when(step < turns)
        def _():
            for j in range(group):
                strips(out[j * rows : (j + 1) * rows], far_ref, (j,))

    return pl.pallas_call(
        body,
        grid_spec=pltpu.PrefetchScalarGridSpec(
            num_scalar_prefetch=1,
            grid=(2 * turns,),
            in_specs=[
                pl.BlockSpec((own, model), lambda t, c: (0, 0)),
                pl.BlockSpec((own, width), lambda t, c: (0, 0)),
            ],
            out_specs=[
                pl.BlockSpec((group, long, 128), lambda t, c: (jnp.maximum(t - turns, 0), 0, 0)),
                pl.BlockSpec((group, long, 128), lambda t, c: (jnp.minimum(t, turns - 1), 0, 0)),
            ],
        ),
        out_shape=[jax.ShapeDtypeStruct((chips, long, 128), BF16)] * 2,
        cost_estimate=tiny(),
        name="weight_grad",
    )(ids, left, right)


def row_grad(ids, left, right, cuts):
    own, depth = left.shape
    model = right.shape[1]
    rows, width = depth // 2, model // cuts
    long = width // 128 * rows

    def body(c_ref, l_ref, r_ref, near_ref, far_ref, full_ref):
        core = c_ref[1]
        full_ref[...] = dot_tn(l_ref[...], r_ref[...])
        near = full_ref[pl.ds(pl.multiple_of(core * rows, 8), rows), :]
        far = full_ref[pl.ds(pl.multiple_of((1 - core) * rows, 8), rows), :]
        strips(near.astype(BF16), near_ref, (0,))
        strips(far.astype(BF16), far_ref, (0,))

    out = pl.BlockSpec((1, long, 128), lambda n, c: (n, 0, 0))
    return pl.pallas_call(
        body,
        grid_spec=pltpu.PrefetchScalarGridSpec(
            num_scalar_prefetch=1,
            grid=(cuts,),
            in_specs=[
                pl.BlockSpec((own, depth), lambda n, c: (0, 0)),
                pl.BlockSpec((own, width), lambda n, c: (0, n)),
            ],
            out_specs=[out] * 2,
            scratch_shapes=[pltpu.VMEM((depth, width), F32)],
        ),
        out_shape=[jax.ShapeDtypeStruct((cuts, long, 128), BF16)] * 2,
        cost_estimate=tiny(),
        name="row_grad",
    )(ids, left, right)


def chain_step(ids, own, outer, sent, inner, coming):
    def size(v):
        return 0 if v is None else v[0].shape[1] if isinstance(v, tuple) else v.shape[0]

    ins = [own, outer if own is not None else None, sent, inner, coming]
    have = [v is not None for v in ins]
    sizes = [size(own), max(size(sent), size(coming))]

    def body(s_ref, *refs):
        refs = list(refs)
        o_ref, x_ref, i_ref, y_ref, c_ref = [refs.pop(0) if h else None for h in have]
        s_out, a_out = [refs.pop(0) if n else None for n in sizes]
        ends = s_ref[3] == 1

        def each(count, work):
            step = math.gcd(512, count)

            def turn(n, carry):
                work(pl.ds(pl.multiple_of(n * step, step), step))
                return carry

            lax.fori_loop(0, count // step, turn, 0)

        if s_out is not None:

            def add_own(at):
                s_out[at, :] = o_ref[at, :] + x_ref[at, :]

            each(size(own), add_own)
        if c_ref is not None:

            @pl.when(ends)
            def _():
                def copy(at):
                    a_out[at, :] = c_ref[at, :]

                each(size(coming), copy)

        if i_ref is not None:

            @pl.when(jnp.logical_not(ends))
            def _():
                def add_sent(at):
                    a_out[at, :] = i_ref[at, :] + y_ref[at, :]

                each(size(sent), add_sent)

    def spec(v):
        if not isinstance(v, tuple):
            return pl.BlockSpec(v.shape, lambda i: (0, 0))
        block = v[1]
        return pl.BlockSpec((pl.Squeezed(), *v[0].shape[1:]), lambda i: (block, 0, 0))

    outs = pl.pallas_call(
        body,
        grid=(1,),
        in_specs=[scalars()] + [spec(v) for v in ins if v is not None],
        out_specs=[pl.BlockSpec((n, 128), lambda i: (0, 0)) for n in sizes if n],
        out_shape=[jax.ShapeDtypeStruct((n, 128), BF16) for n in sizes if n],
        cost_estimate=tiny(),
        name="chain_step",
    )(ids, *[v[0] if isinstance(v, tuple) else v for v in ins if v is not None])
    outs = list(outs)
    return [outs.pop(0) if n else None for n in sizes]


def beside(ids, blocks, rows, width, scale=None):
    count = len(blocks)
    tiles = pl.cdiv(width, 128)
    long = tiles * rows
    if scale is None:
        scale = jnp.ones((rows, 1), F32)
    if width % 128:
        full = [
            a[:long].reshape(tiles, rows, 128).transpose(1, 0, 2).reshape(rows, -1)
            for a, b in blocks
        ]
        return jnp.concatenate([f[:, :width] for f in full], axis=1).astype(F32) * scale

    def body(c_ref, s_ref, *refs):
        scale, out_ref = s_ref[...], refs[-1]
        for k in range(count):
            for end in (0, 1):

                @pl.when((pl.program_id(0) == k) & (c_ref[3] == end))
                def _(ref=refs[2 * k + end]):
                    for t in range(tiles):
                        v = ref[t * rows : (t + 1) * rows, :].astype(F32)
                        out_ref[:, t * 128 : (t + 1) * 128] = v * scale

    return pl.pallas_call(
        body,
        grid_spec=pltpu.PrefetchScalarGridSpec(
            num_scalar_prefetch=1,
            grid=(count,),
            in_specs=[pl.BlockSpec((rows, 1), lambda k, c: (0, 0))]
            + [pl.BlockSpec((long, 128), lambda k, c: (0, 0))] * (2 * count),
            out_specs=pl.BlockSpec((rows, width), lambda k, c: (0, k)),
        ),
        out_shape=jax.ShapeDtypeStruct((rows, count * width), F32),
        cost_estimate=tiny(),
        name="beside",
    )(ids, scale, *[v for pair in blocks for v in pair])


def pair_sum(near, far):
    count, rows, lanes = near.shape

    def body(a_ref, b_ref, out_ref):
        out_ref[...] = a_ref[...] + b_ref[...]

    spec = pl.BlockSpec((1, rows, lanes), lambda k: (k, 0, 0))
    return pl.pallas_call(
        body,
        grid=(count,),
        in_specs=[spec] * 2,
        out_specs=spec,
        out_shape=jax.ShapeDtypeStruct(near.shape, BF16),
        cost_estimate=tiny(),
        name="pair_sum",
    )(near, far)


def local(
    tokens,
    cotangent,
    doc_lengths,
    norm1_gain,
    w_query,
    w_key,
    w_value,
    w_out,
    norm2_gain,
    w_gate,
    w_up,
    w_down,
):
    rows, model = tokens.shape
    group = lax.axis_size("fsdp")
    reps = lax.axis_size("rep")
    chips = group // 2
    dev = lax.axis_index("fsdp").astype(jnp.int32)
    rep = lax.axis_index("rep").astype(jnp.int32)
    chip, core, half = dev >> 1, dev & 1, rep & 1
    ends = jnp.where((rep == 0) | (rep == reps - 1), 1, 0).astype(jnp.int32)
    ids = jnp.stack([chip, core, half, ends, rep])
    seq_len = rows * group
    own = rows * chips
    wrows = w_query.shape[0]
    width = w_gate.shape[1] // chips
    kv_share = chips // KVH
    qw = H // chips * HD
    tie = lax.optimization_barrier
    sides = [[2 * k + c for k in range(chips)] for c in range(2)]

    def exchange(v):
        return lax.all_to_all(v, "fsdp", 0, 0, axis_index_groups=sides, tiled=True)

    def hop(v, k):
        return lax.ppermute(v, "fsdp", [(i, i ^ (2 * k)) for i in range(group)])

    def hops(blocks):
        return [blocks[0]] + [hop(blocks[k], k) for k in range(1, chips)]

    def swap(v):
        return lax.ppermute(v, "fsdp", [(i, i ^ 1) for i in range(group)])

    def trade(v):
        return lax.ppermute(v, "rep", [(i, i ^ 1) for i in range(reps)])

    def copies(v):
        return jnp.broadcast_to(v[None], (chips,) + v.shape).reshape(chips * v.shape[0], -1)

    sums_of = {}
    outer_pairs = [(0, 1), (1, 0), (2, 3), (3, 2)]

    class Line:
        def __init__(self):
            self.own = self.sent = self.total = self.outer = self.inner = None

        def busy(self):
            return any(v is not None for v in (self.own, self.sent, self.total))

    lines = [Line(), Line()]
    turn = [0]

    def visit(*carry, new=None):
        if reps != 4:
            if new is not None:
                value = lax.psum(new[1][new[2]], "rep")
                sums_of[f"{new[0]}{new[2]}"] = (value, value)
            return carry if len(carry) != 1 else carry[0]
        line = lines[turn[0] % 2]
        turn[0] += 1
        extra = [line.outer, line.inner, None if new is None else new[1]]
        tied = tie(tuple(carry) + tuple(v for v in extra if v is not None))
        carry, tied = tied[: len(carry)], list(tied[len(carry) :])
        outer, inner, coming = [None if v is None else tied.pop(0) for v in extra]
        coming = None if new is None else (coming, new[2])
        value = lambda pair: None if pair is None else pair[1]
        if line.total is not None:
            sums_of[line.total[0]] = (line.total[1], outer)
        own_sum = ahead = None
        if outer is None:
            ahead = None if coming is None else coming[0][coming[1]]
        elif line.own is not None or line.sent is not None or coming is not None:
            own_sum, ahead = chain_step(
                ids, value(line.own), outer, value(line.sent), inner, coming
            )
        line.total = None if line.sent is None else (line.sent[0], ahead)
        line.sent = None if line.own is None else (line.own[0], own_sum)
        line.own = None if coming is None else (f"{new[0]}{new[2]}", coming)
        line.outer = None if ahead is None else lax.ppermute(ahead, "rep", outer_pairs)
        line.inner = (
            None if line.sent is None else lax.ppermute(line.sent[1], "rep", [(1, 2), (2, 1)])
        )
        return carry if len(carry) != 1 else carry[0]

    starts = 2 * rows * jnp.arange(chips, dtype=jnp.int32) + core * rows
    own_pos = (starts[:, None] + jnp.arange(rows, dtype=jnp.int32)[None, :]).reshape(own)
    lane = jnp.arange(128)
    inverse = jnp.exp(-math.log(ROPE_BASE) / (HD // 2) * (lane % (HD // 2)).astype(F32))
    angles = own_pos.astype(F32)[:, None] * inverse[None, :]
    cos_table = jnp.cos(angles)
    sin_table = jnp.sin(angles) * jnp.where(lane % HD < HD // 2, -1.0, 1.0)[None, :]

    gain_one = norm1_gain.astype(F32)[:, None]
    gain_two = norm2_gain.astype(F32)[:, None]
    x_blocks = hops([tokens] * chips)
    qkv_near = exchange(pick_qkv(w_query, w_key, w_value, gain_one, chips))
    gate_part, up_part = pick_half(w_gate, w_up, gain_two, ids, chips)
    w_out_far = swap(w_out)
    w_down_c = join_cores(ids, w_down, swap(w_down))
    *x_blocks, cos_table, sin_table, gate_part, up_part, w_out_far, w_down_c = tie(
        (*x_blocks, cos_table, sin_table, gate_part, up_part, w_out_far, w_down_c)
    )
    gate_near = exchange(gate_part)
    normed_one, queries, kv_near, w_qkv = qkv_kernel(
        ids, x_blocks, qkv_near, swap(qkv_near), cos_table, sin_table
    )
    queries, gate_near, up_part, cot = tie((queries, gate_near, up_part, cotangent))
    up_near = exchange(up_part)
    gate_traded = trade(gate_near)
    kv_far = swap(kv_near)
    attn, sums = attention_forward(ids, doc_lengths, queries, kv_near, kv_far, rows)
    attn, up_near = tie((attn, up_near))
    up_traded = trade(up_near)
    *mixed, w_out_c = out_proj(ids, attn, w_out, w_out_far, chips)
    *mixed, cot = tie((*mixed, cot))
    parts = hops(mixed)
    cot_rows = exchange(copies(cot))
    *parts, gate_traded = tie((*parts, gate_traded))
    resid, normed = residual_norm(tokens, parts)
    z_blocks = hops([normed] * chips)
    weights = [
        [near, far, swap(near), swap(far)]
        for near, far in ((gate_near, gate_traded), (up_near, up_traded))
    ]
    inner, grad_gate, grad_up, normed_two, back = feed_forward(
        ids, z_blocks, cot_rows, weights, w_down_c
    )

    parts = exchange(back)
    down_near, down_far = row_grad(ids, inner, cot_rows, 4)
    down_far = swap(down_far)
    grad_gate, down_near = tie((grad_gate, down_near))
    gate_near, gate_far = weight_grad(ids, normed_two, grad_gate, chips)
    gate_near, gate_far, down_far, grad_up = tie((gate_near, gate_far, down_far, grad_up))
    gate_far = swap(gate_far)
    down = pair_sum(down_near, down_far)
    grad_up = visit(grad_up, new=("down", down, 0))
    up_near, up_far = weight_grad(ids, normed_two, grad_up, chips)
    up_near, up_far, parts = visit(up_near, up_far, parts, new=("down", down, 1))
    gate_part = exchange(pair_sum(gate_near, gate_far))
    up_far = swap(up_far)
    grad_resid, da, gain_two_local = residual_norm_back(cotangent, parts, resid, chips)
    da, inner = visit(da, inner, new=("down", down, 2))
    out = dot(inner, w_down_c).astype(BF16)
    up_part = pair_sum(up_near, up_far)
    out, up_part, gate_part = visit(out, up_part, gate_part, new=("down", down, 3))
    da = exchange(da)
    da, up_part = visit(da, up_part, new=("gate", gate_part, 0))
    up_part = exchange(up_part)
    dob = dot_nt(da, w_out_c).astype(BF16)
    out_near, out_far = row_grad(ids, attn, da, 2)
    dob, out_near, out_far = visit(dob, out_near, out_far, new=("gate", gate_part, 1))
    out_far = swap(out_far)
    dq, dkv = attention_backward(
        ids, doc_lengths, queries, kv_near, kv_far, sums, dob, cos_table, sin_table, rows
    )
    dq, dkv = visit(dq, dkv, new=("gate", gate_part, 2))
    dkv = dkv[:own] + swap(dkv[own:].astype(BF16)).astype(F32)
    half_turn = jnp.concatenate([dkv[:, HD // 2 : HD], dkv[:, : HD // 2]], axis=1)
    dk = dkv[:, :HD] * cos_table[:, :HD] - half_turn * sin_table[:, :HD]
    dqkv = jnp.concatenate([dq, dk.astype(BF16), dkv[:, HD:].astype(BF16)], axis=1)
    back = dot_nt(dqkv, w_qkv).astype(BF16)
    dqkv, back, up_part = visit(dqkv, back, up_part, new=("gate", gate_part, 3))
    parts = exchange(back)
    qkv_near, qkv_far = weight_grad(ids, normed_one, dqkv, chips)
    qkv_near, qkv_far = visit(qkv_near, qkv_far, new=("up", up_part, 0))
    qkv_part = pair_sum(qkv_near, swap(qkv_far))
    qkv_part, parts = visit(qkv_part, parts, new=("up", up_part, 1))
    qkv_part = exchange(qkv_part)
    _, grad_inputs, gain_one_local = residual_norm_back(grad_resid, parts, tokens, 1)
    gain_one_local = visit(gain_one_local, new=("up", up_part, 2))
    norms = jnp.concatenate([gain_one_local, gain_two_local], axis=0)
    norms = norms.reshape(2, chips, 2, wrows).transpose(2, 1, 0, 3)
    mine = lax.dynamic_index_in_dim(norms, core, 0, keepdims=False)
    other = lax.dynamic_index_in_dim(norms, 1 - core, 0, keepdims=False)
    norms = mine + swap(other)
    out_part = pair_sum(out_near, out_far)
    norms, qkv_part, out_part = visit(norms, qkv_part, out_part, new=("up", up_part, 3))
    parts = exchange(out).reshape(chips, rows, model)
    visit(new=("out", out_part, 0))
    parts = visit(parts, new=("out", out_part, 1))
    norms = jnp.sum(exchange(norms), axis=0)
    result = (resid + jnp.sum(parts.astype(F32), axis=0)).astype(BF16)
    visit(new=("qkv", qkv_part, 0))
    norms = visit(norms, new=("qkv", qkv_part, 1))
    for k in range(2, chips):
        visit(new=("qkv", qkv_part, k))
    if reps != 4:
        for k in range(4, chips):
            visit(new=("gate", gate_part, k))
            visit(new=("up", up_part, k))
    if reps == 4:
        norms = norms + lax.ppermute(norms, "rep", [(0, 1), (3, 2)])
        norms = norms + lax.ppermute(norms, "rep", [(1, 2), (2, 1)])
        norms = jnp.where(ends == 1, lax.ppermute(norms, "rep", [(1, 0), (2, 3)]), norms)
    else:
        norms = lax.psum(norms, "rep")
    while any(line.busy() for line in lines):
        visit()

    def summed(name, count):
        return [sums_of[f"{name}{k}"] for k in range(count)]

    qkv = summed("qkv", chips)
    grad_query = beside(ids, qkv, wrows, qw, gain_one)
    at = qw // 128 * wrows
    kv = [jnp.where(ends == 1, b[at : at + wrows], a[at : at + wrows]) for a, b in qkv]
    kv = jnp.stack(kv).astype(F32).reshape(KVH, kv_share, wrows, 2, HD).sum(axis=1)
    kv = kv * gain_one[None, :, :, None]
    grad_key = kv[:, :, 0].transpose(1, 0, 2).reshape(wrows, KVH * HD)
    grad_value = kv[:, :, 1].transpose(1, 0, 2).reshape(wrows, KVH * HD)
    return (
        result,
        grad_inputs,
        norms[0] / gain_one[:, 0],
        grad_query,
        grad_key,
        grad_value,
        beside(ids, summed("out", 2), wrows, model // 2),
        norms[1] / gain_two[:, 0],
        beside(ids, summed("gate", chips), wrows, width, gain_two),
        beside(ids, summed("up", chips), wrows, width, gain_two),
        beside(ids, summed("down", 4), w_down.shape[0], model // 4),
    )


def solution(mesh):
    placed = (
        P(("rep", "fsdp"), None),
        P(("rep", "fsdp"), None),
        P(),
        P("fsdp"),
        P("fsdp", None),
        P("fsdp", None),
        P("fsdp", None),
        P("fsdp", None),
        P("fsdp"),
        P("fsdp", None),
        P("fsdp", None),
        P("fsdp", None),
    )
    return jax.shard_map(
        local,
        mesh=mesh,
        in_specs=placed,
        out_specs=(
            P(("rep", "fsdp"), None),
            P(("rep", "fsdp"), None),
            P("fsdp"),
            P("fsdp", None),
            P("fsdp", None),
            P("fsdp", None),
            P("fsdp", None),
            P("fsdp"),
            P("fsdp", None),
            P("fsdp", None),
            P("fsdp", None),
        ),
        check_vma=False,
    )
```

```python
import math

import jax
import jax.numpy as jnp
from jax import lax
from jax.experimental import pallas as pl
from jax.experimental.pallas import tpu as pltpu
from jax.sharding import PartitionSpec as P

H = 32
KVH = 4
HD = 64
DOCS = 8

NORM_EPS = 1e-05
ROPE_BASE = 10000.0
MASK_FILL = -1e30
TILE = 512
F32 = jnp.float32
BF16 = jnp.bfloat16


def dot(a, b):
    return jnp.dot(a, b, preferred_element_type=F32)


def dot_nt(a, b):
    return lax.dot_general(a, b, (((1,), (1,)), ((), ())), preferred_element_type=F32)


def dot_tn(a, b):
    return lax.dot_general(a, b, (((0,), (0,)), ((), ())), preferred_element_type=F32)


def tiny():
    return pl.CostEstimate(flops=1024, bytes_accessed=1024, transcendentals=0)


def whole():
    return pl.BlockSpec(memory_space=pltpu.VMEM)


def turned(v):
    low = lax.broadcasted_iota(jnp.int32, v.shape, 1) % HD < HD // 2
    return jnp.where(low, pltpu.roll(v, 128 - HD // 2, 1), pltpu.roll(v, HD // 2, 1))


def scalars():
    return pl.BlockSpec(memory_space=pltpu.SMEM)


def pick_qkv(w_query, w_key, w_value, gain, chips):
    rows, cols = w_query.shape
    qw, share = cols // chips, chips // KVH

    def body(g_ref, q_ref, k_ref, v_ref, out_ref):
        gain = g_ref[...]
        out_ref[0, :, :qw] = (q_ref[...].astype(F32) * gain).astype(BF16)
        for n in range(KVH):

            @pl.when(pl.program_id(0) // share == n)
            def _():
                at = slice(n * HD, (n + 1) * HD)
                kv = jnp.concatenate([k_ref[:, at], v_ref[:, at]], axis=1)
                out_ref[0, :, qw:] = (kv.astype(F32) * gain).astype(BF16)

    small = pl.BlockSpec((rows, KVH * HD), lambda k: (0, 0))
    return pl.pallas_call(
        body,
        grid=(chips,),
        in_specs=[
            pl.BlockSpec((rows, 1), lambda k: (0, 0)),
            pl.BlockSpec((rows, qw), lambda k: (0, k)),
            small,
            small,
        ],
        out_specs=pl.BlockSpec((1, rows, qw + 2 * HD), lambda k: (k, 0, 0)),
        out_shape=jax.ShapeDtypeStruct((chips, rows, qw + 2 * HD), BF16),
        cost_estimate=tiny(),
        name="pick_qkv",
    )(gain, w_query, w_key, w_value)


def pick_half(w_gate, w_up, gain, ids, count):
    rows, cols = w_gate.shape
    width, part = cols // count, rows // 2
    if width % 128:
        out = []
        for w in (w_gate, w_up):
            v = lax.dynamic_slice_in_dim((w.astype(F32) * gain).astype(BF16), ids[2] * part, part)
            out.append(v.reshape(part, count, width).transpose(1, 0, 2))
        return out

    def body(s_ref, n_ref, a_ref, b_ref, c_ref, d_ref):
        c_ref[0] = (a_ref[...].astype(F32) * n_ref[...]).astype(BF16)
        d_ref[0] = (b_ref[...].astype(F32) * n_ref[...]).astype(BF16)

    return pl.pallas_call(
        body,
        grid_spec=pltpu.PrefetchScalarGridSpec(
            num_scalar_prefetch=1,
            grid=(count,),
            in_specs=[pl.BlockSpec((part, 1), lambda k, s: (s[2], 0))]
            + [pl.BlockSpec((part, width), lambda k, s: (s[2], k))] * 2,
            out_specs=[pl.BlockSpec((1, part, width), lambda k, s: (k, 0, 0))] * 2,
        ),
        out_shape=[jax.ShapeDtypeStruct((count, part, width), BF16)] * 2,
        cost_estimate=tiny(),
        name="pick_half",
    )(ids, gain, w_gate, w_up)


def join_cores(ids, near, far):
    rows, cols = near.shape

    def body(s_ref, a_ref, b_ref, out_ref):
        @pl.when(pl.program_id(0) == 0)
        def _():
            out_ref[...] = a_ref[...]

        @pl.when(pl.program_id(0) == 1)
        def _():
            out_ref[...] = b_ref[...]

    return pl.pallas_call(
        body,
        grid_spec=pltpu.PrefetchScalarGridSpec(
            num_scalar_prefetch=1,
            grid=(2,),
            in_specs=[pl.BlockSpec((rows, cols), lambda f, s: (0, 0))] * 2,
            out_specs=pl.BlockSpec((rows, cols), lambda f, s: (s[1] ^ f, 0)),
        ),
        out_shape=jax.ShapeDtypeStruct((2 * rows, cols), near.dtype),
        cost_estimate=tiny(),
        name="join_cores",
    )(ids, near, far)


def qkv_kernel(ids, x_blocks, near, far, cos_table, sin_table):
    rows, model = x_blocks[0].shape
    chips = len(x_blocks)
    own = rows * chips
    wrows, width = near.shape[1:]
    qw = width - 2 * HD

    def body(c_ref, cos_ref, sin_ref, n_ref, f_ref, *refs):
        x_refs, (z_ref, q_ref, kv_ref, w_ref) = refs[:chips], refs[chips:]
        chip, core = c_ref[0], c_ref[1]
        for k in range(chips):
            at = pl.multiple_of((2 * k + core) * wrows, wrows)
            w_ref[pl.ds(at, wrows), :] = n_ref[k]
            at = pl.multiple_of((2 * k + 1 - core) * wrows, wrows)
            w_ref[pl.ds(at, wrows), :] = f_ref[k]
            x = x_refs[k][...].astype(F32)
            inv = lax.rsqrt(jnp.mean(x * x, axis=-1, keepdims=True) + NORM_EPS)
            at = pl.multiple_of((chip ^ k) * rows, rows)
            z_ref[pl.ds(at, rows), :] = (x * inv).astype(BF16)
        total = dot(z_ref[...], w_ref[...])
        cos, sin = cos_ref[...], sin_ref[...]
        for j in range(qw // 128):
            v = total[:, j * 128 : (j + 1) * 128]
            q_ref[:, j * 128 : (j + 1) * 128] = (v * cos + turned(v) * sin).astype(BF16)
        v = total[:, qw:]
        key = lax.broadcasted_iota(jnp.int32, v.shape, 1) < HD
        kv_ref[...] = jnp.where(key, v * cos + turned(v) * sin, v).astype(BF16)

    return pl.pallas_call(
        body,
        in_specs=[scalars()] + [whole()] * (4 + chips),
        out_specs=[whole()] * 4,
        out_shape=[
            jax.ShapeDtypeStruct((own, model), BF16),
            jax.ShapeDtypeStruct((own, qw), BF16),
            jax.ShapeDtypeStruct((own, 2 * HD), BF16),
            jax.ShapeDtypeStruct((2 * chips * wrows, width), BF16),
        ],
        cost_estimate=tiny(),
        name="qkv_forward",
    )(ids, cos_table, sin_table, near, far, *x_blocks)


def attention_mask(s_ref, l_ref, rows, block):
    core, rep, span = s_ref[1], s_ref[4], (block + 1) * rows

    def coded(pos):
        bound, code = 0, jnp.zeros(pos.shape, jnp.int32)
        for n in range(DOCS):
            bound = bound + l_ref[rep, n]
            code = code + jnp.where(pos >= bound, 1, 0)
        return jnp.where(code < DOCS - 1, code, 1000 + pos)

    q_pos = (2 * block + core) * rows + lax.broadcasted_iota(jnp.int32, (rows, 1), 0)
    index = lax.broadcasted_iota(jnp.int32, (1, 2 * span), 1)
    side = jnp.where(index < span, core, 1 - core)
    index = jnp.where(index < span, index, index - span)
    k_pos = (2 * (index // rows) + side) * rows + index % rows
    q_code = coded(q_pos)
    allowed = (coded(k_pos) == q_code) & (k_pos <= q_pos)
    return jnp.where(allowed, 0.0, MASK_FILL), jnp.where(q_code < DOCS, 1.0, 0.0)


def attention_forward(ids, lengths, q, kv_own, kv_other, rows, stack=4):
    own, qw = q.shape
    scale = 1.0 / math.sqrt(HD)
    heads = qw // HD
    stack = min(stack, heads)

    def body(s_ref, d_ref, q_ref, a_ref, b_ref, o_ref, l_ref):
        for block in range(own // rows):

            @pl.when(pl.program_id(0) == block)
            def _(block=block):
                span = (block + 1) * rows
                bias, valid = attention_mask(s_ref, d_ref, rows, block)
                lane = lax.broadcasted_iota(jnp.int32, (rows, 128), 1)
                sums = jnp.zeros((rows, 128), F32)
                keys = jnp.concatenate([a_ref[:span, :], b_ref[:span, :]], axis=0)
                k, v = keys[:, :HD], keys[:, HD:]
                for g in range(heads // stack):
                    qs = [q_ref[:, h * HD : (h + 1) * HD] for h in range(g * stack, (g + 1) * stack)]
                    qs = jnp.concatenate(qs, axis=0) * jnp.asarray(scale, BF16)
                    s = dot_nt(qs, k).reshape(stack, rows, 2 * span) + bias[None]
                    top = jnp.max(s, axis=-1, keepdims=True)
                    p = jnp.exp(s - top)
                    tot = jnp.sum(p, axis=-1, keepdims=True)
                    p = (p * (1.0 / tot)).astype(BF16).reshape(stack * rows, 2 * span)
                    o = dot(p, v).reshape(stack, rows, HD) * valid[None]
                    o = o.astype(BF16)
                    lse = top + jnp.log(tot)
                    for t in range(stack):
                        h = g * stack + t
                        sums = jnp.where(lane == h, lse[t], sums)
                        if t % 2:
                            pair = jnp.concatenate([o[t - 1], o[t]], axis=1)
                            o_ref[:, (h - 1) * HD : (h + 1) * HD] = pair
                l_ref[...] = sums

    blocked = lambda i: (i, 0)
    fixed = pl.BlockSpec((own, 2 * HD), lambda i: (0, 0))
    return pl.pallas_call(
        body,
        grid=(own // rows,),
        in_specs=[scalars(), scalars(), pl.BlockSpec((rows, qw), blocked), fixed, fixed],
        out_specs=[pl.BlockSpec((rows, qw), blocked), pl.BlockSpec((rows, 128), blocked)],
        out_shape=[
            jax.ShapeDtypeStruct((own, qw), BF16),
            jax.ShapeDtypeStruct((own, 128), F32),
        ],
        cost_estimate=tiny(),
        name="attention_forward",
    )(ids, lengths, q, kv_own, kv_other)


def attention_backward(
    ids, lengths, q, kv_own, kv_other, sums, d_out, cos_table, sin_table, rows, stack=4
):
    own, qw = q.shape
    scale = 1.0 / math.sqrt(HD)
    heads = qw // HD
    stack = min(stack, heads)
    blocks = own // rows

    def body(
        s_ref, n_ref, q_ref, a_ref, b_ref, l_ref, d_ref, cos_ref, sin_ref, dq_ref, dkv_ref,
    ):
        @pl.when(pl.program_id(0) == 0)
        def _():
            dkv_ref[...] = jnp.zeros_like(dkv_ref)

        for block in range(blocks):

            @pl.when(pl.program_id(0) == block)
            def _(block=block):
                span = (block + 1) * rows
                bias, valid = attention_mask(s_ref, n_ref, rows, block)
                valid = valid.astype(BF16)
                cos, sin = cos_ref[...], sin_ref[...]
                keys = jnp.concatenate([a_ref[:span, :], b_ref[:span, :]], axis=0)
                k, v = keys[:, :HD], keys[:, HD:]
                lane = lax.broadcasted_iota(jnp.int32, (rows, 128), 1)

                def some(g, carry):
                    at = pl.ds(pl.multiple_of(g * stack * HD, 128), stack * HD)
                    wide_q = q_ref[:, at] * jnp.asarray(scale, BF16)
                    wide_d = d_ref[:, at] * valid
                    qs = [wide_q[:, h * HD : (h + 1) * HD] for h in range(stack)]
                    qs = jnp.concatenate(qs, axis=0)
                    ds = [wide_d[:, h * HD : (h + 1) * HD] for h in range(stack)]
                    ds = jnp.concatenate(ds, axis=0)
                    lse = [jnp.where(lane == g * stack + t, l_ref[...], 0.0) for t in range(stack)]
                    lse = jnp.stack([jnp.sum(v, axis=-1, keepdims=True) for v in lse])
                    s = dot_nt(qs, k).reshape(stack, rows, 2 * span) + bias[None]
                    p = jnp.exp(s - lse)
                    dp = dot_nt(ds, v).reshape(stack, rows, 2 * span)
                    inner = jnp.sum(p * dp, axis=-1, keepdims=True)
                    grad = (p * (dp - inner)).astype(BF16).reshape(stack * rows, 2 * span)
                    p = p.astype(BF16).reshape(stack * rows, 2 * span)
                    dq = (dot(grad, k) * scale).reshape(stack, rows, HD)
                    both = jnp.concatenate([dot_tn(grad, qs), dot_tn(p, ds)], axis=1)
                    dkv_ref[:span, :] += both[:span]
                    dkv_ref[own : own + span, :] += both[span:]
                    for t in range(1, stack, 2):
                        w = jnp.concatenate([dq[t - 1], dq[t]], axis=1)
                        w = w * cos - turned(w) * sin
                        to = pl.ds(pl.multiple_of((g * stack + t - 1) * HD, 128), 2 * HD)
                        dq_ref[:, to] = w.astype(BF16)
                    return carry

                lax.fori_loop(0, heads // stack, some, 0)

    blocked = lambda i: (i, 0)
    fixed = pl.BlockSpec((own, 2 * HD), lambda i: (0, 0))
    table = pl.BlockSpec((rows, 128), blocked)
    wide = pl.BlockSpec((rows, qw), blocked)
    return pl.pallas_call(
        body,
        grid=(blocks,),
        in_specs=[scalars(), scalars(), wide, fixed, fixed, table, wide, table, table],
        out_specs=[wide, pl.BlockSpec((2 * own, 2 * HD), lambda i: (0, 0))],
        out_shape=[
            jax.ShapeDtypeStruct((own, qw), BF16),
            jax.ShapeDtypeStruct((2 * own, 2 * HD), F32),
        ],
        cost_estimate=tiny(),
        name="attention_backward",
    )(ids, lengths, q, kv_own, kv_other, sums, d_out, cos_table, sin_table)


def feed_forward(ids, z_blocks, cot, weights, w_down):
    rows, model = z_blocks[0].shape
    chips = len(z_blocks)
    part, width = weights[0][0].shape[1:]
    own, tile = rows * chips, min(TILE, width)
    turns = pl.cdiv(width, tile)

    def body(s_ref, *refs):
        z_refs, c_ref, w_refs = refs[:chips], refs[chips], refs[chips + 1 : chips + 9]
        d_ref, m_ref, dg_ref, du_ref, z_ref, b_ref, w_ref, acc_ref = refs[chips + 9 :]
        chip, core, half = s_ref[0], s_ref[1], s_ref[2]
        turn = pl.program_id(0)

        @pl.when(turn == 0)
        def _():
            for k in range(chips):
                at = pl.multiple_of((chip ^ k) * rows, rows)
                z_ref[pl.ds(at, rows), :] = z_refs[k][...]
            acc_ref[...] = jnp.zeros_like(acc_ref)

        def work(cols, last):
            for m in range(2):
                for i in range(4):
                    side = core if i < 2 else 1 - core
                    piece = half if i % 2 == 0 else 1 - half
                    for j in range(chips):
                        at = pl.multiple_of((2 * (2 * j + side) + piece) * part, part)
                        w_ref[m, pl.ds(at, part), :cols] = w_refs[4 * m + i][j, :, :cols]
            gate = dot(z_ref[...], w_ref[0, :, :cols])
            up = dot(z_ref[...], w_ref[1, :, :cols])
            dm = dot_nt(c_ref[...], d_ref[:cols, :])
            sig = 1.0 / (1.0 + jnp.exp(-gate))
            silu = gate * sig
            m_ref[:, :cols] = (silu * up).astype(BF16)
            dg = (dm * up * sig * (1.0 + gate * (1.0 - sig))).astype(BF16)
            du = (dm * silu).astype(BF16)
            dg_ref[:, :cols] = dg
            du_ref[:, :cols] = du
            back = dot_nt(dg, w_ref[0, :, :cols]) + dot_nt(du, w_ref[1, :, :cols])
            back = back + acc_ref[...]
            if last:
                b_ref[...] = back.astype(BF16)
            else:
                acc_ref[...] = back

        if turns > 1:

            @pl.when(turn < turns - 1)
            def _():
                work(tile, False)

        @pl.when(turn == turns - 1)
        def _():
            work(width - (turns - 1) * tile, True)

    joined = pl.BlockSpec((own, model), lambda n, s: (0, 0))
    out_tile = pl.BlockSpec((own, tile), lambda n, s: (0, n))
    return pl.pallas_call(
        body,
        grid_spec=pltpu.PrefetchScalarGridSpec(
            num_scalar_prefetch=1,
            grid=(turns,),
            in_specs=[pl.BlockSpec((rows, model), lambda n, s: (0, 0))] * chips
            + [joined]
            + [pl.BlockSpec((chips, part, tile), lambda n, s: (0, 0, n))] * 8
            + [pl.BlockSpec((tile, model), lambda n, s: (n, 0))],
            out_specs=[out_tile] * 3 + [joined] * 2,
            scratch_shapes=[
                pltpu.VMEM((2, model, tile), BF16),
                pltpu.VMEM((own, model), F32),
            ],
        ),
        out_shape=[jax.ShapeDtypeStruct((own, width), BF16)] * 3
        + [jax.ShapeDtypeStruct((own, model), BF16)] * 2,
        cost_estimate=tiny(),
        name="feed_forward",
    )(ids, *z_blocks, cot, *weights[0], *weights[1], w_down)


def out_proj(ids, attn, near, far, chips):
    own, depth = attn.shape
    wrows, model = near.shape
    rows = own // chips

    def body(c_ref, a_ref, n_ref, f_ref, *outs):
        chip, core, w_ref = c_ref[0], c_ref[1], outs[-1]
        w_ref[pl.ds(pl.multiple_of(core * wrows, wrows), wrows), :] = n_ref[...]
        w_ref[pl.ds(pl.multiple_of((1 - core) * wrows, wrows), wrows), :] = f_ref[...]
        for k in range(chips):
            at = pl.multiple_of((chip ^ k) * rows, rows)
            outs[k][...] = dot(a_ref[pl.ds(at, rows), :], w_ref[...]).astype(BF16)

    return pl.pallas_call(
        body,
        in_specs=[scalars()] + [whole()] * 3,
        out_specs=[whole()] * (chips + 1),
        out_shape=[jax.ShapeDtypeStruct((rows, model), BF16)] * chips
        + [jax.ShapeDtypeStruct((depth, model), BF16)],
        cost_estimate=tiny(),
        name="out_proj",
    )(ids, attn, near, far)


def residual_norm(tokens, parts):
    rows, model = tokens.shape

    def body(x_ref, *refs):
        y_ref, z_ref = refs[-2:]
        y = x_ref[...].astype(F32)
        for p in refs[:-2]:
            y = y + p[...].astype(F32)
        y_ref[...] = y
        inv = lax.rsqrt(jnp.mean(y * y, axis=-1, keepdims=True) + NORM_EPS)
        z_ref[...] = (y * inv).astype(BF16)

    return pl.pallas_call(
        body,
        in_specs=[whole()] * (1 + len(parts)),
        out_specs=[whole()] * 2,
        out_shape=[
            jax.ShapeDtypeStruct((rows, model), F32),
            jax.ShapeDtypeStruct((rows, model), BF16),
        ],
        cost_estimate=tiny(),
        name="residual_norm",
    )(tokens, *parts)


def residual_norm_back(base, parts, y, copies):
    rows, model = y.shape
    count = parts.shape[0] // rows

    def body(b_ref, y_ref, p_ref, f_ref, l_ref, n_ref):
        e = p_ref[:rows, :].astype(F32)
        for i in range(1, count):
            e = e + p_ref[i * rows : (i + 1) * rows, :].astype(F32)
        v = y_ref[...].astype(F32)
        inv = lax.rsqrt(jnp.mean(v * v, axis=-1, keepdims=True) + NORM_EPS)
        z = v * inv
        ez = e * z
        n_ref[...] = jnp.sum(ez, axis=0, keepdims=True)
        out = b_ref[...].astype(F32) + inv * (e - z * jnp.mean(ez, axis=-1, keepdims=True))
        f_ref[...] = out
        for i in range(copies):
            l_ref[i * rows : (i + 1) * rows, :] = out.astype(BF16)

    return pl.pallas_call(
        body,
        in_specs=[whole()] * 3,
        out_specs=[whole()] * 3,
        out_shape=[
            jax.ShapeDtypeStruct((rows, model), F32),
            jax.ShapeDtypeStruct((copies * rows, model), BF16),
            jax.ShapeDtypeStruct((1, model), F32),
        ],
        cost_estimate=tiny(),
        name="residual_norm_back",
    )(base, y, parts)


def strips(value, ref, lead=()):
    rows, width = value.shape
    for t in range(pl.cdiv(width, 128)):
        v = value[:, t * 128 : (t + 1) * 128]
        if v.shape[1] < 128:
            v = jnp.concatenate([v, jnp.zeros((rows, 128 - v.shape[1]), v.dtype)], axis=1)
        ref[(*lead, slice(t * rows, (t + 1) * rows), slice(None))] = v


def weight_grad(ids, left, right, chips):
    own, model = left.shape
    width = right.shape[1]
    rows = model // (2 * chips)
    long = pl.cdiv(width, 128) * rows
    group = min(4, chips)
    turns = chips // group

    def body(c_ref, l_ref, r_ref, near_ref, far_ref):
        step = pl.program_id(0)
        near = step >= turns
        side = jnp.where(near, c_ref[1], 1 - c_ref[1])
        first = jnp.where(near, step - turns, step) * group
        blocks = []
        for j in range(group):
            at = pl.multiple_of((2 * (first + j) + side) * rows, rows)
            blocks.append(l_ref[:, pl.ds(at, rows)])
        out = dot_tn(jnp.concatenate(blocks, axis=1), r_ref[...]).astype(BF16)

        @pl.when(near)
        def _():
            for j in range(group):
                strips(out[j * rows : (j + 1) * rows], near_ref, (j,))

        @pl.when(step < turns)
        def _():
            for j in range(group):
                strips(out[j * rows : (j + 1) * rows], far_ref, (j,))

    return pl.pallas_call(
        body,
        grid_spec=pltpu.PrefetchScalarGridSpec(
            num_scalar_prefetch=1,
            grid=(2 * turns,),
            in_specs=[
                pl.BlockSpec((own, model), lambda t, c: (0, 0)),
                pl.BlockSpec((own, width), lambda t, c: (0, 0)),
            ],
            out_specs=[
                pl.BlockSpec((group, long, 128), lambda t, c: (jnp.maximum(t - turns, 0), 0, 0)),
                pl.BlockSpec((group, long, 128), lambda t, c: (jnp.minimum(t, turns - 1), 0, 0)),
            ],
        ),
        out_shape=[jax.ShapeDtypeStruct((chips, long, 128), BF16)] * 2,
        cost_estimate=tiny(),
        name="weight_grad",
    )(ids, left, right)


def row_grad(ids, left, right, cuts):
    own, depth = left.shape
    model = right.shape[1]
    rows, width = depth // 2, model // cuts
    long = width // 128 * rows

    def body(c_ref, l_ref, r_ref, near_ref, far_ref, full_ref):
        core = c_ref[1]
        full_ref[...] = dot_tn(l_ref[...], r_ref[...])
        near = full_ref[pl.ds(pl.multiple_of(core * rows, 8), rows), :]
        far = full_ref[pl.ds(pl.multiple_of((1 - core) * rows, 8), rows), :]
        strips(near.astype(BF16), near_ref, (0,))
        strips(far.astype(BF16), far_ref, (0,))

    out = pl.BlockSpec((1, long, 128), lambda n, c: (n, 0, 0))
    return pl.pallas_call(
        body,
        grid_spec=pltpu.PrefetchScalarGridSpec(
            num_scalar_prefetch=1,
            grid=(cuts,),
            in_specs=[
                pl.BlockSpec((own, depth), lambda n, c: (0, 0)),
                pl.BlockSpec((own, width), lambda n, c: (0, n)),
            ],
            out_specs=[out] * 2,
            scratch_shapes=[pltpu.VMEM((depth, width), F32)],
        ),
        out_shape=[jax.ShapeDtypeStruct((cuts, long, 128), BF16)] * 2,
        cost_estimate=tiny(),
        name="row_grad",
    )(ids, left, right)


def chain_step(ids, own, outer, sent, inner, coming):
    def size(v):
        return 0 if v is None else v[0].shape[1] if isinstance(v, tuple) else v.shape[0]

    ins = [own, outer if own is not None else None, sent, inner, coming]
    have = [v is not None for v in ins]
    sizes = [size(own), max(size(sent), size(coming))]

    def body(s_ref, *refs):
        refs = list(refs)
        o_ref, x_ref, i_ref, y_ref, c_ref = [refs.pop(0) if h else None for h in have]
        s_out, a_out = [refs.pop(0) if n else None for n in sizes]
        ends = s_ref[3] == 1

        def each(count, work):
            step = math.gcd(512, count)

            def turn(n, carry):
                work(pl.ds(pl.multiple_of(n * step, step), step))
                return carry

            lax.fori_loop(0, count // step, turn, 0)

        if s_out is not None:

            def add_own(at):
                s_out[at, :] = o_ref[at, :] + x_ref[at, :]

            each(size(own), add_own)
        if c_ref is not None:

            @pl.when(ends)
            def _():
                def copy(at):
                    a_out[at, :] = c_ref[at, :]

                each(size(coming), copy)

        if i_ref is not None:

            @pl.when(jnp.logical_not(ends))
            def _():
                def add_sent(at):
                    a_out[at, :] = i_ref[at, :] + y_ref[at, :]

                each(size(sent), add_sent)

    def spec(v):
        if not isinstance(v, tuple):
            return pl.BlockSpec(v.shape, lambda i: (0, 0))
        block = v[1]
        return pl.BlockSpec((pl.Squeezed(), *v[0].shape[1:]), lambda i: (block, 0, 0))

    outs = pl.pallas_call(
        body,
        grid=(1,),
        in_specs=[scalars()] + [spec(v) for v in ins if v is not None],
        out_specs=[pl.BlockSpec((n, 128), lambda i: (0, 0)) for n in sizes if n],
        out_shape=[jax.ShapeDtypeStruct((n, 128), BF16) for n in sizes if n],
        cost_estimate=tiny(),
        name="chain_step",
    )(ids, *[v[0] if isinstance(v, tuple) else v for v in ins if v is not None])
    outs = list(outs)
    return [outs.pop(0) if n else None for n in sizes]


def beside(ids, blocks, rows, width, scale=None):
    count = len(blocks)
    tiles = pl.cdiv(width, 128)
    long = tiles * rows
    if scale is None:
        scale = jnp.ones((rows, 1), F32)
    if width % 128:
        full = [
            a[:long].reshape(tiles, rows, 128).transpose(1, 0, 2).reshape(rows, -1)
            for a, b in blocks
        ]
        return jnp.concatenate([f[:, :width] for f in full], axis=1).astype(F32) * scale

    def body(c_ref, s_ref, *refs):
        scale, out_ref = s_ref[...], refs[-1]
        for k in range(count):
            for end in (0, 1):

                @pl.when((pl.program_id(0) == k) & (c_ref[3] == end))
                def _(ref=refs[2 * k + end]):
                    for t in range(tiles):
                        v = ref[t * rows : (t + 1) * rows, :].astype(F32)
                        out_ref[:, t * 128 : (t + 1) * 128] = v * scale

    return pl.pallas_call(
        body,
        grid_spec=pltpu.PrefetchScalarGridSpec(
            num_scalar_prefetch=1,
            grid=(count,),
            in_specs=[pl.BlockSpec((rows, 1), lambda k, c: (0, 0))]
            + [pl.BlockSpec((long, 128), lambda k, c: (0, 0))] * (2 * count),
            out_specs=pl.BlockSpec((rows, width), lambda k, c: (0, k)),
        ),
        out_shape=jax.ShapeDtypeStruct((rows, count * width), F32),
        cost_estimate=tiny(),
        name="beside",
    )(ids, scale, *[v for pair in blocks for v in pair])


def pair_sum(near, far):
    count, rows, lanes = near.shape

    def body(a_ref, b_ref, out_ref):
        out_ref[...] = a_ref[...] + b_ref[...]

    spec = pl.BlockSpec((1, rows, lanes), lambda k: (k, 0, 0))
    return pl.pallas_call(
        body,
        grid=(count,),
        in_specs=[spec] * 2,
        out_specs=spec,
        out_shape=jax.ShapeDtypeStruct(near.shape, BF16),
        cost_estimate=tiny(),
        name="pair_sum",
    )(near, far)


def local(
    tokens,
    cotangent,
    doc_lengths,
    norm1_gain,
    w_query,
    w_key,
    w_value,
    w_out,
    norm2_gain,
    w_gate,
    w_up,
    w_down,
):
    rows, model = tokens.shape
    group = lax.axis_size("fsdp")
    reps = lax.axis_size("rep")
    chips = group // 2
    dev = lax.axis_index("fsdp").astype(jnp.int32)
    rep = lax.axis_index("rep").astype(jnp.int32)
    chip, core, half = dev >> 1, dev & 1, rep & 1
    ends = jnp.where((rep == 0) | (rep == reps - 1), 1, 0).astype(jnp.int32)
    ids = jnp.stack([chip, core, half, ends, rep])
    seq_len = rows * group
    own = rows * chips
    wrows = w_query.shape[0]
    width = w_gate.shape[1] // chips
    kv_share = chips // KVH
    qw = H // chips * HD
    tie = lax.optimization_barrier
    sides = [[2 * k + c for k in range(chips)] for c in range(2)]

    def exchange(v):
        return lax.all_to_all(v, "fsdp", 0, 0, axis_index_groups=sides, tiled=True)

    def hop(v, k):
        return lax.ppermute(v, "fsdp", [(i, i ^ (2 * k)) for i in range(group)])

    def hops(blocks):
        return [blocks[0]] + [hop(blocks[k], k) for k in range(1, chips)]

    def swap(v):
        return lax.ppermute(v, "fsdp", [(i, i ^ 1) for i in range(group)])

    def trade(v):
        return lax.ppermute(v, "rep", [(i, i ^ 1) for i in range(reps)])

    def copies(v):
        return jnp.broadcast_to(v[None], (chips,) + v.shape).reshape(chips * v.shape[0], -1)

    sums_of = {}
    outer_pairs = [(0, 1), (1, 0), (2, 3), (3, 2)]

    class Line:
        def __init__(self):
            self.own = self.sent = self.total = self.outer = self.inner = None

        def busy(self):
            return any(v is not None for v in (self.own, self.sent, self.total))

    lines = [Line(), Line()]
    turn = [0]

    def visit(*carry, new=None):
        if reps != 4:
            if new is not None:
                value = lax.psum(new[1][new[2]], "rep")
                sums_of[f"{new[0]}{new[2]}"] = (value, value)
            return carry if len(carry) != 1 else carry[0]
        line = lines[turn[0] % 2]
        turn[0] += 1
        extra = [line.outer, line.inner, None if new is None else new[1]]
        tied = tie(tuple(carry) + tuple(v for v in extra if v is not None))
        carry, tied = tied[: len(carry)], list(tied[len(carry) :])
        outer, inner, coming = [None if v is None else tied.pop(0) for v in extra]
        coming = None if new is None else (coming, new[2])
        value = lambda pair: None if pair is None else pair[1]
        if line.total is not None:
            sums_of[line.total[0]] = (line.total[1], outer)
        own_sum = ahead = None
        if outer is None:
            ahead = None if coming is None else coming[0][coming[1]]
        elif line.own is not None or line.sent is not None or coming is not None:
            own_sum, ahead = chain_step(
                ids, value(line.own), outer, value(line.sent), inner, coming
            )
        line.total = None if line.sent is None else (line.sent[0], ahead)
        line.sent = None if line.own is None else (line.own[0], own_sum)
        line.own = None if coming is None else (f"{new[0]}{new[2]}", coming)
        line.outer = None if ahead is None else lax.ppermute(ahead, "rep", outer_pairs)
        line.inner = (
            None if line.sent is None else lax.ppermute(line.sent[1], "rep", [(1, 2), (2, 1)])
        )
        return carry if len(carry) != 1 else carry[0]

    def summed(name, count):
        return [sums_of[f"{name}{k}"] for k in range(count)]

    starts = 2 * rows * jnp.arange(chips, dtype=jnp.int32) + core * rows
    own_pos = (starts[:, None] + jnp.arange(rows, dtype=jnp.int32)[None, :]).reshape(own)
    lane = jnp.arange(128)
    inverse = jnp.exp(-math.log(ROPE_BASE) / (HD // 2) * (lane % (HD // 2)).astype(F32))
    angles = own_pos.astype(F32)[:, None] * inverse[None, :]
    cos_table = jnp.cos(angles)
    sin_table = jnp.sin(angles) * jnp.where(lane % HD < HD // 2, -1.0, 1.0)[None, :]

    gain_one = norm1_gain.astype(F32)[:, None]
    gain_two = norm2_gain.astype(F32)[:, None]
    x_blocks = hops([tokens] * chips)
    qkv_near = exchange(pick_qkv(w_query, w_key, w_value, gain_one, chips))
    gate_part, up_part = pick_half(w_gate, w_up, gain_two, ids, chips)
    w_out_far = swap(w_out)
    w_down_c = join_cores(ids, w_down, swap(w_down))
    *x_blocks, cos_table, sin_table, gate_part, up_part, w_out_far, w_down_c = tie(
        (*x_blocks, cos_table, sin_table, gate_part, up_part, w_out_far, w_down_c)
    )
    gate_near = exchange(gate_part)
    normed_one, queries, kv_near, w_qkv = qkv_kernel(
        ids, x_blocks, qkv_near, swap(qkv_near), cos_table, sin_table
    )
    queries, gate_near, up_part, cot = tie((queries, gate_near, up_part, cotangent))
    up_near = exchange(up_part)
    gate_traded = trade(gate_near)
    kv_far = swap(kv_near)
    attn, sums = attention_forward(ids, doc_lengths, queries, kv_near, kv_far, rows)
    gate_far = swap(gate_near)
    attn, up_near, gate_far = tie((attn, up_near, gate_far))
    up_traded = trade(up_near)
    *mixed, w_out_c = out_proj(ids, attn, w_out, w_out_far, chips)
    *mixed, cot = tie((*mixed, cot))
    parts = hops(mixed)
    cot_rows = exchange(copies(cot))
    *parts, gate_traded, up_far = tie((*parts, gate_traded, swap(up_near)))
    resid, normed = residual_norm(tokens, parts)
    z_blocks = hops([normed] * chips)
    weights = [
        [gate_near, gate_traded, gate_far, swap(gate_traded)],
        [up_near, up_traded, up_far, swap(up_traded)],
    ]
    inner, grad_gate, grad_up, normed_two, back = feed_forward(
        ids, z_blocks, cot_rows, weights, w_down_c
    )

    parts = exchange(back)
    down_near, down_far = row_grad(ids, inner, cot_rows, 4)
    down_far = swap(down_far)
    grad_gate, down_near = tie((grad_gate, down_near))
    gate_near, gate_far = weight_grad(ids, normed_two, grad_gate, chips)
    gate_near, gate_far, down_far, grad_up = tie((gate_near, gate_far, down_far, grad_up))
    gate_far = swap(gate_far)
    down = pair_sum(down_near, down_far)
    grad_up = visit(grad_up, new=("down", down, 0))
    up_near, up_far = weight_grad(ids, normed_two, grad_up, chips)
    up_near, up_far, parts = visit(up_near, up_far, parts, new=("down", down, 1))
    gate_part = exchange(pair_sum(gate_near, gate_far))
    up_far = swap(up_far)
    grad_resid, da, gain_two_local = residual_norm_back(cotangent, parts, resid, chips)
    da, inner = visit(da, inner, new=("down", down, 2))
    out = dot(inner, w_down_c).astype(BF16)
    up_part = pair_sum(up_near, up_far)
    out, up_part, gate_part = visit(out, up_part, gate_part, new=("down", down, 3))
    da = exchange(da)
    da, up_part = visit(da, up_part, new=("gate", gate_part, 0))
    up_part = exchange(up_part)
    dob = dot_nt(da, w_out_c).astype(BF16)
    out_near, out_far = row_grad(ids, attn, da, 2)
    dob, out_near, out_far = visit(dob, out_near, out_far, new=("gate", gate_part, 1))
    out_far = swap(out_far)
    dq, dkv = attention_backward(
        ids, doc_lengths, queries, kv_near, kv_far, sums, dob, cos_table, sin_table, rows
    )
    dq, dkv = visit(dq, dkv, new=("gate", gate_part, 2))
    dkv = dkv[:own] + swap(dkv[own:].astype(BF16)).astype(F32)
    half_turn = jnp.concatenate([dkv[:, HD // 2 : HD], dkv[:, : HD // 2]], axis=1)
    dk = dkv[:, :HD] * cos_table[:, :HD] - half_turn * sin_table[:, :HD]
    dqkv = jnp.concatenate([dq, dk.astype(BF16), dkv[:, HD:].astype(BF16)], axis=1)
    back = dot_nt(dqkv, w_qkv).astype(BF16)
    dqkv, back, up_part = visit(dqkv, back, up_part, new=("gate", gate_part, 3))
    parts = exchange(back)
    qkv_near, qkv_far = weight_grad(ids, normed_one, dqkv, chips)
    qkv_near, qkv_far = visit(qkv_near, qkv_far, new=("up", up_part, 0))
    qkv_part = pair_sum(qkv_near, swap(qkv_far))
    qkv_part, parts = visit(qkv_part, parts, new=("up", up_part, 1))
    qkv_part = exchange(qkv_part)
    _, grad_inputs, gain_one_local = residual_norm_back(grad_resid, parts, tokens, 1)
    gain_one_local = visit(gain_one_local, new=("up", up_part, 2))
    norms = jnp.concatenate([gain_one_local, gain_two_local], axis=0)
    norms = norms.reshape(2, chips, 2, wrows).transpose(2, 1, 0, 3)
    mine = lax.dynamic_index_in_dim(norms, core, 0, keepdims=False)
    other = lax.dynamic_index_in_dim(norms, 1 - core, 0, keepdims=False)
    mine = mine + swap(other)
    out_part = pair_sum(out_near, out_far)
    if reps == 4:
        grad_down = beside(ids, summed("down", 4), w_down.shape[0], model // 4)
        mine, grad_down = tie((mine, grad_down))
    mine, qkv_part, out_part = visit(mine, qkv_part, out_part, new=("up", up_part, 3))
    parts = exchange(out).reshape(chips, rows, model)
    norms = lax.dynamic_index_in_dim(mine, chip, 0, keepdims=False)
    for k in range(1, chips):
        norms = norms + hop(lax.dynamic_index_in_dim(mine, chip ^ k, 0, keepdims=False), k)
    qkv_part = qkv_part.reshape(2, -1, 128)
    norms = visit(norms, new=("qkv", qkv_part, 0))
    parts, norms = visit(parts, norms, new=("qkv", qkv_part, 1))
    result = (resid + jnp.sum(parts.astype(F32), axis=0)).astype(BF16)
    norms = norms.astype(BF16).reshape(-1, 128)
    norms = jnp.pad(norms, ((0, 256 - norms.shape[0]), (0, 0)))
    last = jnp.concatenate([out_part[1], norms], axis=0)[None]
    if reps == 4:
        grad_gate_out = beside(ids, summed("gate", 4), wrows, width, gain_two)
        last, grad_gate_out = visit(last, grad_gate_out, new=("out", out_part, 0))
    else:
        visit(new=("out", out_part, 0))
    visit(new=("last", last, 0))
    if reps != 4:
        for k in range(4, chips):
            visit(new=("gate", gate_part, k))
            visit(new=("up", up_part, k))
        grad_gate_out = beside(ids, summed("gate", chips), wrows, width, gain_two)
    while any(line.busy() for line in lines):
        visit()

    if reps != 4:
        grad_down = beside(ids, summed("down", 4), w_down.shape[0], model // 4)
    rows_of = wrows * pl.cdiv(qw + 2 * HD, 128)
    qkv = [
        (a[n : n + rows_of], b[n : n + rows_of])
        for a, b in summed("qkv", 2)
        for n in range(0, chips // 2 * rows_of, rows_of)
    ]
    last = sums_of["last0"]
    at = out_part.shape[1]
    norms = jnp.where(ends == 1, last[1], last[0])[at : at + 2 * wrows // 128]
    norms = norms.astype(F32).reshape(2, wrows)
    grad_query = beside(ids, qkv, wrows, qw, gain_one)
    kv_at = qw // 128 * wrows
    kv = [
        jnp.where(ends == 1, b[kv_at : kv_at + wrows], a[kv_at : kv_at + wrows]) for a, b in qkv
    ]
    kv = jnp.stack(kv).astype(F32).reshape(KVH, kv_share, wrows, 2, HD).sum(axis=1)
    kv = kv * gain_one[None, :, :, None]
    grad_key = kv[:, :, 0].transpose(1, 0, 2).reshape(wrows, KVH * HD)
    grad_value = kv[:, :, 1].transpose(1, 0, 2).reshape(wrows, KVH * HD)
    return (
        result,
        grad_inputs,
        norms[0] / gain_one[:, 0],
        grad_query,
        grad_key,
        grad_value,
        beside(ids, [sums_of["out0"], tuple(v[:at] for v in last)], wrows, model // 2),
        norms[1] / gain_two[:, 0],
        grad_gate_out,
        beside(ids, summed("up", chips), wrows, width, gain_two),
        grad_down,
    )


def solution(mesh):
    placed = (
        P(("rep", "fsdp"), None),
        P(("rep", "fsdp"), None),
        P(),
        P("fsdp"),
        P("fsdp", None),
        P("fsdp", None),
        P("fsdp", None),
        P("fsdp", None),
        P("fsdp"),
        P("fsdp", None),
        P("fsdp", None),
        P("fsdp", None),
    )
    return jax.shard_map(
        local,
        mesh=mesh,
        in_specs=placed,
        out_specs=(
            P(("rep", "fsdp"), None),
            P(("rep", "fsdp"), None),
            P("fsdp"),
            P("fsdp", None),
            P("fsdp", None),
            P("fsdp", None),
            P("fsdp", None),
            P("fsdp"),
            P("fsdp", None),
            P("fsdp", None),
            P("fsdp", None),
        ),
        check_vma=False,
    )
```

```python
import math

import jax
import jax.numpy as jnp
from jax import lax
from jax.experimental import pallas as pl
from jax.experimental.pallas import tpu as pltpu
from jax.sharding import PartitionSpec as P

H = 32
KVH = 4
HD = 64
DOCS = 8

NORM_EPS = 1e-05
ROPE_BASE = 10000.0
MASK_FILL = -1e30
TILE = 512
F32 = jnp.float32
BF16 = jnp.bfloat16


def dot(a, b):
    return jnp.dot(a, b, preferred_element_type=F32)


def dot_nt(a, b):
    return lax.dot_general(a, b, (((1,), (1,)), ((), ())), preferred_element_type=F32)


def dot_tn(a, b):
    return lax.dot_general(a, b, (((0,), (0,)), ((), ())), preferred_element_type=F32)


def tiny():
    return pl.CostEstimate(flops=1024, bytes_accessed=1024, transcendentals=0)


def whole():
    return pl.BlockSpec(memory_space=pltpu.VMEM)


def turned(v):
    low = lax.broadcasted_iota(jnp.int32, v.shape, 1) % HD < HD // 2
    return jnp.where(low, pltpu.roll(v, 128 - HD // 2, 1), pltpu.roll(v, HD // 2, 1))


def scalars():
    return pl.BlockSpec(memory_space=pltpu.SMEM)


def pick_qkv(w_query, w_key, w_value, gain, chips):
    rows, cols = w_query.shape
    qw, share = cols // chips, chips // KVH

    def body(g_ref, q_ref, k_ref, v_ref, out_ref):
        gain = g_ref[...]
        out_ref[0, :, :qw] = (q_ref[...].astype(F32) * gain).astype(BF16)
        for n in range(KVH):

            @pl.when(pl.program_id(0) // share == n)
            def _():
                at = slice(n * HD, (n + 1) * HD)
                kv = jnp.concatenate([k_ref[:, at], v_ref[:, at]], axis=1)
                out_ref[0, :, qw:] = (kv.astype(F32) * gain).astype(BF16)

    small = pl.BlockSpec((rows, KVH * HD), lambda k: (0, 0))
    return pl.pallas_call(
        body,
        grid=(chips,),
        in_specs=[
            pl.BlockSpec((rows, 1), lambda k: (0, 0)),
            pl.BlockSpec((rows, qw), lambda k: (0, k)),
            small,
            small,
        ],
        out_specs=pl.BlockSpec((1, rows, qw + 2 * HD), lambda k: (k, 0, 0)),
        out_shape=jax.ShapeDtypeStruct((chips, rows, qw + 2 * HD), BF16),
        cost_estimate=tiny(),
        name="pick_qkv",
    )(gain, w_query, w_key, w_value)


def pick_half(w_gate, w_up, gain, ids, count):
    rows, cols = w_gate.shape
    width, part = cols // count, rows // 2
    if width % 128:
        out = []
        for w in (w_gate, w_up):
            v = lax.dynamic_slice_in_dim((w.astype(F32) * gain).astype(BF16), ids[2] * part, part)
            out.append(v.reshape(part, count, width).transpose(1, 0, 2))
        return out

    def body(s_ref, n_ref, a_ref, b_ref, c_ref, d_ref):
        c_ref[0] = (a_ref[...].astype(F32) * n_ref[...]).astype(BF16)
        d_ref[0] = (b_ref[...].astype(F32) * n_ref[...]).astype(BF16)

    return pl.pallas_call(
        body,
        grid_spec=pltpu.PrefetchScalarGridSpec(
            num_scalar_prefetch=1,
            grid=(count,),
            in_specs=[pl.BlockSpec((part, 1), lambda k, s: (s[2], 0))]
            + [pl.BlockSpec((part, width), lambda k, s: (s[2], k))] * 2,
            out_specs=[pl.BlockSpec((1, part, width), lambda k, s: (k, 0, 0))] * 2,
        ),
        out_shape=[jax.ShapeDtypeStruct((count, part, width), BF16)] * 2,
        cost_estimate=tiny(),
        name="pick_half",
    )(ids, gain, w_gate, w_up)


def join_cores(ids, near, far):
    rows, cols = near.shape

    def body(s_ref, a_ref, b_ref, out_ref):
        @pl.when(pl.program_id(0) == 0)
        def _():
            out_ref[...] = a_ref[...]

        @pl.when(pl.program_id(0) == 1)
        def _():
            out_ref[...] = b_ref[...]

    return pl.pallas_call(
        body,
        grid_spec=pltpu.PrefetchScalarGridSpec(
            num_scalar_prefetch=1,
            grid=(2,),
            in_specs=[pl.BlockSpec((rows, cols), lambda f, s: (0, 0))] * 2,
            out_specs=pl.BlockSpec((rows, cols), lambda f, s: (s[1] ^ f, 0)),
        ),
        out_shape=jax.ShapeDtypeStruct((2 * rows, cols), near.dtype),
        cost_estimate=tiny(),
        name="join_cores",
    )(ids, near, far)


def qkv_kernel(ids, x_blocks, near, far, cos_table, sin_table):
    rows, model = x_blocks[0].shape
    chips = len(x_blocks)
    own = rows * chips
    wrows, width = near.shape[1:]
    qw = width - 2 * HD

    def body(c_ref, cos_ref, sin_ref, n_ref, f_ref, *refs):
        x_refs, (z_ref, q_ref, kv_ref, w_ref) = refs[:chips], refs[chips:]
        chip, core = c_ref[0], c_ref[1]
        for k in range(chips):
            at = pl.multiple_of((2 * k + core) * wrows, wrows)
            w_ref[pl.ds(at, wrows), :] = n_ref[k]
            at = pl.multiple_of((2 * k + 1 - core) * wrows, wrows)
            w_ref[pl.ds(at, wrows), :] = f_ref[k]
            x = x_refs[k][...].astype(F32)
            inv = lax.rsqrt(jnp.mean(x * x, axis=-1, keepdims=True) + NORM_EPS)
            at = pl.multiple_of((chip ^ k) * rows, rows)
            z_ref[pl.ds(at, rows), :] = (x * inv).astype(BF16)
        total = dot(z_ref[...], w_ref[...])
        cos, sin = cos_ref[...], sin_ref[...]
        for j in range(qw // 128):
            v = total[:, j * 128 : (j + 1) * 128]
            q_ref[:, j * 128 : (j + 1) * 128] = (v * cos + turned(v) * sin).astype(BF16)
        v = total[:, qw:]
        key = lax.broadcasted_iota(jnp.int32, v.shape, 1) < HD
        kv_ref[...] = jnp.where(key, v * cos + turned(v) * sin, v).astype(BF16)

    return pl.pallas_call(
        body,
        in_specs=[scalars()] + [whole()] * (4 + chips),
        out_specs=[whole()] * 4,
        out_shape=[
            jax.ShapeDtypeStruct((own, model), BF16),
            jax.ShapeDtypeStruct((own, qw), BF16),
            jax.ShapeDtypeStruct((own, 2 * HD), BF16),
            jax.ShapeDtypeStruct((2 * chips * wrows, width), BF16),
        ],
        cost_estimate=tiny(),
        name="qkv_forward",
    )(ids, cos_table, sin_table, near, far, *x_blocks)


def attention_mask(s_ref, l_ref, rows, block):
    core, rep, span = s_ref[1], s_ref[4], (block + 1) * rows

    def coded(pos):
        bound, code = 0, jnp.zeros(pos.shape, jnp.int32)
        for n in range(DOCS):
            bound = bound + l_ref[rep, n]
            code = code + jnp.where(pos >= bound, 1, 0)
        return jnp.where(code < DOCS - 1, code, 1000 + pos)

    q_pos = (2 * block + core) * rows + lax.broadcasted_iota(jnp.int32, (rows, 1), 0)
    index = lax.broadcasted_iota(jnp.int32, (1, 2 * span), 1)
    side = jnp.where(index < span, core, 1 - core)
    index = jnp.where(index < span, index, index - span)
    k_pos = (2 * (index // rows) + side) * rows + index % rows
    q_code = coded(q_pos)
    allowed = (coded(k_pos) == q_code) & (k_pos <= q_pos)
    return jnp.where(allowed, 0.0, MASK_FILL), jnp.where(q_code < DOCS, 1.0, 0.0)


def attention_forward(ids, lengths, q, kv_own, kv_other, rows, stack=4):
    own, qw = q.shape
    scale = 1.0 / math.sqrt(HD)
    heads = qw // HD
    stack = min(stack, heads)

    def body(s_ref, d_ref, q_ref, a_ref, b_ref, o_ref, l_ref):
        for block in range(own // rows):

            @pl.when(pl.program_id(0) == block)
            def _(block=block):
                span = (block + 1) * rows
                bias, valid = attention_mask(s_ref, d_ref, rows, block)
                lane = lax.broadcasted_iota(jnp.int32, (rows, 128), 1)
                sums = jnp.zeros((rows, 128), F32)
                keys = jnp.concatenate([a_ref[:span, :], b_ref[:span, :]], axis=0)
                k, v = keys[:, :HD], keys[:, HD:]
                for g in range(heads // stack):
                    qs = [q_ref[:, h * HD : (h + 1) * HD] for h in range(g * stack, (g + 1) * stack)]
                    qs = jnp.concatenate(qs, axis=0) * jnp.asarray(scale, BF16)
                    s = dot_nt(qs, k).reshape(stack, rows, 2 * span) + bias[None]
                    top = jnp.max(s, axis=-1, keepdims=True)
                    p = jnp.exp(s - top)
                    tot = jnp.sum(p, axis=-1, keepdims=True)
                    p = (p * (1.0 / tot)).astype(BF16).reshape(stack * rows, 2 * span)
                    o = dot(p, v).reshape(stack, rows, HD) * valid[None]
                    o = o.astype(BF16)
                    lse = top + jnp.log(tot)
                    for t in range(stack):
                        h = g * stack + t
                        sums = jnp.where(lane == h, lse[t], sums)
                        if t % 2:
                            pair = jnp.concatenate([o[t - 1], o[t]], axis=1)
                            o_ref[:, (h - 1) * HD : (h + 1) * HD] = pair
                l_ref[...] = sums

    blocked = lambda i: (i, 0)
    fixed = pl.BlockSpec((own, 2 * HD), lambda i: (0, 0))
    return pl.pallas_call(
        body,
        grid=(own // rows,),
        in_specs=[scalars(), scalars(), pl.BlockSpec((rows, qw), blocked), fixed, fixed],
        out_specs=[pl.BlockSpec((rows, qw), blocked), pl.BlockSpec((rows, 128), blocked)],
        out_shape=[
            jax.ShapeDtypeStruct((own, qw), BF16),
            jax.ShapeDtypeStruct((own, 128), F32),
        ],
        cost_estimate=tiny(),
        name="attention_forward",
    )(ids, lengths, q, kv_own, kv_other)


def attention_backward(
    ids, lengths, q, kv_own, kv_other, sums, d_out, cos_table, sin_table, rows, stack=4
):
    own, qw = q.shape
    scale = 1.0 / math.sqrt(HD)
    heads = qw // HD
    stack = min(stack, heads)
    blocks = own // rows

    def body(
        s_ref, n_ref, q_ref, a_ref, b_ref, l_ref, d_ref, cos_ref, sin_ref, dq_ref, dkv_ref,
    ):
        @pl.when(pl.program_id(0) == 0)
        def _():
            dkv_ref[...] = jnp.zeros_like(dkv_ref)

        for block in range(blocks):

            @pl.when(pl.program_id(0) == block)
            def _(block=block):
                span = (block + 1) * rows
                bias, valid = attention_mask(s_ref, n_ref, rows, block)
                valid = valid.astype(BF16)
                cos, sin = cos_ref[...], sin_ref[...]
                keys = jnp.concatenate([a_ref[:span, :], b_ref[:span, :]], axis=0)
                k, v = keys[:, :HD], keys[:, HD:]
                lane = lax.broadcasted_iota(jnp.int32, (rows, 128), 1)

                def some(g, carry):
                    at = pl.ds(pl.multiple_of(g * stack * HD, 128), stack * HD)
                    wide_q = q_ref[:, at] * jnp.asarray(scale, BF16)
                    wide_d = d_ref[:, at] * valid
                    qs = [wide_q[:, h * HD : (h + 1) * HD] for h in range(stack)]
                    qs = jnp.concatenate(qs, axis=0)
                    ds = [wide_d[:, h * HD : (h + 1) * HD] for h in range(stack)]
                    ds = jnp.concatenate(ds, axis=0)
                    lse = [jnp.where(lane == g * stack + t, l_ref[...], 0.0) for t in range(stack)]
                    lse = jnp.stack([jnp.sum(v, axis=-1, keepdims=True) for v in lse])
                    s = dot_nt(qs, k).reshape(stack, rows, 2 * span) + bias[None]
                    p = jnp.exp(s - lse)
                    dp = dot_nt(ds, v).reshape(stack, rows, 2 * span)
                    inner = jnp.sum(p * dp, axis=-1, keepdims=True)
                    grad = (p * (dp - inner)).astype(BF16).reshape(stack * rows, 2 * span)
                    p = p.astype(BF16).reshape(stack * rows, 2 * span)
                    dq = (dot(grad, k) * scale).reshape(stack, rows, HD)
                    both = jnp.concatenate([dot_tn(grad, qs), dot_tn(p, ds)], axis=1)
                    dkv_ref[:span, :] += both[:span]
                    dkv_ref[own : own + span, :] += both[span:]
                    for t in range(1, stack, 2):
                        w = jnp.concatenate([dq[t - 1], dq[t]], axis=1)
                        w = w * cos - turned(w) * sin
                        to = pl.ds(pl.multiple_of((g * stack + t - 1) * HD, 128), 2 * HD)
                        dq_ref[:, to] = w.astype(BF16)
                    return carry

                lax.fori_loop(0, heads // stack, some, 0)

    blocked = lambda i: (i, 0)
    fixed = pl.BlockSpec((own, 2 * HD), lambda i: (0, 0))
    table = pl.BlockSpec((rows, 128), blocked)
    wide = pl.BlockSpec((rows, qw), blocked)
    return pl.pallas_call(
        body,
        grid=(blocks,),
        in_specs=[scalars(), scalars(), wide, fixed, fixed, table, wide, table, table],
        out_specs=[wide, pl.BlockSpec((2 * own, 2 * HD), lambda i: (0, 0))],
        out_shape=[
            jax.ShapeDtypeStruct((own, qw), BF16),
            jax.ShapeDtypeStruct((2 * own, 2 * HD), F32),
        ],
        cost_estimate=tiny(),
        name="attention_backward",
    )(ids, lengths, q, kv_own, kv_other, sums, d_out, cos_table, sin_table)


def feed_forward(ids, z_blocks, cot, weights, w_down):
    rows, model = z_blocks[0].shape
    chips = len(z_blocks)
    part, width = weights[0][0].shape[1:]
    own, tile = rows * chips, min(TILE, width)
    turns = pl.cdiv(width, tile)

    def body(s_ref, *refs):
        z_refs, c_ref, w_refs = refs[:chips], refs[chips], refs[chips + 1 : chips + 9]
        d_ref, m_ref, dg_ref, du_ref, z_ref, b_ref, w_ref, acc_ref = refs[chips + 9 :]
        chip, core, half = s_ref[0], s_ref[1], s_ref[2]
        turn = pl.program_id(0)

        @pl.when(turn == 0)
        def _():
            for k in range(chips):
                at = pl.multiple_of((chip ^ k) * rows, rows)
                z_ref[pl.ds(at, rows), :] = z_refs[k][...]
            acc_ref[...] = jnp.zeros_like(acc_ref)

        def work(cols, last):
            for m in range(2):
                for i in range(4):
                    side = core if i < 2 else 1 - core
                    piece = half if i % 2 == 0 else 1 - half
                    for j in range(chips):
                        at = pl.multiple_of((2 * (2 * j + side) + piece) * part, part)
                        w_ref[m, pl.ds(at, part), :cols] = w_refs[4 * m + i][j, :, :cols]
            gate = dot(z_ref[...], w_ref[0, :, :cols])
            up = dot(z_ref[...], w_ref[1, :, :cols])
            dm = dot_nt(c_ref[...], d_ref[:cols, :])
            sig = 1.0 / (1.0 + jnp.exp(-gate))
            silu = gate * sig
            m_ref[:, :cols] = (silu * up).astype(BF16)
            dg = (dm * up * sig * (1.0 + gate * (1.0 - sig))).astype(BF16)
            du = (dm * silu).astype(BF16)
            dg_ref[:, :cols] = dg
            du_ref[:, :cols] = du
            back = dot_nt(dg, w_ref[0, :, :cols]) + dot_nt(du, w_ref[1, :, :cols])
            back = back + acc_ref[...]
            if last:
                b_ref[...] = back.astype(BF16)
            else:
                acc_ref[...] = back

        if turns > 1:

            @pl.when(turn < turns - 1)
            def _():
                work(tile, False)

        @pl.when(turn == turns - 1)
        def _():
            work(width - (turns - 1) * tile, True)

    joined = pl.BlockSpec((own, model), lambda n, s: (0, 0))
    out_tile = pl.BlockSpec((own, tile), lambda n, s: (0, n))
    return pl.pallas_call(
        body,
        grid_spec=pltpu.PrefetchScalarGridSpec(
            num_scalar_prefetch=1,
            grid=(turns,),
            in_specs=[pl.BlockSpec((rows, model), lambda n, s: (0, 0))] * chips
            + [joined]
            + [pl.BlockSpec((chips, part, tile), lambda n, s: (0, 0, n))] * 8
            + [pl.BlockSpec((tile, model), lambda n, s: (n, 0))],
            out_specs=[out_tile] * 3 + [joined] * 2,
            scratch_shapes=[
                pltpu.VMEM((2, model, tile), BF16),
                pltpu.VMEM((own, model), F32),
            ],
        ),
        out_shape=[jax.ShapeDtypeStruct((own, width), BF16)] * 3
        + [jax.ShapeDtypeStruct((own, model), BF16)] * 2,
        cost_estimate=tiny(),
        name="feed_forward",
    )(ids, *z_blocks, cot, *weights[0], *weights[1], w_down)


def out_proj(ids, attn, near, far, chips):
    own, depth = attn.shape
    wrows, model = near.shape
    rows = own // chips

    def body(c_ref, a_ref, n_ref, f_ref, *outs):
        chip, core, w_ref = c_ref[0], c_ref[1], outs[-1]
        w_ref[pl.ds(pl.multiple_of(core * wrows, wrows), wrows), :] = n_ref[...]
        w_ref[pl.ds(pl.multiple_of((1 - core) * wrows, wrows), wrows), :] = f_ref[...]
        for k in range(chips):
            at = pl.multiple_of((chip ^ k) * rows, rows)
            outs[k][...] = dot(a_ref[pl.ds(at, rows), :], w_ref[...]).astype(BF16)

    return pl.pallas_call(
        body,
        in_specs=[scalars()] + [whole()] * 3,
        out_specs=[whole()] * (chips + 1),
        out_shape=[jax.ShapeDtypeStruct((rows, model), BF16)] * chips
        + [jax.ShapeDtypeStruct((depth, model), BF16)],
        cost_estimate=tiny(),
        name="out_proj",
    )(ids, attn, near, far)


def residual_norm(tokens, parts):
    rows, model = tokens.shape

    def body(x_ref, *refs):
        y_ref, z_ref = refs[-2:]
        y = x_ref[...].astype(F32)
        for p in refs[:-2]:
            y = y + p[...].astype(F32)
        y_ref[...] = y
        inv = lax.rsqrt(jnp.mean(y * y, axis=-1, keepdims=True) + NORM_EPS)
        z_ref[...] = (y * inv).astype(BF16)

    return pl.pallas_call(
        body,
        in_specs=[whole()] * (1 + len(parts)),
        out_specs=[whole()] * 2,
        out_shape=[
            jax.ShapeDtypeStruct((rows, model), F32),
            jax.ShapeDtypeStruct((rows, model), BF16),
        ],
        cost_estimate=tiny(),
        name="residual_norm",
    )(tokens, *parts)


def residual_norm_back(base, parts, y, copies):
    rows, model = y.shape
    count = parts.shape[0] // rows

    def body(b_ref, y_ref, p_ref, f_ref, l_ref, n_ref):
        e = p_ref[:rows, :].astype(F32)
        for i in range(1, count):
            e = e + p_ref[i * rows : (i + 1) * rows, :].astype(F32)
        v = y_ref[...].astype(F32)
        inv = lax.rsqrt(jnp.mean(v * v, axis=-1, keepdims=True) + NORM_EPS)
        z = v * inv
        ez = e * z
        n_ref[...] = jnp.sum(ez, axis=0, keepdims=True)
        out = b_ref[...].astype(F32) + inv * (e - z * jnp.mean(ez, axis=-1, keepdims=True))
        f_ref[...] = out
        for i in range(copies):
            l_ref[i * rows : (i + 1) * rows, :] = out.astype(BF16)

    return pl.pallas_call(
        body,
        in_specs=[whole()] * 3,
        out_specs=[whole()] * 3,
        out_shape=[
            jax.ShapeDtypeStruct((rows, model), F32),
            jax.ShapeDtypeStruct((copies * rows, model), BF16),
            jax.ShapeDtypeStruct((1, model), F32),
        ],
        cost_estimate=tiny(),
        name="residual_norm_back",
    )(base, y, parts)


def strips(value, ref, lead=()):
    rows, width = value.shape
    for t in range(pl.cdiv(width, 128)):
        v = value[:, t * 128 : (t + 1) * 128]
        if v.shape[1] < 128:
            v = jnp.concatenate([v, jnp.zeros((rows, 128 - v.shape[1]), v.dtype)], axis=1)
        ref[(*lead, slice(t * rows, (t + 1) * rows), slice(None))] = v


def weight_grad(ids, left, right, chips):
    own, model = left.shape
    width = right.shape[1]
    rows = model // (2 * chips)
    long = pl.cdiv(width, 128) * rows
    group = min(2, chips)
    turns = chips // group

    def body(c_ref, l_ref, r_ref, near_ref, far_ref):
        step = pl.program_id(0)
        near = step >= turns
        side = jnp.where(near, c_ref[1], 1 - c_ref[1])
        first = jnp.where(near, step - turns, step) * group
        blocks = []
        for j in range(group):
            at = pl.multiple_of((2 * (first + j) + side) * rows, rows)
            blocks.append(l_ref[:, pl.ds(at, rows)])
        out = dot_tn(jnp.concatenate(blocks, axis=1), r_ref[...]).astype(BF16)

        @pl.when(near)
        def _():
            for j in range(group):
                strips(out[j * rows : (j + 1) * rows], near_ref, (j,))

        @pl.when(step < turns)
        def _():
            for j in range(group):
                strips(out[j * rows : (j + 1) * rows], far_ref, (j,))

    return pl.pallas_call(
        body,
        grid_spec=pltpu.PrefetchScalarGridSpec(
            num_scalar_prefetch=1,
            grid=(2 * turns,),
            in_specs=[
                pl.BlockSpec((own, model), lambda t, c: (0, 0)),
                pl.BlockSpec((own, width), lambda t, c: (0, 0)),
            ],
            out_specs=[
                pl.BlockSpec((group, long, 128), lambda t, c: (jnp.maximum(t - turns, 0), 0, 0)),
                pl.BlockSpec((group, long, 128), lambda t, c: (jnp.minimum(t, turns - 1), 0, 0)),
            ],
        ),
        out_shape=[jax.ShapeDtypeStruct((chips, long, 128), BF16)] * 2,
        cost_estimate=tiny(),
        name="weight_grad",
    )(ids, left, right)


def row_grad(ids, left, right, cuts):
    own, depth = left.shape
    model = right.shape[1]
    rows, width = depth // 2, model // cuts
    long = width // 128 * rows

    def body(c_ref, l_ref, r_ref, near_ref, far_ref, full_ref):
        core = c_ref[1]
        full_ref[...] = dot_tn(l_ref[...], r_ref[...]).astype(BF16)
        near = full_ref[pl.ds(pl.multiple_of(core * rows, 16), rows), :]
        far = full_ref[pl.ds(pl.multiple_of((1 - core) * rows, 16), rows), :]
        strips(near, near_ref, (0,))
        strips(far, far_ref, (0,))

    out = pl.BlockSpec((1, long, 128), lambda n, c: (n, 0, 0))
    return pl.pallas_call(
        body,
        grid_spec=pltpu.PrefetchScalarGridSpec(
            num_scalar_prefetch=1,
            grid=(cuts,),
            in_specs=[
                pl.BlockSpec((own, depth), lambda n, c: (0, 0)),
                pl.BlockSpec((own, width), lambda n, c: (0, n)),
            ],
            out_specs=[out] * 2,
            scratch_shapes=[pltpu.VMEM((depth, width), BF16)],
        ),
        out_shape=[jax.ShapeDtypeStruct((cuts, long, 128), BF16)] * 2,
        cost_estimate=tiny(),
        name="row_grad",
    )(ids, left, right)


def chain_step(ids, own, outer, sent, inner, coming):
    def size(v):
        return 0 if v is None else v[0].shape[1] if isinstance(v, tuple) else v.shape[0]

    ins = [own, outer if own is not None else None, sent, inner, coming]
    have = [v is not None for v in ins]
    sizes = [size(own), max(size(sent), size(coming))]

    def body(s_ref, *refs):
        refs = list(refs)
        o_ref, x_ref, i_ref, y_ref, c_ref = [refs.pop(0) if h else None for h in have]
        s_out, a_out = [refs.pop(0) if n else None for n in sizes]
        ends = s_ref[3] == 1

        def each(count, work):
            step = math.gcd(512, count)

            def turn(n, carry):
                work(pl.ds(pl.multiple_of(n * step, step), step))
                return carry

            lax.fori_loop(0, count // step, turn, 0)

        if s_out is not None:

            def add_own(at):
                s_out[at, :] = o_ref[at, :] + x_ref[at, :]

            each(size(own), add_own)
        if c_ref is not None:

            @pl.when(ends)
            def _():
                def copy(at):
                    a_out[at, :] = c_ref[at, :]

                each(size(coming), copy)

        if i_ref is not None:

            @pl.when(jnp.logical_not(ends))
            def _():
                def add_sent(at):
                    a_out[at, :] = i_ref[at, :] + y_ref[at, :]

                each(size(sent), add_sent)

    def spec(v):
        if not isinstance(v, tuple):
            return pl.BlockSpec(v.shape, lambda i: (0, 0))
        block = v[1]
        return pl.BlockSpec((pl.Squeezed(), *v[0].shape[1:]), lambda i: (block, 0, 0))

    outs = pl.pallas_call(
        body,
        grid=(1,),
        in_specs=[scalars()] + [spec(v) for v in ins if v is not None],
        out_specs=[pl.BlockSpec((n, 128), lambda i: (0, 0)) for n in sizes if n],
        out_shape=[jax.ShapeDtypeStruct((n, 128), BF16) for n in sizes if n],
        cost_estimate=tiny(),
        name="chain_step",
    )(ids, *[v[0] if isinstance(v, tuple) else v for v in ins if v is not None])
    outs = list(outs)
    return [outs.pop(0) if n else None for n in sizes]


def beside(ids, blocks, rows, width, scale=None):
    count = len(blocks)
    tiles = pl.cdiv(width, 128)
    long = tiles * rows
    if scale is None:
        scale = jnp.ones((rows, 1), F32)
    if width % 128:
        full = [
            a[:long].reshape(tiles, rows, 128).transpose(1, 0, 2).reshape(rows, -1)
            for a, b in blocks
        ]
        return jnp.concatenate([f[:, :width] for f in full], axis=1).astype(F32) * scale

    def body(c_ref, s_ref, *refs):
        scale, out_ref = s_ref[...], refs[-1]
        for k in range(count):
            for end in (0, 1):

                @pl.when((pl.program_id(0) == k) & (c_ref[3] == end))
                def _(ref=refs[2 * k + end]):
                    for t in range(tiles):
                        v = ref[t * rows : (t + 1) * rows, :].astype(F32)
                        out_ref[:, t * 128 : (t + 1) * 128] = v * scale

    return pl.pallas_call(
        body,
        grid_spec=pltpu.PrefetchScalarGridSpec(
            num_scalar_prefetch=1,
            grid=(count,),
            in_specs=[pl.BlockSpec((rows, 1), lambda k, c: (0, 0))]
            + [pl.BlockSpec((long, 128), lambda k, c: (0, 0))] * (2 * count),
            out_specs=pl.BlockSpec((rows, width), lambda k, c: (0, k)),
        ),
        out_shape=jax.ShapeDtypeStruct((rows, count * width), F32),
        cost_estimate=tiny(),
        name="beside",
    )(ids, scale, *[v for pair in blocks for v in pair])


def pair_sum(near, far):
    count, rows, lanes = near.shape

    def body(a_ref, b_ref, out_ref):
        out_ref[...] = a_ref[...] + b_ref[...]

    spec = pl.BlockSpec((2, rows, lanes), lambda k: (k, 0, 0))
    return pl.pallas_call(
        body,
        grid=(count // 2,),
        in_specs=[spec] * 2,
        out_specs=spec,
        out_shape=jax.ShapeDtypeStruct(near.shape, BF16),
        cost_estimate=tiny(),
        name="pair_sum",
    )(near, far)


def local(
    tokens,
    cotangent,
    doc_lengths,
    norm1_gain,
    w_query,
    w_key,
    w_value,
    w_out,
    norm2_gain,
    w_gate,
    w_up,
    w_down,
):
    rows, model = tokens.shape
    group = lax.axis_size("fsdp")
    reps = lax.axis_size("rep")
    chips = group // 2
    dev = lax.axis_index("fsdp").astype(jnp.int32)
    rep = lax.axis_index("rep").astype(jnp.int32)
    chip, core, half = dev >> 1, dev & 1, rep & 1
    ends = jnp.where((rep == 0) | (rep == reps - 1), 1, 0).astype(jnp.int32)
    ids = jnp.stack([chip, core, half, ends, rep])
    seq_len = rows * group
    own = rows * chips
    wrows = w_query.shape[0]
    width = w_gate.shape[1] // chips
    kv_share = chips // KVH
    qw = H // chips * HD
    tie = lax.optimization_barrier
    sides = [[2 * k + c for k in range(chips)] for c in range(2)]

    def exchange(v):
        return lax.all_to_all(v, "fsdp", 0, 0, axis_index_groups=sides, tiled=True)

    def hop(v, k):
        return lax.ppermute(v, "fsdp", [(i, i ^ (2 * k)) for i in range(group)])

    def hops(blocks):
        return [blocks[0]] + [hop(blocks[k], k) for k in range(1, chips)]

    def swap(v):
        return lax.ppermute(v, "fsdp", [(i, i ^ 1) for i in range(group)])

    def trade(v):
        return lax.ppermute(v, "rep", [(i, i ^ 1) for i in range(reps)])

    def copies(v):
        return jnp.broadcast_to(v[None], (chips,) + v.shape).reshape(chips * v.shape[0], -1)

    sums_of = {}
    outer_pairs = [(0, 1), (1, 0), (2, 3), (3, 2)]

    class Line:
        def __init__(self):
            self.own = self.sent = self.total = self.outer = self.inner = None

        def busy(self):
            return any(v is not None for v in (self.own, self.sent, self.total))

    lines = [Line(), Line()]
    turn = [0]

    def visit(*carry, new=None):
        if reps != 4:
            if new is not None:
                value = lax.psum(new[1][new[2]], "rep")
                sums_of[f"{new[0]}{new[2]}"] = (value, value)
            return carry if len(carry) != 1 else carry[0]
        line = lines[turn[0] % 2]
        turn[0] += 1
        extra = [line.outer, line.inner, None if new is None else new[1]]
        tied = tie(tuple(carry) + tuple(v for v in extra if v is not None))
        carry, tied = tied[: len(carry)], list(tied[len(carry) :])
        outer, inner, coming = [None if v is None else tied.pop(0) for v in extra]
        coming = None if new is None else (coming, new[2])
        value = lambda pair: None if pair is None else pair[1]
        if line.total is not None:
            sums_of[line.total[0]] = (line.total[1], outer)
        own_sum = ahead = None
        if outer is None:
            ahead = None if coming is None else coming[0][coming[1]]
        elif line.own is not None or line.sent is not None or coming is not None:
            own_sum, ahead = chain_step(
                ids, value(line.own), outer, value(line.sent), inner, coming
            )
        line.total = None if line.sent is None else (line.sent[0], ahead)
        line.sent = None if line.own is None else (line.own[0], own_sum)
        line.own = None if coming is None else (f"{new[0]}{new[2]}", coming)
        line.outer = None if ahead is None else lax.ppermute(ahead, "rep", outer_pairs)
        line.inner = (
            None if line.sent is None else lax.ppermute(line.sent[1], "rep", [(1, 2), (2, 1)])
        )
        return carry if len(carry) != 1 else carry[0]

    def summed(name, count):
        return [sums_of[f"{name}{k}"] for k in range(count)]

    starts = 2 * rows * jnp.arange(chips, dtype=jnp.int32) + core * rows
    own_pos = (starts[:, None] + jnp.arange(rows, dtype=jnp.int32)[None, :]).reshape(own)
    lane = jnp.arange(128)
    inverse = jnp.exp(-math.log(ROPE_BASE) / (HD // 2) * (lane % (HD // 2)).astype(F32))
    angles = own_pos.astype(F32)[:, None] * inverse[None, :]
    cos_table = jnp.cos(angles)
    sin_table = jnp.sin(angles) * jnp.where(lane % HD < HD // 2, -1.0, 1.0)[None, :]

    gain_one = norm1_gain.astype(F32)[:, None]
    gain_two = norm2_gain.astype(F32)[:, None]
    x_blocks = hops([tokens] * chips)
    qkv_near = exchange(pick_qkv(w_query, w_key, w_value, gain_one, chips))
    gate_part, up_part = pick_half(w_gate, w_up, gain_two, ids, chips)
    w_out_far = swap(w_out)
    w_down_c = join_cores(ids, w_down, swap(w_down))
    *x_blocks, cos_table, sin_table, gate_part, up_part, w_out_far, w_down_c = tie(
        (*x_blocks, cos_table, sin_table, gate_part, up_part, w_out_far, w_down_c)
    )
    gate_near = exchange(gate_part)
    normed_one, queries, kv_near, w_qkv = qkv_kernel(
        ids, x_blocks, qkv_near, swap(qkv_near), cos_table, sin_table
    )
    queries, gate_near, up_part, cot = tie((queries, gate_near, up_part, cotangent))
    up_near = exchange(up_part)
    gate_traded = trade(gate_near)
    kv_far = swap(kv_near)
    attn, sums = attention_forward(ids, doc_lengths, queries, kv_near, kv_far, rows)
    gate_far = swap(gate_near)
    attn, up_near, gate_far = tie((attn, up_near, gate_far))
    up_traded = trade(up_near)
    *mixed, w_out_c = out_proj(ids, attn, w_out, w_out_far, chips)
    *mixed, cot = tie((*mixed, cot))
    parts = hops(mixed)
    cot_rows = exchange(copies(cot))
    *parts, gate_traded, up_far = tie((*parts, gate_traded, swap(up_near)))
    resid, normed = residual_norm(tokens, parts)
    z_blocks = hops([normed] * chips)
    weights = [
        [gate_near, gate_traded, gate_far, swap(gate_traded)],
        [up_near, up_traded, up_far, swap(up_traded)],
    ]
    inner, grad_gate, grad_up, normed_two, back = feed_forward(
        ids, z_blocks, cot_rows, weights, w_down_c
    )

    parts = exchange(back)
    down_near, down_far = row_grad(ids, inner, cot_rows, 4)
    down_far = swap(down_far)
    grad_gate, down_near = tie((grad_gate, down_near))
    gate_near, gate_far = weight_grad(ids, normed_two, grad_gate, chips)
    gate_near, gate_far, down_far, grad_up = tie((gate_near, gate_far, down_far, grad_up))
    gate_far = swap(gate_far)
    down = pair_sum(down_near, down_far)
    grad_up = visit(grad_up, new=("down", down, 0))
    up_near, up_far = weight_grad(ids, normed_two, grad_up, chips)
    up_near, up_far, parts = visit(up_near, up_far, parts, new=("down", down, 1))
    gate_part = exchange(pair_sum(gate_near, gate_far))
    up_far = swap(up_far)
    grad_resid, da, gain_two_local = residual_norm_back(cotangent, parts, resid, chips)
    da, inner = visit(da, inner, new=("down", down, 2))
    out = dot(inner, w_down_c).astype(BF16)
    up_part = pair_sum(up_near, up_far)
    out, up_part, gate_part = visit(out, up_part, gate_part, new=("down", down, 3))
    da = exchange(da)
    da, up_part = visit(da, up_part, new=("gate", gate_part, 0))
    up_part = exchange(up_part)
    dob = dot_nt(da, w_out_c).astype(BF16)
    out_near, out_far = row_grad(ids, attn, da, 2)
    dob, out_near, out_far = visit(dob, out_near, out_far, new=("gate", gate_part, 1))
    out_far = swap(out_far)
    dq, dkv = attention_backward(
        ids, doc_lengths, queries, kv_near, kv_far, sums, dob, cos_table, sin_table, rows
    )
    dq, dkv = visit(dq, dkv, new=("gate", gate_part, 2))
    dkv = dkv[:own] + swap(dkv[own:].astype(BF16)).astype(F32)
    half_turn = jnp.concatenate([dkv[:, HD // 2 : HD], dkv[:, : HD // 2]], axis=1)
    dk = dkv[:, :HD] * cos_table[:, :HD] - half_turn * sin_table[:, :HD]
    dqkv = jnp.concatenate([dq, dk.astype(BF16), dkv[:, HD:].astype(BF16)], axis=1)
    back = dot_nt(dqkv, w_qkv).astype(BF16)
    dqkv, back, up_part = visit(dqkv, back, up_part, new=("gate", gate_part, 3))
    parts = exchange(back)
    qkv_near, qkv_far = weight_grad(ids, normed_one, dqkv, chips)
    qkv_near, qkv_far = visit(qkv_near, qkv_far, new=("up", up_part, 0))
    qkv_part = pair_sum(qkv_near, swap(qkv_far))
    qkv_part, parts = visit(qkv_part, parts, new=("up", up_part, 1))
    qkv_part = exchange(qkv_part)
    _, grad_inputs, gain_one_local = residual_norm_back(grad_resid, parts, tokens, 1)
    gain_one_local = visit(gain_one_local, new=("up", up_part, 2))
    norms = jnp.concatenate([gain_one_local, gain_two_local], axis=0)
    norms = norms.reshape(2, chips, 2, wrows).transpose(2, 1, 0, 3)
    mine = lax.dynamic_index_in_dim(norms, core, 0, keepdims=False)
    other = lax.dynamic_index_in_dim(norms, 1 - core, 0, keepdims=False)
    mine = mine + swap(other)
    out_part = pair_sum(out_near, out_far)
    if reps == 4:
        grad_down = beside(ids, summed("down", 4), w_down.shape[0], model // 4)
        mine, grad_down = tie((mine, grad_down))
    mine, qkv_part, out_part = visit(mine, qkv_part, out_part, new=("up", up_part, 3))
    parts = exchange(out).reshape(chips, rows, model)
    norms = lax.dynamic_index_in_dim(mine, chip, 0, keepdims=False)
    for k in range(1, chips):
        norms = norms + hop(lax.dynamic_index_in_dim(mine, chip ^ k, 0, keepdims=False), k)
    qkv_part = qkv_part.reshape(2, -1, 128)
    norms = visit(norms, new=("qkv", qkv_part, 0))
    parts, norms = visit(parts, norms, new=("qkv", qkv_part, 1))
    result = (resid + jnp.sum(parts.astype(F32), axis=0)).astype(BF16)
    norms = norms.astype(BF16).reshape(-1, 128)
    norms = jnp.pad(norms, ((0, 256 - norms.shape[0]), (0, 0)))
    last = jnp.concatenate([out_part[1], norms], axis=0)[None]
    if reps == 4:
        grad_gate_out = beside(ids, summed("gate", 4), wrows, width, gain_two)
        last, grad_gate_out = visit(last, grad_gate_out, new=("out", out_part, 0))
    else:
        visit(new=("out", out_part, 0))
    visit(new=("last", last, 0))
    if reps != 4:
        for k in range(4, chips):
            visit(new=("gate", gate_part, k))
            visit(new=("up", up_part, k))
        grad_gate_out = beside(ids, summed("gate", chips), wrows, width, gain_two)
    while any(line.busy() for line in lines):
        visit()

    if reps != 4:
        grad_down = beside(ids, summed("down", 4), w_down.shape[0], model // 4)
    rows_of = wrows * pl.cdiv(qw + 2 * HD, 128)
    qkv = [
        (a[n : n + rows_of], b[n : n + rows_of])
        for a, b in summed("qkv", 2)
        for n in range(0, chips // 2 * rows_of, rows_of)
    ]
    last = sums_of["last0"]
    at = out_part.shape[1]
    norms = jnp.where(ends == 1, last[1], last[0])[at : at + 2 * wrows // 128]
    norms = norms.astype(F32).reshape(2, wrows)
    grad_query = beside(ids, qkv, wrows, qw, gain_one)
    kv_at = qw // 128 * wrows
    kv = [
        jnp.where(ends == 1, b[kv_at : kv_at + wrows], a[kv_at : kv_at + wrows]) for a, b in qkv
    ]
    kv = jnp.stack(kv).astype(F32).reshape(KVH, kv_share, wrows, 2, HD).sum(axis=1)
    kv = kv * gain_one[None, :, :, None]
    grad_key = kv[:, :, 0].transpose(1, 0, 2).reshape(wrows, KVH * HD)
    grad_value = kv[:, :, 1].transpose(1, 0, 2).reshape(wrows, KVH * HD)
    return (
        result,
        grad_inputs,
        norms[0] / gain_one[:, 0],
        grad_query,
        grad_key,
        grad_value,
        beside(ids, [sums_of["out0"], tuple(v[:at] for v in last)], wrows, model // 2),
        norms[1] / gain_two[:, 0],
        grad_gate_out,
        beside(ids, summed("up", chips), wrows, width, gain_two),
        grad_down,
    )


def solution(mesh):
    placed = (
        P(("rep", "fsdp"), None),
        P(("rep", "fsdp"), None),
        P(),
        P("fsdp"),
        P("fsdp", None),
        P("fsdp", None),
        P("fsdp", None),
        P("fsdp", None),
        P("fsdp"),
        P("fsdp", None),
        P("fsdp", None),
        P("fsdp", None),
    )
    return jax.shard_map(
        local,
        mesh=mesh,
        in_specs=placed,
        out_specs=(
            P(("rep", "fsdp"), None),
            P(("rep", "fsdp"), None),
            P("fsdp"),
            P("fsdp", None),
            P("fsdp", None),
            P("fsdp", None),
            P("fsdp", None),
            P("fsdp"),
            P("fsdp", None),
            P("fsdp", None),
            P("fsdp", None),
        ),
        check_vma=False,
    )
```

```python
import math

import jax
import jax.numpy as jnp
from jax import lax
from jax.experimental import pallas as pl
from jax.experimental.pallas import tpu as pltpu
from jax.sharding import PartitionSpec as P

H = 32
KVH = 4
HD = 64
DOCS = 8

NORM_EPS = 1e-05
ROPE_BASE = 10000.0
MASK_FILL = -1e30
TILE = 512
F32 = jnp.float32
BF16 = jnp.bfloat16


def dot(a, b):
    return jnp.dot(a, b, preferred_element_type=F32)


def dot_nt(a, b):
    return lax.dot_general(a, b, (((1,), (1,)), ((), ())), preferred_element_type=F32)


def dot_tn(a, b):
    return lax.dot_general(a, b, (((0,), (0,)), ((), ())), preferred_element_type=F32)


def tiny():
    return pl.CostEstimate(flops=1024, bytes_accessed=1024, transcendentals=0)


def whole():
    return pl.BlockSpec(memory_space=pltpu.VMEM)


def turned(v):
    low = lax.broadcasted_iota(jnp.int32, v.shape, 1) % HD < HD // 2
    return jnp.where(low, pltpu.roll(v, 128 - HD // 2, 1), pltpu.roll(v, HD // 2, 1))


def scalars():
    return pl.BlockSpec(memory_space=pltpu.SMEM)


def pick_qkv(w_query, w_key, w_value, gain, chips):
    rows, cols = w_query.shape
    qw, share = cols // chips, chips // KVH

    def body(g_ref, q_ref, k_ref, v_ref, out_ref):
        gain = g_ref[...]
        out_ref[0, :, :qw] = (q_ref[...].astype(F32) * gain).astype(BF16)
        for n in range(KVH):

            @pl.when(pl.program_id(0) // share == n)
            def _():
                at = slice(n * HD, (n + 1) * HD)
                kv = jnp.concatenate([k_ref[:, at], v_ref[:, at]], axis=1)
                out_ref[0, :, qw:] = (kv.astype(F32) * gain).astype(BF16)

    small = pl.BlockSpec((rows, KVH * HD), lambda k: (0, 0))
    return pl.pallas_call(
        body,
        grid=(chips,),
        in_specs=[
            pl.BlockSpec((rows, 1), lambda k: (0, 0)),
            pl.BlockSpec((rows, qw), lambda k: (0, k)),
            small,
            small,
        ],
        out_specs=pl.BlockSpec((1, rows, qw + 2 * HD), lambda k: (k, 0, 0)),
        out_shape=jax.ShapeDtypeStruct((chips, rows, qw + 2 * HD), BF16),
        cost_estimate=tiny(),
        name="pick_qkv",
    )(gain, w_query, w_key, w_value)


def pick_half(w_gate, w_up, gain, ids, count):
    rows, cols = w_gate.shape
    width, part = cols // count, rows // 2
    if width % 128:
        out = []
        for w in (w_gate, w_up):
            v = lax.dynamic_slice_in_dim((w.astype(F32) * gain).astype(BF16), ids[2] * part, part)
            out.append(v.reshape(part, count, width).transpose(1, 0, 2))
        return out

    def body(s_ref, n_ref, a_ref, b_ref, c_ref, d_ref):
        c_ref[0] = (a_ref[...].astype(F32) * n_ref[...]).astype(BF16)
        d_ref[0] = (b_ref[...].astype(F32) * n_ref[...]).astype(BF16)

    return pl.pallas_call(
        body,
        grid_spec=pltpu.PrefetchScalarGridSpec(
            num_scalar_prefetch=1,
            grid=(count,),
            in_specs=[pl.BlockSpec((part, 1), lambda k, s: (s[2], 0))]
            + [pl.BlockSpec((part, width), lambda k, s: (s[2], k))] * 2,
            out_specs=[pl.BlockSpec((1, part, width), lambda k, s: (k, 0, 0))] * 2,
        ),
        out_shape=[jax.ShapeDtypeStruct((count, part, width), BF16)] * 2,
        cost_estimate=tiny(),
        name="pick_half",
    )(ids, gain, w_gate, w_up)


def join_cores(ids, near, far):
    rows, cols = near.shape

    def body(s_ref, a_ref, b_ref, out_ref):
        @pl.when(pl.program_id(0) == 0)
        def _():
            out_ref[...] = a_ref[...]

        @pl.when(pl.program_id(0) == 1)
        def _():
            out_ref[...] = b_ref[...]

    return pl.pallas_call(
        body,
        grid_spec=pltpu.PrefetchScalarGridSpec(
            num_scalar_prefetch=1,
            grid=(2,),
            in_specs=[pl.BlockSpec((rows, cols), lambda f, s: (0, 0))] * 2,
            out_specs=pl.BlockSpec((rows, cols), lambda f, s: (s[1] ^ f, 0)),
        ),
        out_shape=jax.ShapeDtypeStruct((2 * rows, cols), near.dtype),
        cost_estimate=tiny(),
        name="join_cores",
    )(ids, near, far)


def qkv_kernel(ids, x_blocks, near, far, cos_table, sin_table):
    rows, model = x_blocks[0].shape
    chips = len(x_blocks)
    own = rows * chips
    wrows, width = near.shape[1:]
    qw = width - 2 * HD

    def body(c_ref, cos_ref, sin_ref, n_ref, f_ref, *refs):
        x_refs, (z_ref, q_ref, kv_ref, w_ref) = refs[:chips], refs[chips:]
        chip, core = c_ref[0], c_ref[1]
        for k in range(chips):
            at = pl.multiple_of((2 * k + core) * wrows, wrows)
            w_ref[pl.ds(at, wrows), :] = n_ref[k]
            at = pl.multiple_of((2 * k + 1 - core) * wrows, wrows)
            w_ref[pl.ds(at, wrows), :] = f_ref[k]
            x = x_refs[k][...].astype(F32)
            inv = lax.rsqrt(jnp.mean(x * x, axis=-1, keepdims=True) + NORM_EPS)
            at = pl.multiple_of((chip ^ k) * rows, rows)
            z_ref[pl.ds(at, rows), :] = (x * inv).astype(BF16)
        total = dot(z_ref[...], w_ref[...])
        cos, sin = cos_ref[...], sin_ref[...]
        for j in range(qw // 128):
            v = total[:, j * 128 : (j + 1) * 128]
            q_ref[:, j * 128 : (j + 1) * 128] = (v * cos + turned(v) * sin).astype(BF16)
        v = total[:, qw:]
        key = lax.broadcasted_iota(jnp.int32, v.shape, 1) < HD
        kv_ref[...] = jnp.where(key, v * cos + turned(v) * sin, v).astype(BF16)

    return pl.pallas_call(
        body,
        in_specs=[scalars()] + [whole()] * (4 + chips),
        out_specs=[whole()] * 4,
        out_shape=[
            jax.ShapeDtypeStruct((own, model), BF16),
            jax.ShapeDtypeStruct((own, qw), BF16),
            jax.ShapeDtypeStruct((own, 2 * HD), BF16),
            jax.ShapeDtypeStruct((2 * chips * wrows, width), BF16),
        ],
        cost_estimate=tiny(),
        name="qkv_forward",
    )(ids, cos_table, sin_table, near, far, *x_blocks)


def attention_mask(s_ref, l_ref, rows, block):
    core, rep, span = s_ref[1], s_ref[4], (block + 1) * rows

    def coded(pos):
        bound, code = 0, jnp.zeros(pos.shape, jnp.int32)
        for n in range(DOCS):
            bound = bound + l_ref[rep, n]
            code = code + jnp.where(pos >= bound, 1, 0)
        return jnp.where(code < DOCS - 1, code, 1000 + pos)

    q_pos = (2 * block + core) * rows + lax.broadcasted_iota(jnp.int32, (rows, 1), 0)
    index = lax.broadcasted_iota(jnp.int32, (1, 2 * span), 1)
    side = jnp.where(index < span, core, 1 - core)
    index = jnp.where(index < span, index, index - span)
    k_pos = (2 * (index // rows) + side) * rows + index % rows
    q_code = coded(q_pos)
    allowed = (coded(k_pos) == q_code) & (k_pos <= q_pos)
    return jnp.where(allowed, 0.0, MASK_FILL), jnp.where(q_code < DOCS, 1.0, 0.0)


def attention_forward(ids, lengths, q, kv_own, kv_other, rows, stack=4):
    own, qw = q.shape
    scale = 1.0 / math.sqrt(HD)
    heads = qw // HD
    stack = min(stack, heads)

    def body(s_ref, d_ref, q_ref, a_ref, b_ref, o_ref, l_ref):
        for block in range(own // rows):

            @pl.when(pl.program_id(0) == block)
            def _(block=block):
                span = (block + 1) * rows
                bias, valid = attention_mask(s_ref, d_ref, rows, block)
                lane = lax.broadcasted_iota(jnp.int32, (rows, 128), 1)
                sums = jnp.zeros((rows, 128), F32)
                keys = jnp.concatenate([a_ref[:span, :], b_ref[:span, :]], axis=0)
                k, v = keys[:, :HD], keys[:, HD:]
                for g in range(heads // stack):
                    qs = [q_ref[:, h * HD : (h + 1) * HD] for h in range(g * stack, (g + 1) * stack)]
                    qs = jnp.concatenate(qs, axis=0) * jnp.asarray(scale, BF16)
                    s = dot_nt(qs, k).reshape(stack, rows, 2 * span) + bias[None]
                    top = jnp.max(s, axis=-1, keepdims=True)
                    p = jnp.exp(s - top)
                    tot = jnp.sum(p, axis=-1, keepdims=True)
                    p = (p * (1.0 / tot)).astype(BF16).reshape(stack * rows, 2 * span)
                    o = dot(p, v).reshape(stack, rows, HD) * valid[None]
                    o = o.astype(BF16)
                    lse = top + jnp.log(tot)
                    for t in range(stack):
                        h = g * stack + t
                        sums = jnp.where(lane == h, lse[t], sums)
                        if t % 2:
                            pair = jnp.concatenate([o[t - 1], o[t]], axis=1)
                            o_ref[:, (h - 1) * HD : (h + 1) * HD] = pair
                l_ref[...] = sums

    blocked = lambda i: (i, 0)
    fixed = pl.BlockSpec((own, 2 * HD), lambda i: (0, 0))
    return pl.pallas_call(
        body,
        grid=(own // rows,),
        in_specs=[scalars(), scalars(), pl.BlockSpec((rows, qw), blocked), fixed, fixed],
        out_specs=[pl.BlockSpec((rows, qw), blocked), pl.BlockSpec((rows, 128), blocked)],
        out_shape=[
            jax.ShapeDtypeStruct((own, qw), BF16),
            jax.ShapeDtypeStruct((own, 128), F32),
        ],
        cost_estimate=tiny(),
        name="attention_forward",
    )(ids, lengths, q, kv_own, kv_other)


def attention_backward(
    ids, lengths, q, kv_own, kv_other, sums, d_out, cos_table, sin_table, rows, stack=4
):
    own, qw = q.shape
    scale = 1.0 / math.sqrt(HD)
    heads = qw // HD
    stack = min(stack, heads)
    blocks = own // rows

    def body(
        s_ref, n_ref, q_ref, a_ref, b_ref, l_ref, d_ref, cos_ref, sin_ref, dq_ref, dkv_ref,
    ):
        @pl.when(pl.program_id(0) == 0)
        def _():
            dkv_ref[...] = jnp.zeros_like(dkv_ref)

        for block in range(blocks):

            @pl.when(pl.program_id(0) == block)
            def _(block=block):
                span = (block + 1) * rows
                bias, valid = attention_mask(s_ref, n_ref, rows, block)
                valid = valid.astype(BF16)
                cos, sin = cos_ref[...], sin_ref[...]
                keys = jnp.concatenate([a_ref[:span, :], b_ref[:span, :]], axis=0)
                k, v = keys[:, :HD], keys[:, HD:]
                lane = lax.broadcasted_iota(jnp.int32, (rows, 128), 1)

                def some(g, carry):
                    at = pl.ds(pl.multiple_of(g * stack * HD, 128), stack * HD)
                    wide_q = q_ref[:, at] * jnp.asarray(scale, BF16)
                    wide_d = d_ref[:, at] * valid
                    qs = [wide_q[:, h * HD : (h + 1) * HD] for h in range(stack)]
                    qs = jnp.concatenate(qs, axis=0)
                    ds = [wide_d[:, h * HD : (h + 1) * HD] for h in range(stack)]
                    ds = jnp.concatenate(ds, axis=0)
                    lse = [jnp.where(lane == g * stack + t, l_ref[...], 0.0) for t in range(stack)]
                    lse = jnp.stack([jnp.sum(v, axis=-1, keepdims=True) for v in lse])
                    s = dot_nt(qs, k).reshape(stack, rows, 2 * span) + bias[None]
                    p = jnp.exp(s - lse)
                    dp = dot_nt(ds, v).reshape(stack, rows, 2 * span)
                    inner = jnp.sum(p * dp, axis=-1, keepdims=True)
                    grad = (p * (dp - inner)).astype(BF16).reshape(stack * rows, 2 * span)
                    p = p.astype(BF16).reshape(stack * rows, 2 * span)
                    dq = (dot(grad, k) * scale).reshape(stack, rows, HD)
                    both = jnp.concatenate([dot_tn(grad, qs), dot_tn(p, ds)], axis=1)
                    dkv_ref[:span, :] += both[:span]
                    dkv_ref[own : own + span, :] += both[span:]
                    for t in range(1, stack, 2):
                        w = jnp.concatenate([dq[t - 1], dq[t]], axis=1)
                        w = w * cos - turned(w) * sin
                        to = pl.ds(pl.multiple_of((g * stack + t - 1) * HD, 128), 2 * HD)
                        dq_ref[:, to] = w.astype(BF16)
                    return carry

                lax.fori_loop(0, heads // stack, some, 0)

    blocked = lambda i: (i, 0)
    fixed = pl.BlockSpec((own, 2 * HD), lambda i: (0, 0))
    table = pl.BlockSpec((rows, 128), blocked)
    wide = pl.BlockSpec((rows, qw), blocked)
    return pl.pallas_call(
        body,
        grid=(blocks,),
        in_specs=[scalars(), scalars(), wide, fixed, fixed, table, wide, table, table],
        out_specs=[wide, pl.BlockSpec((2 * own, 2 * HD), lambda i: (0, 0))],
        out_shape=[
            jax.ShapeDtypeStruct((own, qw), BF16),
            jax.ShapeDtypeStruct((2 * own, 2 * HD), F32),
        ],
        cost_estimate=tiny(),
        name="attention_backward",
    )(ids, lengths, q, kv_own, kv_other, sums, d_out, cos_table, sin_table)


def feed_forward(ids, z_blocks, cot, weights, w_down):
    rows, model = z_blocks[0].shape
    chips = len(z_blocks)
    part, width = weights[0][0].shape[1:]
    own, tile = rows * chips, min(TILE, width)
    turns = pl.cdiv(width, tile)

    def body(s_ref, *refs):
        z_refs, c_ref, w_refs = refs[:chips], refs[chips], refs[chips + 1 : chips + 9]
        d_ref, m_ref, dg_ref, du_ref, z_ref = refs[chips + 9 : chips + 14]
        b_refs, (w_ref, acc_ref) = refs[chips + 14 : -2], refs[-2:]
        chip, core, half = s_ref[0], s_ref[1], s_ref[2]
        turn = pl.program_id(0)

        @pl.when(turn == 0)
        def _():
            for k in range(chips):
                at = pl.multiple_of((chip ^ k) * rows, rows)
                z_ref[pl.ds(at, rows), :] = z_refs[k][...]
            acc_ref[...] = jnp.zeros_like(acc_ref)

        def work(cols, last):
            for m in range(2):
                for i in range(4):
                    side = core if i < 2 else 1 - core
                    piece = half if i % 2 == 0 else 1 - half
                    for j in range(chips):
                        at = pl.multiple_of((2 * (2 * j + side) + piece) * part, part)
                        w_ref[m, pl.ds(at, part), :cols] = w_refs[4 * m + i][j, :, :cols]
            gate = dot(z_ref[...], w_ref[0, :, :cols])
            up = dot(z_ref[...], w_ref[1, :, :cols])
            dm = dot_nt(c_ref[...], d_ref[:cols, :])
            sig = 1.0 / (1.0 + jnp.exp(-gate))
            silu = gate * sig
            m_ref[:, :cols] = (silu * up).astype(BF16)
            dg = (dm * up * sig * (1.0 + gate * (1.0 - sig))).astype(BF16)
            du = (dm * silu).astype(BF16)
            dg_ref[:, :cols] = dg
            du_ref[:, :cols] = du
            back = dot_nt(dg, w_ref[0, :, :cols]) + dot_nt(du, w_ref[1, :, :cols])
            back = back + acc_ref[...]
            acc_ref[...] = back
            if last:
                for k in range(chips):
                    at = pl.multiple_of((chip ^ k) * rows, rows)
                    b_refs[k][...] = acc_ref[pl.ds(at, rows), :].astype(BF16)

        if turns > 1:

            @pl.when(turn < turns - 1)
            def _():
                work(tile, False)

        @pl.when(turn == turns - 1)
        def _():
            work(width - (turns - 1) * tile, True)

    joined = pl.BlockSpec((own, model), lambda n, s: (0, 0))
    out_tile = pl.BlockSpec((own, tile), lambda n, s: (0, n))
    return pl.pallas_call(
        body,
        grid_spec=pltpu.PrefetchScalarGridSpec(
            num_scalar_prefetch=1,
            grid=(turns,),
            in_specs=[pl.BlockSpec((rows, model), lambda n, s: (0, 0))] * chips
            + [joined]
            + [pl.BlockSpec((chips, part, tile), lambda n, s: (0, 0, n))] * 8
            + [pl.BlockSpec((tile, model), lambda n, s: (n, 0))],
            out_specs=[out_tile] * 3
            + [joined]
            + [pl.BlockSpec((rows, model), lambda n, s: (0, 0))] * chips,
            scratch_shapes=[
                pltpu.VMEM((2, model, tile), BF16),
                pltpu.VMEM((own, model), F32),
            ],
        ),
        out_shape=[jax.ShapeDtypeStruct((own, width), BF16)] * 3
        + [jax.ShapeDtypeStruct((own, model), BF16)]
        + [jax.ShapeDtypeStruct((rows, model), BF16)] * chips,
        cost_estimate=tiny(),
        name="feed_forward",
    )(ids, *z_blocks, cot, *weights[0], *weights[1], w_down)


def out_proj(ids, attn, near, far, chips):
    own, depth = attn.shape
    wrows, model = near.shape
    rows = own // chips

    def body(c_ref, a_ref, n_ref, f_ref, *outs):
        chip, core, w_ref = c_ref[0], c_ref[1], outs[-1]
        w_ref[pl.ds(pl.multiple_of(core * wrows, wrows), wrows), :] = n_ref[...]
        w_ref[pl.ds(pl.multiple_of((1 - core) * wrows, wrows), wrows), :] = f_ref[...]
        for k in range(chips):
            at = pl.multiple_of((chip ^ k) * rows, rows)
            outs[k][...] = dot(a_ref[pl.ds(at, rows), :], w_ref[...]).astype(BF16)

    return pl.pallas_call(
        body,
        in_specs=[scalars()] + [whole()] * 3,
        out_specs=[whole()] * (chips + 1),
        out_shape=[jax.ShapeDtypeStruct((rows, model), BF16)] * chips
        + [jax.ShapeDtypeStruct((depth, model), BF16)],
        cost_estimate=tiny(),
        name="out_proj",
    )(ids, attn, near, far)


def residual_norm(tokens, parts):
    rows, model = tokens.shape

    def body(x_ref, *refs):
        y_ref, z_ref = refs[-2:]
        y = x_ref[...].astype(F32)
        for p in refs[:-2]:
            y = y + p[...].astype(F32)
        y_ref[...] = y
        inv = lax.rsqrt(jnp.mean(y * y, axis=-1, keepdims=True) + NORM_EPS)
        z_ref[...] = (y * inv).astype(BF16)

    return pl.pallas_call(
        body,
        in_specs=[whole()] * (1 + len(parts)),
        out_specs=[whole()] * 2,
        out_shape=[
            jax.ShapeDtypeStruct((rows, model), F32),
            jax.ShapeDtypeStruct((rows, model), BF16),
        ],
        cost_estimate=tiny(),
        name="residual_norm",
    )(tokens, *parts)


def residual_norm_back(base, parts, y, copies):
    rows, model = y.shape
    parts = parts if isinstance(parts, (list, tuple)) else [parts]

    def body(b_ref, y_ref, *refs):
        p_refs, (f_ref, l_ref, n_ref) = refs[:-3], refs[-3:]
        e = 0.0
        for p_ref in p_refs:
            for i in range(p_ref.shape[0] // rows):
                e = e + p_ref[i * rows : (i + 1) * rows, :].astype(F32)
        v = y_ref[...].astype(F32)
        inv = lax.rsqrt(jnp.mean(v * v, axis=-1, keepdims=True) + NORM_EPS)
        z = v * inv
        ez = e * z
        n_ref[...] = jnp.sum(ez, axis=0, keepdims=True)
        out = b_ref[...].astype(F32) + inv * (e - z * jnp.mean(ez, axis=-1, keepdims=True))
        f_ref[...] = out
        for i in range(copies):
            l_ref[i * rows : (i + 1) * rows, :] = out.astype(BF16)

    return pl.pallas_call(
        body,
        in_specs=[whole()] * (2 + len(parts)),
        out_specs=[whole()] * 3,
        out_shape=[
            jax.ShapeDtypeStruct((rows, model), F32),
            jax.ShapeDtypeStruct((copies * rows, model), BF16),
            jax.ShapeDtypeStruct((1, model), F32),
        ],
        cost_estimate=tiny(),
        name="residual_norm_back",
    )(base, y, *parts)


def strips(value, ref, lead=()):
    rows, width = value.shape
    for t in range(pl.cdiv(width, 128)):
        v = value[:, t * 128 : (t + 1) * 128]
        if v.shape[1] < 128:
            v = jnp.concatenate([v, jnp.zeros((rows, 128 - v.shape[1]), v.dtype)], axis=1)
        ref[(*lead, slice(t * rows, (t + 1) * rows), slice(None))] = v


def weight_grad(ids, left, right, chips):
    own, model = left.shape
    width = right.shape[1]
    rows = model // (2 * chips)
    long = pl.cdiv(width, 128) * rows
    group = min(2, chips)
    turns = chips // group

    def body(c_ref, l_ref, r_ref, near_ref, far_ref):
        step = pl.program_id(0)
        near = step >= turns
        side = jnp.where(near, c_ref[1], 1 - c_ref[1])
        first = jnp.where(near, step - turns, step) * group
        blocks = []
        for j in range(group):
            at = pl.multiple_of((2 * (first + j) + side) * rows, rows)
            blocks.append(l_ref[:, pl.ds(at, rows)])
        out = dot_tn(jnp.concatenate(blocks, axis=1), r_ref[...]).astype(BF16)

        @pl.when(near)
        def _():
            for j in range(group):
                strips(out[j * rows : (j + 1) * rows], near_ref, (j,))

        @pl.when(step < turns)
        def _():
            for j in range(group):
                strips(out[j * rows : (j + 1) * rows], far_ref, (j,))

    return pl.pallas_call(
        body,
        grid_spec=pltpu.PrefetchScalarGridSpec(
            num_scalar_prefetch=1,
            grid=(2 * turns,),
            in_specs=[
                pl.BlockSpec((own, model), lambda t, c: (0, 0)),
                pl.BlockSpec((own, width), lambda t, c: (0, 0)),
            ],
            out_specs=[
                pl.BlockSpec((group, long, 128), lambda t, c: (jnp.maximum(t - turns, 0), 0, 0)),
                pl.BlockSpec((group, long, 128), lambda t, c: (jnp.minimum(t, turns - 1), 0, 0)),
            ],
        ),
        out_shape=[jax.ShapeDtypeStruct((chips, long, 128), BF16)] * 2,
        cost_estimate=tiny(),
        name="weight_grad",
    )(ids, left, right)


def row_grad(ids, left, right, cuts):
    own, depth = left.shape
    model = right.shape[1]
    rows, width = depth // 2, model // cuts
    long = width // 128 * rows

    def body(c_ref, l_ref, r_ref, near_ref, far_ref, full_ref):
        core = c_ref[1]
        full_ref[...] = dot_tn(l_ref[...], r_ref[...]).astype(BF16)
        near = full_ref[pl.ds(pl.multiple_of(core * rows, 16), rows), :]
        far = full_ref[pl.ds(pl.multiple_of((1 - core) * rows, 16), rows), :]
        strips(near, near_ref, (0,))
        strips(far, far_ref, (0,))

    out = pl.BlockSpec((1, long, 128), lambda n, c: (n, 0, 0))
    return pl.pallas_call(
        body,
        grid_spec=pltpu.PrefetchScalarGridSpec(
            num_scalar_prefetch=1,
            grid=(cuts,),
            in_specs=[
                pl.BlockSpec((own, depth), lambda n, c: (0, 0)),
                pl.BlockSpec((own, width), lambda n, c: (0, n)),
            ],
            out_specs=[out] * 2,
            scratch_shapes=[pltpu.VMEM((depth, width), BF16)],
        ),
        out_shape=[jax.ShapeDtypeStruct((cuts, long, 128), BF16)] * 2,
        cost_estimate=tiny(),
        name="row_grad",
    )(ids, left, right)


def chain_step(ids, own, outer, sent, inner, coming):
    def size(v):
        return 0 if v is None else v[0].shape[1] if isinstance(v, tuple) else v.shape[0]

    ins = [own, outer if own is not None else None, sent, inner, coming]
    have = [v is not None for v in ins]
    sizes = [size(own), max(size(sent), size(coming))]

    def body(s_ref, *refs):
        refs = list(refs)
        o_ref, x_ref, i_ref, y_ref, c_ref = [refs.pop(0) if h else None for h in have]
        s_out, a_out = [refs.pop(0) if n else None for n in sizes]
        ends = s_ref[3] == 1

        def each(count, work):
            step = math.gcd(512, count)

            def turn(n, carry):
                work(pl.ds(pl.multiple_of(n * step, step), step))
                return carry

            lax.fori_loop(0, count // step, turn, 0)

        if s_out is not None:

            def add_own(at):
                s_out[at, :] = o_ref[at, :] + x_ref[at, :]

            each(size(own), add_own)
        if c_ref is not None:

            @pl.when(ends)
            def _():
                def copy(at):
                    a_out[at, :] = c_ref[at, :]

                each(size(coming), copy)

        if i_ref is not None:

            @pl.when(jnp.logical_not(ends))
            def _():
                def add_sent(at):
                    a_out[at, :] = i_ref[at, :] + y_ref[at, :]

                each(size(sent), add_sent)

    def spec(v):
        if not isinstance(v, tuple):
            return pl.BlockSpec(v.shape, lambda i: (0, 0))
        block = v[1]
        return pl.BlockSpec((pl.Squeezed(), *v[0].shape[1:]), lambda i: (block, 0, 0))

    outs = pl.pallas_call(
        body,
        grid=(1,),
        in_specs=[scalars()] + [spec(v) for v in ins if v is not None],
        out_specs=[pl.BlockSpec((n, 128), lambda i: (0, 0)) for n in sizes if n],
        out_shape=[jax.ShapeDtypeStruct((n, 128), BF16) for n in sizes if n],
        cost_estimate=tiny(),
        name="chain_step",
    )(ids, *[v[0] if isinstance(v, tuple) else v for v in ins if v is not None])
    outs = list(outs)
    return [outs.pop(0) if n else None for n in sizes]


def beside(ids, blocks, rows, width, scale=None):
    count = len(blocks)
    tiles = pl.cdiv(width, 128)
    long = tiles * rows
    if scale is None:
        scale = jnp.ones((rows, 1), F32)
    if width % 128:
        full = [
            a[:long].reshape(tiles, rows, 128).transpose(1, 0, 2).reshape(rows, -1)
            for a, b in blocks
        ]
        return jnp.concatenate([f[:, :width] for f in full], axis=1).astype(F32) * scale

    def body(c_ref, s_ref, *refs):
        scale, out_ref = s_ref[...], refs[-1]
        for k in range(count):
            for end in (0, 1):

                @pl.when((pl.program_id(0) == k) & (c_ref[3] == end))
                def _(ref=refs[2 * k + end]):
                    for t in range(tiles):
                        v = ref[t * rows : (t + 1) * rows, :].astype(F32)
                        out_ref[:, t * 128 : (t + 1) * 128] = v * scale

    return pl.pallas_call(
        body,
        grid_spec=pltpu.PrefetchScalarGridSpec(
            num_scalar_prefetch=1,
            grid=(count,),
            in_specs=[pl.BlockSpec((rows, 1), lambda k, c: (0, 0))]
            + [pl.BlockSpec((long, 128), lambda k, c: (0, 0))] * (2 * count),
            out_specs=pl.BlockSpec((rows, width), lambda k, c: (0, k)),
        ),
        out_shape=jax.ShapeDtypeStruct((rows, count * width), F32),
        cost_estimate=tiny(),
        name="beside",
    )(ids, scale, *[v for pair in blocks for v in pair])


def pair_sum(near, far):
    count, rows, lanes = near.shape

    def body(a_ref, b_ref, out_ref):
        out_ref[...] = a_ref[...] + b_ref[...]

    spec = pl.BlockSpec((2, rows, lanes), lambda k: (k, 0, 0))
    return pl.pallas_call(
        body,
        grid=(count // 2,),
        in_specs=[spec] * 2,
        out_specs=spec,
        out_shape=jax.ShapeDtypeStruct(near.shape, BF16),
        cost_estimate=tiny(),
        name="pair_sum",
    )(near, far)


def local(
    tokens,
    cotangent,
    doc_lengths,
    norm1_gain,
    w_query,
    w_key,
    w_value,
    w_out,
    norm2_gain,
    w_gate,
    w_up,
    w_down,
):
    rows, model = tokens.shape
    group = lax.axis_size("fsdp")
    reps = lax.axis_size("rep")
    chips = group // 2
    dev = lax.axis_index("fsdp").astype(jnp.int32)
    rep = lax.axis_index("rep").astype(jnp.int32)
    chip, core, half = dev >> 1, dev & 1, rep & 1
    ends = jnp.where((rep == 0) | (rep == reps - 1), 1, 0).astype(jnp.int32)
    ids = jnp.stack([chip, core, half, ends, rep])
    seq_len = rows * group
    own = rows * chips
    wrows = w_query.shape[0]
    width = w_gate.shape[1] // chips
    kv_share = chips // KVH
    qw = H // chips * HD
    tie = lax.optimization_barrier
    sides = [[2 * k + c for k in range(chips)] for c in range(2)]

    def exchange(v):
        return lax.all_to_all(v, "fsdp", 0, 0, axis_index_groups=sides, tiled=True)

    def hop(v, k):
        return lax.ppermute(v, "fsdp", [(i, i ^ (2 * k)) for i in range(group)])

    def hops(blocks):
        return [blocks[0]] + [hop(blocks[k], k) for k in range(1, chips)]

    def swap(v):
        return lax.ppermute(v, "fsdp", [(i, i ^ 1) for i in range(group)])

    def trade(v):
        return lax.ppermute(v, "rep", [(i, i ^ 1) for i in range(reps)])

    def copies(v):
        return jnp.broadcast_to(v[None], (chips,) + v.shape).reshape(chips * v.shape[0], -1)

    sums_of = {}
    outer_pairs = [(0, 1), (1, 0), (2, 3), (3, 2)]

    class Line:
        def __init__(self):
            self.own = self.sent = self.total = self.outer = self.inner = None

        def busy(self):
            return any(v is not None for v in (self.own, self.sent, self.total))

    lines = [Line(), Line()]
    turn = [0]

    def visit(*carry, new=None):
        if reps != 4:
            if new is not None:
                value = lax.psum(new[1][new[2]], "rep")
                sums_of[f"{new[0]}{new[2]}"] = (value, value)
            return carry if len(carry) != 1 else carry[0]
        line = lines[turn[0] % 2]
        turn[0] += 1
        extra = [line.outer, line.inner, None if new is None else new[1]]
        tied = tie(tuple(carry) + tuple(v for v in extra if v is not None))
        carry, tied = tied[: len(carry)], list(tied[len(carry) :])
        outer, inner, coming = [None if v is None else tied.pop(0) for v in extra]
        coming = None if new is None else (coming, new[2])
        value = lambda pair: None if pair is None else pair[1]
        if line.total is not None:
            sums_of[line.total[0]] = (line.total[1], outer)
        own_sum = ahead = None
        if outer is None:
            ahead = None if coming is None else coming[0][coming[1]]
        elif line.own is not None or line.sent is not None or coming is not None:
            own_sum, ahead = chain_step(
                ids, value(line.own), outer, value(line.sent), inner, coming
            )
        line.total = None if line.sent is None else (line.sent[0], ahead)
        line.sent = None if line.own is None else (line.own[0], own_sum)
        line.own = None if coming is None else (f"{new[0]}{new[2]}", coming)
        line.outer = None if ahead is None else lax.ppermute(ahead, "rep", outer_pairs)
        line.inner = (
            None if line.sent is None else lax.ppermute(line.sent[1], "rep", [(1, 2), (2, 1)])
        )
        return carry if len(carry) != 1 else carry[0]

    def summed(name, count):
        return [sums_of[f"{name}{k}"] for k in range(count)]

    starts = 2 * rows * jnp.arange(chips, dtype=jnp.int32) + core * rows
    own_pos = (starts[:, None] + jnp.arange(rows, dtype=jnp.int32)[None, :]).reshape(own)
    lane = jnp.arange(128)
    inverse = jnp.exp(-math.log(ROPE_BASE) / (HD // 2) * (lane % (HD // 2)).astype(F32))
    angles = own_pos.astype(F32)[:, None] * inverse[None, :]
    cos_table = jnp.cos(angles)
    sin_table = jnp.sin(angles) * jnp.where(lane % HD < HD // 2, -1.0, 1.0)[None, :]

    gain_one = norm1_gain.astype(F32)[:, None]
    gain_two = norm2_gain.astype(F32)[:, None]
    x_blocks = hops([tokens] * chips)
    qkv_near = exchange(pick_qkv(w_query, w_key, w_value, gain_one, chips))
    gate_part, up_part = pick_half(w_gate, w_up, gain_two, ids, chips)
    w_out_far = swap(w_out)
    w_down_c = join_cores(ids, w_down, swap(w_down))
    *x_blocks, cos_table, sin_table, gate_part, up_part, w_out_far, w_down_c = tie(
        (*x_blocks, cos_table, sin_table, gate_part, up_part, w_out_far, w_down_c)
    )
    gate_near = exchange(gate_part)
    normed_one, queries, kv_near, w_qkv = qkv_kernel(
        ids, x_blocks, qkv_near, swap(qkv_near), cos_table, sin_table
    )
    queries, gate_near, up_part, cot = tie((queries, gate_near, up_part, cotangent))
    up_near = exchange(up_part)
    gate_traded = trade(gate_near)
    kv_far = swap(kv_near)
    attn, sums = attention_forward(ids, doc_lengths, queries, kv_near, kv_far, rows)
    gate_far = swap(gate_near)
    attn, up_near, gate_far = tie((attn, up_near, gate_far))
    up_traded = trade(up_near)
    *mixed, w_out_c = out_proj(ids, attn, w_out, w_out_far, chips)
    *mixed, cot = tie((*mixed, cot))
    parts = hops(mixed)
    cot_rows = exchange(copies(cot))
    *parts, gate_traded, up_far = tie((*parts, gate_traded, swap(up_near)))
    resid, normed = residual_norm(tokens, parts)
    z_blocks = hops([normed] * chips)
    weights = [
        [gate_near, gate_traded, gate_far, swap(gate_traded)],
        [up_near, up_traded, up_far, swap(up_traded)],
    ]
    inner, grad_gate, grad_up, normed_two, *back = feed_forward(
        ids, z_blocks, cot_rows, weights, w_down_c
    )

    parts = hops(back)
    down_near, down_far = row_grad(ids, inner, cot_rows, 4)
    down_far = swap(down_far)
    grad_gate, down_near = tie((grad_gate, down_near))
    gate_near, gate_far = weight_grad(ids, normed_two, grad_gate, chips)
    gate_near, gate_far, down_far, grad_up, *parts = tie(
        (gate_near, gate_far, down_far, grad_up, *parts)
    )
    gate_far = swap(gate_far)
    down = pair_sum(down_near, down_far)
    grad_up = visit(grad_up, new=("down", down, 0))
    up_near, up_far = weight_grad(ids, normed_two, grad_up, chips)
    up_near, up_far, *parts = visit(up_near, up_far, *parts, new=("down", down, 1))
    gate_part = exchange(pair_sum(gate_near, gate_far))
    up_far = swap(up_far)
    grad_resid, da, gain_two_local = residual_norm_back(cotangent, parts, resid, chips)
    da, inner = visit(da, inner, new=("down", down, 2))
    out = dot(inner, w_down_c).astype(BF16)
    up_part = pair_sum(up_near, up_far)
    out, up_part, gate_part = visit(out, up_part, gate_part, new=("down", down, 3))
    da = exchange(da)
    da, up_part = visit(da, up_part, new=("gate", gate_part, 0))
    up_part = exchange(up_part)
    dob = dot_nt(da, w_out_c).astype(BF16)
    out_near, out_far = row_grad(ids, attn, da, 2)
    dob, out_near, out_far = visit(dob, out_near, out_far, new=("gate", gate_part, 1))
    out_far = swap(out_far)
    dq, dkv = attention_backward(
        ids, doc_lengths, queries, kv_near, kv_far, sums, dob, cos_table, sin_table, rows
    )
    dq, dkv = visit(dq, dkv, new=("gate", gate_part, 2))
    dkv = dkv[:own] + swap(dkv[own:].astype(BF16)).astype(F32)
    half_turn = jnp.concatenate([dkv[:, HD // 2 : HD], dkv[:, : HD // 2]], axis=1)
    dk = dkv[:, :HD] * cos_table[:, :HD] - half_turn * sin_table[:, :HD]
    dqkv = jnp.concatenate([dq, dk.astype(BF16), dkv[:, HD:].astype(BF16)], axis=1)
    back = dot_nt(dqkv, w_qkv).astype(BF16)
    dqkv, back, up_part = visit(dqkv, back, up_part, new=("gate", gate_part, 3))
    parts = exchange(back)
    qkv_near, qkv_far = weight_grad(ids, normed_one, dqkv, chips)
    qkv_near, qkv_far = visit(qkv_near, qkv_far, new=("up", up_part, 0))
    qkv_part = pair_sum(qkv_near, swap(qkv_far))
    qkv_part, parts = visit(qkv_part, parts, new=("up", up_part, 1))
    qkv_part = exchange(qkv_part)
    _, grad_inputs, gain_one_local = residual_norm_back(grad_resid, parts, tokens, 1)
    gain_one_local = visit(gain_one_local, new=("up", up_part, 2))
    norms = jnp.concatenate([gain_one_local, gain_two_local], axis=0)
    norms = norms.reshape(2, chips, 2, wrows).transpose(2, 1, 0, 3)
    mine = lax.dynamic_index_in_dim(norms, core, 0, keepdims=False)
    other = lax.dynamic_index_in_dim(norms, 1 - core, 0, keepdims=False)
    mine = mine + swap(other)
    out_part = pair_sum(out_near, out_far)
    if reps == 4:
        grad_down = beside(ids, summed("down", 4), w_down.shape[0], model // 4)
        mine, grad_down = tie((mine, grad_down))
    mine, qkv_part, out_part = visit(mine, qkv_part, out_part, new=("up", up_part, 3))
    parts = exchange(out).reshape(chips, rows, model)
    norms = lax.dynamic_index_in_dim(mine, chip, 0, keepdims=False)
    for k in range(1, chips):
        norms = norms + hop(lax.dynamic_index_in_dim(mine, chip ^ k, 0, keepdims=False), k)
    qkv_part = qkv_part.reshape(2, -1, 128)
    norms = visit(norms, new=("qkv", qkv_part, 0))
    parts, norms = visit(parts, norms, new=("qkv", qkv_part, 1))
    result = (resid + jnp.sum(parts.astype(F32), axis=0)).astype(BF16)
    norms = norms.astype(BF16).reshape(-1, 128)
    norms = jnp.pad(norms, ((0, 256 - norms.shape[0]), (0, 0)))
    last = jnp.concatenate([out_part[1], norms], axis=0)[None]
    if reps == 4:
        grad_gate_out = beside(ids, summed("gate", 4), wrows, width, gain_two)
        last, grad_gate_out = visit(last, grad_gate_out, new=("out", out_part, 0))
    else:
        visit(new=("out", out_part, 0))
    visit(new=("last", last, 0))
    if reps != 4:
        for k in range(4, chips):
            visit(new=("gate", gate_part, k))
            visit(new=("up", up_part, k))
        grad_gate_out = beside(ids, summed("gate", chips), wrows, width, gain_two)
    while any(line.busy() for line in lines):
        visit()

    if reps != 4:
        grad_down = beside(ids, summed("down", 4), w_down.shape[0], model // 4)
    rows_of = wrows * pl.cdiv(qw + 2 * HD, 128)
    qkv = [
        (a[n : n + rows_of], b[n : n + rows_of])
        for a, b in summed("qkv", 2)
        for n in range(0, chips // 2 * rows_of, rows_of)
    ]
    last = sums_of["last0"]
    at = out_part.shape[1]
    norms = jnp.where(ends == 1, last[1], last[0])[at : at + 2 * wrows // 128]
    norms = norms.astype(F32).reshape(2, wrows)
    grad_query = beside(ids, qkv, wrows, qw, gain_one)
    kv_at = qw // 128 * wrows
    kv = [
        jnp.where(ends == 1, b[kv_at : kv_at + wrows], a[kv_at : kv_at + wrows]) for a, b in qkv
    ]
    kv = jnp.stack(kv).astype(F32).reshape(KVH, kv_share, wrows, 2, HD).sum(axis=1)
    kv = kv * gain_one[None, :, :, None]
    grad_key = kv[:, :, 0].transpose(1, 0, 2).reshape(wrows, KVH * HD)
    grad_value = kv[:, :, 1].transpose(1, 0, 2).reshape(wrows, KVH * HD)
    return (
        result,
        grad_inputs,
        norms[0] / gain_one[:, 0],
        grad_query,
        grad_key,
        grad_value,
        beside(ids, [sums_of["out0"], tuple(v[:at] for v in last)], wrows, model // 2),
        norms[1] / gain_two[:, 0],
        grad_gate_out,
        beside(ids, summed("up", chips), wrows, width, gain_two),
        grad_down,
    )


def solution(mesh):
    placed = (
        P(("rep", "fsdp"), None),
        P(("rep", "fsdp"), None),
        P(),
        P("fsdp"),
        P("fsdp", None),
        P("fsdp", None),
        P("fsdp", None),
        P("fsdp", None),
        P("fsdp"),
        P("fsdp", None),
        P("fsdp", None),
        P("fsdp", None),
    )
    return jax.shard_map(
        local,
        mesh=mesh,
        in_specs=placed,
        out_specs=(
            P(("rep", "fsdp"), None),
            P(("rep", "fsdp"), None),
            P("fsdp"),
            P("fsdp", None),
            P("fsdp", None),
            P("fsdp", None),
            P("fsdp", None),
            P("fsdp"),
            P("fsdp", None),
            P("fsdp", None),
            P("fsdp", None),
        ),
        check_vma=False,
    )
```

```python
import math

import jax
import jax.numpy as jnp
from jax import lax
from jax.experimental import pallas as pl
from jax.experimental.pallas import tpu as pltpu
from jax.sharding import PartitionSpec as P

H = 32
KVH = 4
HD = 64
DOCS = 8

NORM_EPS = 1e-05
ROPE_BASE = 10000.0
MASK_FILL = -1e30
TILE = 512
F32 = jnp.float32
BF16 = jnp.bfloat16


def dot(a, b):
    return jnp.dot(a, b, preferred_element_type=F32)


def dot_nt(a, b):
    return lax.dot_general(a, b, (((1,), (1,)), ((), ())), preferred_element_type=F32)


def dot_tn(a, b):
    return lax.dot_general(a, b, (((0,), (0,)), ((), ())), preferred_element_type=F32)


def tiny():
    return pl.CostEstimate(flops=1024, bytes_accessed=1024, transcendentals=0)


def whole():
    return pl.BlockSpec(memory_space=pltpu.VMEM)


def turned(v):
    low = lax.broadcasted_iota(jnp.int32, v.shape, 1) % HD < HD // 2
    return jnp.where(low, pltpu.roll(v, 128 - HD // 2, 1), pltpu.roll(v, HD // 2, 1))


def scalars():
    return pl.BlockSpec(memory_space=pltpu.SMEM)


def pick_qkv(w_query, w_key, w_value, gain, chips):
    rows, cols = w_query.shape
    qw, share = cols // chips, chips // KVH

    def body(g_ref, q_ref, k_ref, v_ref, out_ref):
        gain = g_ref[...]
        out_ref[0, :, :qw] = (q_ref[...].astype(F32) * gain).astype(BF16)
        for n in range(KVH):

            @pl.when(pl.program_id(0) // share == n)
            def _():
                at = slice(n * HD, (n + 1) * HD)
                kv = jnp.concatenate([k_ref[:, at], v_ref[:, at]], axis=1)
                out_ref[0, :, qw:] = (kv.astype(F32) * gain).astype(BF16)

    small = pl.BlockSpec((rows, KVH * HD), lambda k: (0, 0))
    return pl.pallas_call(
        body,
        grid=(chips,),
        in_specs=[
            pl.BlockSpec((rows, 1), lambda k: (0, 0)),
            pl.BlockSpec((rows, qw), lambda k: (0, k)),
            small,
            small,
        ],
        out_specs=pl.BlockSpec((1, rows, qw + 2 * HD), lambda k: (k, 0, 0)),
        out_shape=jax.ShapeDtypeStruct((chips, rows, qw + 2 * HD), BF16),
        cost_estimate=tiny(),
        name="pick_qkv",
    )(gain, w_query, w_key, w_value)


def pick_half(w_gate, w_up, gain, ids, count):
    rows, cols = w_gate.shape
    width, part = cols // count, rows // 2
    if width % 128:
        out = []
        for w in (w_gate, w_up):
            v = lax.dynamic_slice_in_dim((w.astype(F32) * gain).astype(BF16), ids[2] * part, part)
            out.append(v.reshape(part, count, width).transpose(1, 0, 2))
        return out

    def body(s_ref, n_ref, a_ref, b_ref, c_ref, d_ref):
        c_ref[0] = (a_ref[...].astype(F32) * n_ref[...]).astype(BF16)
        d_ref[0] = (b_ref[...].astype(F32) * n_ref[...]).astype(BF16)

    return pl.pallas_call(
        body,
        grid_spec=pltpu.PrefetchScalarGridSpec(
            num_scalar_prefetch=1,
            grid=(count,),
            in_specs=[pl.BlockSpec((part, 1), lambda k, s: (s[2], 0))]
            + [pl.BlockSpec((part, width), lambda k, s: (s[2], k))] * 2,
            out_specs=[pl.BlockSpec((1, part, width), lambda k, s: (k, 0, 0))] * 2,
        ),
        out_shape=[jax.ShapeDtypeStruct((count, part, width), BF16)] * 2,
        cost_estimate=tiny(),
        name="pick_half",
    )(ids, gain, w_gate, w_up)


def join_cores(ids, near, far):
    rows, cols = near.shape

    def body(s_ref, a_ref, b_ref, out_ref):
        @pl.when(pl.program_id(0) == 0)
        def _():
            out_ref[...] = a_ref[...]

        @pl.when(pl.program_id(0) == 1)
        def _():
            out_ref[...] = b_ref[...]

    return pl.pallas_call(
        body,
        grid_spec=pltpu.PrefetchScalarGridSpec(
            num_scalar_prefetch=1,
            grid=(2,),
            in_specs=[pl.BlockSpec((rows, cols), lambda f, s: (0, 0))] * 2,
            out_specs=pl.BlockSpec((rows, cols), lambda f, s: (s[1] ^ f, 0)),
        ),
        out_shape=jax.ShapeDtypeStruct((2 * rows, cols), near.dtype),
        cost_estimate=tiny(),
        name="join_cores",
    )(ids, near, far)


def qkv_kernel(ids, x_blocks, near, far, cos_table, sin_table):
    rows, model = x_blocks[0].shape
    chips = len(x_blocks)
    own = rows * chips
    wrows, width = near.shape[1:]
    qw = width - 2 * HD

    def body(c_ref, cos_ref, sin_ref, n_ref, f_ref, *refs):
        x_refs, (z_ref, q_ref, kv_ref, w_ref) = refs[:chips], refs[chips:]
        chip, core = c_ref[0], c_ref[1]
        for k in range(chips):
            at = pl.multiple_of((2 * k + core) * wrows, wrows)
            w_ref[pl.ds(at, wrows), :] = n_ref[k]
            at = pl.multiple_of((2 * k + 1 - core) * wrows, wrows)
            w_ref[pl.ds(at, wrows), :] = f_ref[k]
            x = x_refs[k][...].astype(F32)
            inv = lax.rsqrt(jnp.mean(x * x, axis=-1, keepdims=True) + NORM_EPS)
            at = pl.multiple_of((chip ^ k) * rows, rows)
            z_ref[pl.ds(at, rows), :] = (x * inv).astype(BF16)
        total = dot(z_ref[...], w_ref[...])
        cos, sin = cos_ref[...], sin_ref[...]
        for j in range(qw // 128):
            v = total[:, j * 128 : (j + 1) * 128]
            q_ref[:, j * 128 : (j + 1) * 128] = (v * cos + turned(v) * sin).astype(BF16)
        v = total[:, qw:]
        key = lax.broadcasted_iota(jnp.int32, v.shape, 1) < HD
        kv_ref[...] = jnp.where(key, v * cos + turned(v) * sin, v).astype(BF16)

    return pl.pallas_call(
        body,
        in_specs=[scalars()] + [whole()] * (4 + chips),
        out_specs=[whole()] * 4,
        out_shape=[
            jax.ShapeDtypeStruct((own, model), BF16),
            jax.ShapeDtypeStruct((own, qw), BF16),
            jax.ShapeDtypeStruct((own, 2 * HD), BF16),
            jax.ShapeDtypeStruct((2 * chips * wrows, width), BF16),
        ],
        cost_estimate=tiny(),
        name="qkv_forward",
    )(ids, cos_table, sin_table, near, far, *x_blocks)


def attention_mask(s_ref, l_ref, rows, block):
    core, rep, span = s_ref[1], s_ref[4], (block + 1) * rows

    def coded(pos):
        bound, code = 0, jnp.zeros(pos.shape, jnp.int32)
        for n in range(DOCS):
            bound = bound + l_ref[rep, n]
            code = code + jnp.where(pos >= bound, 1, 0)
        return jnp.where(code < DOCS - 1, code, 1000 + pos)

    q_pos = (2 * block + core) * rows + lax.broadcasted_iota(jnp.int32, (rows, 1), 0)
    index = lax.broadcasted_iota(jnp.int32, (1, 2 * span), 1)
    side = jnp.where(index < span, core, 1 - core)
    index = jnp.where(index < span, index, index - span)
    k_pos = (2 * (index // rows) + side) * rows + index % rows
    q_code = coded(q_pos)
    allowed = (coded(k_pos) == q_code) & (k_pos <= q_pos)
    return jnp.where(allowed, 0.0, MASK_FILL), jnp.where(q_code < DOCS, 1.0, 0.0)


def attention_forward(ids, lengths, q, kv_own, kv_other, rows, stack=4):
    own, qw = q.shape
    scale = 1.0 / math.sqrt(HD)
    heads = qw // HD
    stack = min(stack, heads)

    def body(s_ref, d_ref, q_ref, a_ref, b_ref, o_ref, l_ref):
        for block in range(own // rows):

            @pl.when(pl.program_id(0) == block)
            def _(block=block):
                span = (block + 1) * rows
                bias, valid = attention_mask(s_ref, d_ref, rows, block)
                lane = lax.broadcasted_iota(jnp.int32, (rows, 128), 1)
                sums = jnp.zeros((rows, 128), F32)
                keys = jnp.concatenate([a_ref[:span, :], b_ref[:span, :]], axis=0)
                k, v = keys[:, :HD], keys[:, HD:]
                for g in range(heads // stack):
                    qs = [q_ref[:, h * HD : (h + 1) * HD] for h in range(g * stack, (g + 1) * stack)]
                    qs = jnp.concatenate(qs, axis=0) * jnp.asarray(scale, BF16)
                    s = dot_nt(qs, k).reshape(stack, rows, 2 * span) + bias[None]
                    top = jnp.max(s, axis=-1, keepdims=True)
                    p = jnp.exp(s - top)
                    tot = jnp.sum(p, axis=-1, keepdims=True)
                    p = (p * (1.0 / tot)).astype(BF16).reshape(stack * rows, 2 * span)
                    o = dot(p, v).reshape(stack, rows, HD) * valid[None]
                    o = o.astype(BF16)
                    lse = top + jnp.log(tot)
                    for t in range(stack):
                        h = g * stack + t
                        sums = jnp.where(lane == h, lse[t], sums)
                        if t % 2:
                            pair = jnp.concatenate([o[t - 1], o[t]], axis=1)
                            o_ref[:, (h - 1) * HD : (h + 1) * HD] = pair
                l_ref[...] = sums

    blocked = lambda i: (i, 0)
    fixed = pl.BlockSpec((own, 2 * HD), lambda i: (0, 0))
    return pl.pallas_call(
        body,
        grid=(own // rows,),
        in_specs=[scalars(), scalars(), pl.BlockSpec((rows, qw), blocked), fixed, fixed],
        out_specs=[pl.BlockSpec((rows, qw), blocked), pl.BlockSpec((rows, 128), blocked)],
        out_shape=[
            jax.ShapeDtypeStruct((own, qw), BF16),
            jax.ShapeDtypeStruct((own, 128), F32),
        ],
        cost_estimate=tiny(),
        name="attention_forward",
    )(ids, lengths, q, kv_own, kv_other)


def attention_backward(
    ids, lengths, q, kv_own, kv_other, sums, d_out, cos_table, sin_table, rows, stack=4
):
    own, qw = q.shape
    scale = 1.0 / math.sqrt(HD)
    heads = qw // HD
    stack = min(stack, heads)
    blocks = own // rows

    def body(
        s_ref, n_ref, q_ref, a_ref, b_ref, l_ref, d_ref, cos_ref, sin_ref, dq_ref, dkv_ref,
    ):
        @pl.when(pl.program_id(0) == 0)
        def _():
            dkv_ref[...] = jnp.zeros_like(dkv_ref)

        for block in range(blocks):

            @pl.when(pl.program_id(0) == block)
            def _(block=block):
                span = (block + 1) * rows
                bias, valid = attention_mask(s_ref, n_ref, rows, block)
                valid = valid.astype(BF16)
                cos, sin = cos_ref[...], sin_ref[...]
                keys = jnp.concatenate([a_ref[:span, :], b_ref[:span, :]], axis=0)
                k, v = keys[:, :HD], keys[:, HD:]
                lane = lax.broadcasted_iota(jnp.int32, (rows, 128), 1)

                def some(g, carry):
                    at = pl.ds(pl.multiple_of(g * stack * HD, 128), stack * HD)
                    wide_q = q_ref[:, at] * jnp.asarray(scale, BF16)
                    wide_d = d_ref[:, at] * valid
                    qs = [wide_q[:, h * HD : (h + 1) * HD] for h in range(stack)]
                    qs = jnp.concatenate(qs, axis=0)
                    ds = [wide_d[:, h * HD : (h + 1) * HD] for h in range(stack)]
                    ds = jnp.concatenate(ds, axis=0)
                    lse = [jnp.where(lane == g * stack + t, l_ref[...], 0.0) for t in range(stack)]
                    lse = jnp.stack([jnp.sum(v, axis=-1, keepdims=True) for v in lse])
                    s = dot_nt(qs, k).reshape(stack, rows, 2 * span) + bias[None]
                    p = jnp.exp(s - lse)
                    dp = dot_nt(ds, v).reshape(stack, rows, 2 * span)
                    inner = jnp.sum(p * dp, axis=-1, keepdims=True)
                    grad = (p * (dp - inner)).astype(BF16).reshape(stack * rows, 2 * span)
                    p = p.astype(BF16).reshape(stack * rows, 2 * span)
                    dq = (dot(grad, k) * scale).reshape(stack, rows, HD)
                    both = jnp.concatenate([dot_tn(grad, qs), dot_tn(p, ds)], axis=1)
                    dkv_ref[:span, :] += both[:span]
                    dkv_ref[own : own + span, :] += both[span:]
                    for t in range(1, stack, 2):
                        w = jnp.concatenate([dq[t - 1], dq[t]], axis=1)
                        w = w * cos - turned(w) * sin
                        to = pl.ds(pl.multiple_of((g * stack + t - 1) * HD, 128), 2 * HD)
                        dq_ref[:, to] = w.astype(BF16)
                    return carry

                lax.fori_loop(0, heads // stack, some, 0)

    blocked = lambda i: (i, 0)
    fixed = pl.BlockSpec((own, 2 * HD), lambda i: (0, 0))
    table = pl.BlockSpec((rows, 128), blocked)
    wide = pl.BlockSpec((rows, qw), blocked)
    return pl.pallas_call(
        body,
        grid=(blocks,),
        in_specs=[scalars(), scalars(), wide, fixed, fixed, table, wide, table, table],
        out_specs=[wide, pl.BlockSpec((2 * own, 2 * HD), lambda i: (0, 0))],
        out_shape=[
            jax.ShapeDtypeStruct((own, qw), BF16),
            jax.ShapeDtypeStruct((2 * own, 2 * HD), F32),
        ],
        cost_estimate=tiny(),
        name="attention_backward",
    )(ids, lengths, q, kv_own, kv_other, sums, d_out, cos_table, sin_table)


def feed_forward(ids, z_blocks, cot, weights, w_down):
    rows, model = z_blocks[0].shape
    chips = len(z_blocks)
    part, width = weights[0][0].shape[1:]
    own, tile = rows * chips, min(TILE, width)
    turns = pl.cdiv(width, tile)

    def body(s_ref, *refs):
        z_refs, c_ref, w_refs = refs[:chips], refs[chips], refs[chips + 1 : chips + 9]
        d_ref, m_ref, dg_ref, du_ref, z_ref = refs[chips + 9 : chips + 14]
        b_refs, (w_ref, acc_ref) = refs[chips + 14 : -2], refs[-2:]
        chip, core, half = s_ref[0], s_ref[1], s_ref[2]
        turn = pl.program_id(0)

        @pl.when(turn == 0)
        def _():
            for k in range(chips):
                at = pl.multiple_of((chip ^ k) * rows, rows)
                z_ref[pl.ds(at, rows), :] = z_refs[k][...]
            acc_ref[...] = jnp.zeros_like(acc_ref)

        def work(cols, last):
            for m in range(2):
                for i in range(4):
                    side = core if i < 2 else 1 - core
                    piece = half if i % 2 == 0 else 1 - half
                    for j in range(chips):
                        at = pl.multiple_of((2 * (2 * j + side) + piece) * part, part)
                        w_ref[m, pl.ds(at, part), :cols] = w_refs[4 * m + i][j, :, :cols]
            gate = dot(z_ref[...], w_ref[0, :, :cols])
            up = dot(z_ref[...], w_ref[1, :, :cols])
            dm = dot_nt(c_ref[...], d_ref[:cols, :])
            sig = 1.0 / (1.0 + jnp.exp(-gate))
            silu = gate * sig
            m_ref[:, :cols] = (silu * up).astype(BF16)
            dg = (dm * up * sig * (1.0 + gate * (1.0 - sig))).astype(BF16)
            du = (dm * silu).astype(BF16)
            dg_ref[:, :cols] = dg
            du_ref[:, :cols] = du
            back = dot_nt(dg, w_ref[0, :, :cols]) + dot_nt(du, w_ref[1, :, :cols])
            back = back + acc_ref[...]
            acc_ref[...] = back
            if last:
                for k in range(chips):
                    at = pl.multiple_of((chip ^ k) * rows, rows)
                    b_refs[k][...] = acc_ref[pl.ds(at, rows), :].astype(BF16)

        if turns > 1:

            @pl.when(turn < turns - 1)
            def _():
                work(tile, False)

        @pl.when(turn == turns - 1)
        def _():
            work(width - (turns - 1) * tile, True)

    joined = pl.BlockSpec((own, model), lambda n, s: (0, 0))
    out_tile = pl.BlockSpec((own, tile), lambda n, s: (0, n))
    return pl.pallas_call(
        body,
        grid_spec=pltpu.PrefetchScalarGridSpec(
            num_scalar_prefetch=1,
            grid=(turns,),
            in_specs=[pl.BlockSpec((rows, model), lambda n, s: (0, 0))] * chips
            + [joined]
            + [pl.BlockSpec((chips, part, tile), lambda n, s: (0, 0, n))] * 8
            + [pl.BlockSpec((tile, model), lambda n, s: (n, 0))],
            out_specs=[out_tile] * 3
            + [joined]
            + [pl.BlockSpec((rows, model), lambda n, s: (0, 0))] * chips,
            scratch_shapes=[
                pltpu.VMEM((2, model, tile), BF16),
                pltpu.VMEM((own, model), F32),
            ],
        ),
        out_shape=[jax.ShapeDtypeStruct((own, width), BF16)] * 3
        + [jax.ShapeDtypeStruct((own, model), BF16)]
        + [jax.ShapeDtypeStruct((rows, model), BF16)] * chips,
        cost_estimate=tiny(),
        name="feed_forward",
    )(ids, *z_blocks, cot, *weights[0], *weights[1], w_down)


def out_proj(ids, attn, near, far, chips):
    own, depth = attn.shape
    wrows, model = near.shape
    rows = own // chips

    def body(c_ref, a_ref, n_ref, f_ref, *outs):
        chip, core, w_ref = c_ref[0], c_ref[1], outs[-1]
        w_ref[pl.ds(pl.multiple_of(core * wrows, wrows), wrows), :] = n_ref[...]
        w_ref[pl.ds(pl.multiple_of((1 - core) * wrows, wrows), wrows), :] = f_ref[...]
        for k in range(chips):
            at = pl.multiple_of((chip ^ k) * rows, rows)
            outs[k][...] = dot(a_ref[pl.ds(at, rows), :], w_ref[...]).astype(BF16)

    return pl.pallas_call(
        body,
        in_specs=[scalars()] + [whole()] * 3,
        out_specs=[whole()] * (chips + 1),
        out_shape=[jax.ShapeDtypeStruct((rows, model), BF16)] * chips
        + [jax.ShapeDtypeStruct((depth, model), BF16)],
        cost_estimate=tiny(),
        name="out_proj",
    )(ids, attn, near, far)


def residual_norm(tokens, parts):
    rows, model = tokens.shape

    def body(x_ref, *refs):
        y_ref, z_ref = refs[-2:]
        y = x_ref[...].astype(F32)
        for p in refs[:-2]:
            y = y + p[...].astype(F32)
        y_ref[...] = y
        inv = lax.rsqrt(jnp.mean(y * y, axis=-1, keepdims=True) + NORM_EPS)
        z_ref[...] = (y * inv).astype(BF16)

    return pl.pallas_call(
        body,
        in_specs=[whole()] * (1 + len(parts)),
        out_specs=[whole()] * 2,
        out_shape=[
            jax.ShapeDtypeStruct((rows, model), F32),
            jax.ShapeDtypeStruct((rows, model), BF16),
        ],
        cost_estimate=tiny(),
        name="residual_norm",
    )(tokens, *parts)


def residual_norm_back(base, parts, y, copies):
    rows, model = y.shape
    parts = parts if isinstance(parts, (list, tuple)) else [parts]

    def body(b_ref, y_ref, *refs):
        p_refs, (f_ref, l_ref, n_ref) = refs[:-3], refs[-3:]
        e = 0.0
        for p_ref in p_refs:
            for i in range(p_ref.shape[0] // rows):
                e = e + p_ref[i * rows : (i + 1) * rows, :].astype(F32)
        v = y_ref[...].astype(F32)
        inv = lax.rsqrt(jnp.mean(v * v, axis=-1, keepdims=True) + NORM_EPS)
        z = v * inv
        ez = e * z
        n_ref[...] = jnp.sum(ez, axis=0, keepdims=True)
        out = b_ref[...].astype(F32) + inv * (e - z * jnp.mean(ez, axis=-1, keepdims=True))
        f_ref[...] = out
        for i in range(copies):
            l_ref[i * rows : (i + 1) * rows, :] = out.astype(BF16)

    return pl.pallas_call(
        body,
        in_specs=[whole()] * (2 + len(parts)),
        out_specs=[whole()] * 3,
        out_shape=[
            jax.ShapeDtypeStruct((rows, model), F32),
            jax.ShapeDtypeStruct((copies * rows, model), BF16),
            jax.ShapeDtypeStruct((1, model), F32),
        ],
        cost_estimate=tiny(),
        name="residual_norm_back",
    )(base, y, *parts)


def strips(value, ref, lead=()):
    rows, width = value.shape
    for t in range(pl.cdiv(width, 128)):
        v = value[:, t * 128 : (t + 1) * 128]
        if v.shape[1] < 128:
            v = jnp.concatenate([v, jnp.zeros((rows, 128 - v.shape[1]), v.dtype)], axis=1)
        ref[(*lead, slice(t * rows, (t + 1) * rows), slice(None))] = v


def weight_grad(ids, left, right, chips):
    own, model = left.shape
    width = right.shape[1]
    rows = model // (2 * chips)
    long = pl.cdiv(width, 128) * rows
    group = min(2, chips)
    turns = chips // group

    def body(c_ref, l_ref, r_ref, near_ref, far_ref):
        step = pl.program_id(0)
        near = step >= turns
        side = jnp.where(near, c_ref[1], 1 - c_ref[1])
        first = jnp.where(near, step - turns, step) * group
        blocks = []
        for j in range(group):
            at = pl.multiple_of((2 * (first + j) + side) * rows, rows)
            blocks.append(l_ref[:, pl.ds(at, rows)])
        out = dot_tn(jnp.concatenate(blocks, axis=1), r_ref[...]).astype(BF16)

        @pl.when(near)
        def _():
            for j in range(group):
                strips(out[j * rows : (j + 1) * rows], near_ref, (j,))

        @pl.when(step < turns)
        def _():
            for j in range(group):
                strips(out[j * rows : (j + 1) * rows], far_ref, (j,))

    return pl.pallas_call(
        body,
        grid_spec=pltpu.PrefetchScalarGridSpec(
            num_scalar_prefetch=1,
            grid=(2 * turns,),
            in_specs=[
                pl.BlockSpec((own, model), lambda t, c: (0, 0)),
                pl.BlockSpec((own, width), lambda t, c: (0, 0)),
            ],
            out_specs=[
                pl.BlockSpec((group, long, 128), lambda t, c: (jnp.maximum(t - turns, 0), 0, 0)),
                pl.BlockSpec((group, long, 128), lambda t, c: (jnp.minimum(t, turns - 1), 0, 0)),
            ],
        ),
        out_shape=[jax.ShapeDtypeStruct((chips, long, 128), BF16)] * 2,
        cost_estimate=tiny(),
        name="weight_grad",
    )(ids, left, right)


def row_grad(ids, left, right, cuts):
    own, depth = left.shape
    model = right.shape[1]
    rows, width = depth // 2, model // cuts
    long = width // 128 * rows

    def body(c_ref, l_ref, r_ref, near_ref, far_ref, full_ref):
        core = c_ref[1]
        full_ref[...] = dot_tn(l_ref[...], r_ref[...]).astype(BF16)
        near = full_ref[pl.ds(pl.multiple_of(core * rows, 16), rows), :]
        far = full_ref[pl.ds(pl.multiple_of((1 - core) * rows, 16), rows), :]
        strips(near, near_ref, (0,))
        strips(far, far_ref, (0,))

    out = pl.BlockSpec((1, long, 128), lambda n, c: (n, 0, 0))
    return pl.pallas_call(
        body,
        grid_spec=pltpu.PrefetchScalarGridSpec(
            num_scalar_prefetch=1,
            grid=(cuts,),
            in_specs=[
                pl.BlockSpec((own, depth), lambda n, c: (0, 0)),
                pl.BlockSpec((own, width), lambda n, c: (0, n)),
            ],
            out_specs=[out] * 2,
            scratch_shapes=[pltpu.VMEM((depth, width), BF16)],
        ),
        out_shape=[jax.ShapeDtypeStruct((cuts, long, 128), BF16)] * 2,
        cost_estimate=tiny(),
        name="row_grad",
    )(ids, left, right)


def chain_step(ids, own, outer, sent, inner, coming):
    def size(v):
        return 0 if v is None else v[0].shape[1] if isinstance(v, tuple) else v.shape[0]

    ins = [own, outer if own is not None else None, sent, inner, coming]
    have = [v is not None for v in ins]
    sizes = [size(own), max(size(sent), size(coming))]

    def body(s_ref, *refs):
        refs = list(refs)
        o_ref, x_ref, i_ref, y_ref, c_ref = [refs.pop(0) if h else None for h in have]
        s_out, a_out = [refs.pop(0) if n else None for n in sizes]
        ends = s_ref[3] == 1

        def each(count, work):
            step = math.gcd(512, count)

            def turn(n, carry):
                work(pl.ds(pl.multiple_of(n * step, step), step))
                return carry

            lax.fori_loop(0, count // step, turn, 0)

        if s_out is not None:

            def add_own(at):
                s_out[at, :] = o_ref[at, :] + x_ref[at, :]

            each(size(own), add_own)
        if c_ref is not None:

            @pl.when(ends)
            def _():
                def copy(at):
                    a_out[at, :] = c_ref[at, :]

                each(size(coming), copy)

        if i_ref is not None:

            @pl.when(jnp.logical_not(ends))
            def _():
                def add_sent(at):
                    a_out[at, :] = i_ref[at, :] + y_ref[at, :]

                each(size(sent), add_sent)

    def spec(v):
        if not isinstance(v, tuple):
            return pl.BlockSpec(v.shape, lambda i: (0, 0))
        block = v[1]
        return pl.BlockSpec((pl.Squeezed(), *v[0].shape[1:]), lambda i: (block, 0, 0))

    outs = pl.pallas_call(
        body,
        grid=(1,),
        in_specs=[scalars()] + [spec(v) for v in ins if v is not None],
        out_specs=[pl.BlockSpec((n, 128), lambda i: (0, 0)) for n in sizes if n],
        out_shape=[jax.ShapeDtypeStruct((n, 128), BF16) for n in sizes if n],
        cost_estimate=tiny(),
        name="chain_step",
    )(ids, *[v[0] if isinstance(v, tuple) else v for v in ins if v is not None])
    outs = list(outs)
    return [outs.pop(0) if n else None for n in sizes]


def beside(ids, blocks, rows, width, scale=None):
    count = len(blocks)
    tiles = pl.cdiv(width, 128)
    long = tiles * rows
    if scale is None:
        scale = jnp.ones((rows, 1), F32)
    if width % 128:
        full = [
            a[:long].reshape(tiles, rows, 128).transpose(1, 0, 2).reshape(rows, -1)
            for a, b in blocks
        ]
        return jnp.concatenate([f[:, :width] for f in full], axis=1).astype(F32) * scale

    def body(c_ref, s_ref, *refs):
        scale, out_ref = s_ref[...], refs[-1]
        for k in range(count):
            for end in (0, 1):

                @pl.when((pl.program_id(0) == k) & (c_ref[3] == end))
                def _(ref=refs[2 * k + end]):
                    for t in range(tiles):
                        v = ref[t * rows : (t + 1) * rows, :].astype(F32)
                        out_ref[:, t * 128 : (t + 1) * 128] = v * scale

    return pl.pallas_call(
        body,
        grid_spec=pltpu.PrefetchScalarGridSpec(
            num_scalar_prefetch=1,
            grid=(count,),
            in_specs=[pl.BlockSpec((rows, 1), lambda k, c: (0, 0))]
            + [pl.BlockSpec((long, 128), lambda k, c: (0, 0))] * (2 * count),
            out_specs=pl.BlockSpec((rows, width), lambda k, c: (0, k)),
        ),
        out_shape=jax.ShapeDtypeStruct((rows, count * width), F32),
        cost_estimate=tiny(),
        name="beside",
    )(ids, scale, *[v for pair in blocks for v in pair])


def pair_sum(near, far):
    count, rows, lanes = near.shape

    def body(a_ref, b_ref, out_ref):
        out_ref[...] = a_ref[...] + b_ref[...]

    spec = pl.BlockSpec((2, rows, lanes), lambda k: (k, 0, 0))
    return pl.pallas_call(
        body,
        grid=(count // 2,),
        in_specs=[spec] * 2,
        out_specs=spec,
        out_shape=jax.ShapeDtypeStruct(near.shape, BF16),
        cost_estimate=tiny(),
        name="pair_sum",
    )(near, far)


def local(
    tokens,
    cotangent,
    doc_lengths,
    norm1_gain,
    w_query,
    w_key,
    w_value,
    w_out,
    norm2_gain,
    w_gate,
    w_up,
    w_down,
):
    rows, model = tokens.shape
    group = lax.axis_size("fsdp")
    reps = lax.axis_size("rep")
    chips = group // 2
    dev = lax.axis_index("fsdp").astype(jnp.int32)
    rep = lax.axis_index("rep").astype(jnp.int32)
    chip, core, half = dev >> 1, dev & 1, rep & 1
    ends = jnp.where((rep == 0) | (rep == reps - 1), 1, 0).astype(jnp.int32)
    ids = jnp.stack([chip, core, half, ends, rep])
    seq_len = rows * group
    own = rows * chips
    wrows = w_query.shape[0]
    width = w_gate.shape[1] // chips
    kv_share = chips // KVH
    qw = H // chips * HD
    tie = lax.optimization_barrier
    sides = [[2 * k + c for k in range(chips)] for c in range(2)]

    def exchange(v):
        return lax.all_to_all(v, "fsdp", 0, 0, axis_index_groups=sides, tiled=True)

    def hop(v, k):
        return lax.ppermute(v, "fsdp", [(i, i ^ (2 * k)) for i in range(group)])

    def hops(blocks):
        return [blocks[0]] + [hop(blocks[k], k) for k in range(1, chips)]

    def swap(v):
        return lax.ppermute(v, "fsdp", [(i, i ^ 1) for i in range(group)])

    def trade(v):
        return lax.ppermute(v, "rep", [(i, i ^ 1) for i in range(reps)])

    def copies(v):
        return jnp.broadcast_to(v[None], (chips,) + v.shape).reshape(chips * v.shape[0], -1)

    sums_of = {}
    outer_pairs = [(0, 1), (1, 0), (2, 3), (3, 2)]

    class Line:
        def __init__(self):
            self.own = self.sent = self.total = self.outer = self.inner = None

        def busy(self):
            return any(v is not None for v in (self.own, self.sent, self.total))

    lines = [Line(), Line()]
    turn = [0]

    def visit(*carry, new=None):
        if reps != 4:
            if new is not None:
                value = lax.psum(new[1][new[2]], "rep")
                sums_of[f"{new[0]}{new[2]}"] = (value, value)
            return carry if len(carry) != 1 else carry[0]
        line = lines[turn[0] % 2]
        turn[0] += 1
        extra = [line.outer, line.inner, None if new is None else new[1]]
        tied = tie(tuple(carry) + tuple(v for v in extra if v is not None))
        carry, tied = tied[: len(carry)], list(tied[len(carry) :])
        outer, inner, coming = [None if v is None else tied.pop(0) for v in extra]
        coming = None if new is None else (coming, new[2])
        value = lambda pair: None if pair is None else pair[1]
        if line.total is not None:
            sums_of[line.total[0]] = (line.total[1], outer)
        own_sum = ahead = None
        if outer is None:
            ahead = None if coming is None else coming[0][coming[1]]
        elif line.own is not None or line.sent is not None or coming is not None:
            own_sum, ahead = chain_step(
                ids, value(line.own), outer, value(line.sent), inner, coming
            )
        line.total = None if line.sent is None else (line.sent[0], ahead)
        line.sent = None if line.own is None else (line.own[0], own_sum)
        line.own = None if coming is None else (f"{new[0]}{new[2]}", coming)
        line.outer = None if ahead is None else lax.ppermute(ahead, "rep", outer_pairs)
        line.inner = (
            None if line.sent is None else lax.ppermute(line.sent[1], "rep", [(1, 2), (2, 1)])
        )
        return carry if len(carry) != 1 else carry[0]

    def summed(name, count):
        return [sums_of[f"{name}{k}"] for k in range(count)]

    starts = 2 * rows * jnp.arange(chips, dtype=jnp.int32) + core * rows
    own_pos = (starts[:, None] + jnp.arange(rows, dtype=jnp.int32)[None, :]).reshape(own)
    lane = jnp.arange(128)
    inverse = jnp.exp(-math.log(ROPE_BASE) / (HD // 2) * (lane % (HD // 2)).astype(F32))
    angles = own_pos.astype(F32)[:, None] * inverse[None, :]
    cos_table = jnp.cos(angles)
    sin_table = jnp.sin(angles) * jnp.where(lane % HD < HD // 2, -1.0, 1.0)[None, :]

    gain_one = norm1_gain.astype(F32)[:, None]
    gain_two = norm2_gain.astype(F32)[:, None]
    x_blocks = hops([tokens] * chips)
    qkv_near = exchange(pick_qkv(w_query, w_key, w_value, gain_one, chips))
    gate_part, up_part = pick_half(w_gate, w_up, gain_two, ids, chips)
    w_out_far = swap(w_out)
    w_down_c = join_cores(ids, w_down, swap(w_down))
    *x_blocks, cos_table, sin_table, gate_part, up_part, w_out_far, w_down_c = tie(
        (*x_blocks, cos_table, sin_table, gate_part, up_part, w_out_far, w_down_c)
    )
    gate_near = exchange(gate_part)
    normed_one, queries, kv_near, w_qkv = qkv_kernel(
        ids, x_blocks, qkv_near, swap(qkv_near), cos_table, sin_table
    )
    queries, gate_near, up_part, cot = tie((queries, gate_near, up_part, cotangent))
    up_near = exchange(up_part)
    gate_traded = trade(gate_near)
    kv_far = swap(kv_near)
    attn, sums = attention_forward(ids, doc_lengths, queries, kv_near, kv_far, rows)
    gate_far = swap(gate_near)
    attn, up_near, gate_far = tie((attn, up_near, gate_far))
    up_traded = trade(up_near)
    *mixed, w_out_c = out_proj(ids, attn, w_out, w_out_far, chips)
    *mixed, cot = tie((*mixed, cot))
    parts = hops(mixed)
    cot_rows = exchange(copies(cot))
    *parts, gate_traded, up_far = tie((*parts, gate_traded, swap(up_near)))
    resid, normed = residual_norm(tokens, parts)
    z_blocks = hops([normed] * chips)
    weights = [
        [gate_near, gate_traded, gate_far, swap(gate_traded)],
        [up_near, up_traded, up_far, swap(up_traded)],
    ]
    inner, grad_gate, grad_up, normed_two, *back = feed_forward(
        ids, z_blocks, cot_rows, weights, w_down_c
    )

    parts = hops(back)
    down_near, down_far = row_grad(ids, inner, cot_rows, 4)
    down_far = swap(down_far)
    grad_gate, down_near = tie((grad_gate, down_near))
    gate_near, gate_far = weight_grad(ids, normed_two, grad_gate, chips)
    gate_near, gate_far, down_far, grad_up, *parts = tie(
        (gate_near, gate_far, down_far, grad_up, *parts)
    )
    gate_far = swap(gate_far)
    grad_resid, da, gain_two_local = residual_norm_back(cotangent, parts, resid, chips)
    da, gate_near, down_near = tie((da, gate_near, down_near))
    down = pair_sum(down_near, down_far)
    grad_up = visit(grad_up, new=("down", down, 0))
    up_near, up_far = weight_grad(ids, normed_two, grad_up, chips)
    up_near, up_far, da = visit(up_near, up_far, da, new=("down", down, 1))
    gate_part = exchange(pair_sum(gate_near, gate_far))
    up_far = swap(up_far)
    da, inner = visit(da, inner, new=("down", down, 2))
    out = dot(inner, w_down_c).astype(BF16)
    up_part = pair_sum(up_near, up_far)
    out, up_part, gate_part = visit(out, up_part, gate_part, new=("down", down, 3))
    da = exchange(da)
    da, up_part = visit(da, up_part, new=("gate", gate_part, 0))
    up_part = exchange(up_part)
    dob = dot_nt(da, w_out_c).astype(BF16)
    out_near, out_far = row_grad(ids, attn, da, 2)
    dob, out_near, out_far = visit(dob, out_near, out_far, new=("gate", gate_part, 1))
    out_far = swap(out_far)
    dq, dkv = attention_backward(
        ids, doc_lengths, queries, kv_near, kv_far, sums, dob, cos_table, sin_table, rows
    )
    dq, dkv = visit(dq, dkv, new=("gate", gate_part, 2))
    dkv = dkv[:own] + swap(dkv[own:].astype(BF16)).astype(F32)
    half_turn = jnp.concatenate([dkv[:, HD // 2 : HD], dkv[:, : HD // 2]], axis=1)
    dk = dkv[:, :HD] * cos_table[:, :HD] - half_turn * sin_table[:, :HD]
    dqkv = jnp.concatenate([dq, dk.astype(BF16), dkv[:, HD:].astype(BF16)], axis=1)
    back = dot_nt(dqkv, w_qkv).astype(BF16)
    dqkv, back, up_part = visit(dqkv, back, up_part, new=("gate", gate_part, 3))
    parts = exchange(back)
    qkv_near, qkv_far = weight_grad(ids, normed_one, dqkv, chips)
    qkv_near, qkv_far = visit(qkv_near, qkv_far, new=("up", up_part, 0))
    qkv_part = pair_sum(qkv_near, swap(qkv_far))
    qkv_part, parts = visit(qkv_part, parts, new=("up", up_part, 1))
    qkv_part = exchange(qkv_part)
    _, grad_inputs, gain_one_local = residual_norm_back(grad_resid, parts, tokens, 1)
    gain_one_local = visit(gain_one_local, new=("up", up_part, 2))
    norms = jnp.concatenate([gain_one_local, gain_two_local], axis=0)
    norms = norms.reshape(2, chips, 2, wrows).transpose(2, 1, 0, 3)
    mine = lax.dynamic_index_in_dim(norms, core, 0, keepdims=False)
    other = lax.dynamic_index_in_dim(norms, 1 - core, 0, keepdims=False)
    mine = mine + swap(other)
    out_part = pair_sum(out_near, out_far)
    if reps == 4:
        grad_down = beside(ids, summed("down", 4), w_down.shape[0], model // 4)
        mine, grad_down = tie((mine, grad_down))
    mine, qkv_part, out_part = visit(mine, qkv_part, out_part, new=("up", up_part, 3))
    parts = exchange(out).reshape(chips, rows, model)
    norms = lax.dynamic_index_in_dim(mine, chip, 0, keepdims=False)
    for k in range(1, chips):
        norms = norms + hop(lax.dynamic_index_in_dim(mine, chip ^ k, 0, keepdims=False), k)
    qkv_part = qkv_part.reshape(2, -1, 128)
    norms = visit(norms, new=("qkv", qkv_part, 0))
    parts, norms = visit(parts, norms, new=("qkv", qkv_part, 1))
    result = (resid + jnp.sum(parts.astype(F32), axis=0)).astype(BF16)
    norms = norms.astype(BF16).reshape(-1, 128)
    norms = jnp.pad(norms, ((0, 256 - norms.shape[0]), (0, 0)))
    last = jnp.concatenate([out_part[1], norms], axis=0)[None]
    if reps == 4:
        grad_gate_out = beside(ids, summed("gate", 4), wrows, width, gain_two)
        last, grad_gate_out = visit(last, grad_gate_out, new=("out", out_part, 0))
    else:
        visit(new=("out", out_part, 0))
    visit(new=("last", last, 0))
    if reps != 4:
        for k in range(4, chips):
            visit(new=("gate", gate_part, k))
            visit(new=("up", up_part, k))
        grad_gate_out = beside(ids, summed("gate", chips), wrows, width, gain_two)
    while any(line.busy() for line in lines):
        visit()

    if reps != 4:
        grad_down = beside(ids, summed("down", 4), w_down.shape[0], model // 4)
    rows_of = wrows * pl.cdiv(qw + 2 * HD, 128)
    qkv = [
        (a[n : n + rows_of], b[n : n + rows_of])
        for a, b in summed("qkv", 2)
        for n in range(0, chips // 2 * rows_of, rows_of)
    ]
    last = sums_of["last0"]
    at = out_part.shape[1]
    norms = jnp.where(ends == 1, last[1], last[0])[at : at + 2 * wrows // 128]
    norms = norms.astype(F32).reshape(2, wrows)
    grad_query = beside(ids, qkv, wrows, qw, gain_one)
    kv_at = qw // 128 * wrows
    kv = [
        jnp.where(ends == 1, b[kv_at : kv_at + wrows], a[kv_at : kv_at + wrows]) for a, b in qkv
    ]
    kv = jnp.stack(kv).astype(F32).reshape(KVH, kv_share, wrows, 2, HD).sum(axis=1)
    kv = kv * gain_one[None, :, :, None]
    grad_key = kv[:, :, 0].transpose(1, 0, 2).reshape(wrows, KVH * HD)
    grad_value = kv[:, :, 1].transpose(1, 0, 2).reshape(wrows, KVH * HD)
    return (
        result,
        grad_inputs,
        norms[0] / gain_one[:, 0],
        grad_query,
        grad_key,
        grad_value,
        beside(ids, [sums_of["out0"], tuple(v[:at] for v in last)], wrows, model // 2),
        norms[1] / gain_two[:, 0],
        grad_gate_out,
        beside(ids, summed("up", chips), wrows, width, gain_two),
        grad_down,
    )


def solution(mesh):
    placed = (
        P(("rep", "fsdp"), None),
        P(("rep", "fsdp"), None),
        P(),
        P("fsdp"),
        P("fsdp", None),
        P("fsdp", None),
        P("fsdp", None),
        P("fsdp", None),
        P("fsdp"),
        P("fsdp", None),
        P("fsdp", None),
        P("fsdp", None),
    )
    return jax.shard_map(
        local,
        mesh=mesh,
        in_specs=placed,
        out_specs=(
            P(("rep", "fsdp"), None),
            P(("rep", "fsdp"), None),
            P("fsdp"),
            P("fsdp", None),
            P("fsdp", None),
            P("fsdp", None),
            P("fsdp", None),
            P("fsdp"),
            P("fsdp", None),
            P("fsdp", None),
            P("fsdp", None),
        ),
        check_vma=False,
    )
```
